32 devices in a mesh: stream: 4 (over y, core), azim: 8 (over z, x).
Axes of the slice: x: 2, y: 2, z: 4, core: 2. Of those that a mesh axis runs over, the one named last changes fastest.
Arguments:
- fluid: float32 [4, 256, 256, 128], P(None, 'stream', 'azim'), may hold values from -4 to 4
- bubbles: float32 [16384, 5, 128], P(('stream', 'azim'))
- counts: int32 [32], P(('stream', 'azim')), may hold values from 128 to 512
- outgoing_block_order: int32 [16384], P(('stream', 'azim')), may hold values from 0 to 511, as said below
- tiles_first_update: int32 [16384], P(('stream', 'azim')), may hold values from 0 to 2047
- tiles_after: int32 [16384], P(('stream', 'azim')), may hold values from 0 to 2047
Outputs:
- fluid_out: float32 [4, 256, 256, 128], P(None, 'stream', 'azim')
- bubbles_out: float32 [16384, 5, 128], P(('stream', 'azim'))
- void_fraction: float32 [256, 256, 128], P('stream', 'azim')
The draws below stay inside these ranges and needn't reach their ends.
Inputs may be any that keep to these rules, and one draw needn't show every extreme that they name: `outgoing_block_order`: for each device, its 512 entries are each of 0 to 511 once.
All inputs are finite; a program needn't handle non-finite values.
Results may differ from the reference program's by a relative error of at most 0.000076.
Values sent between devices are 32-bit elements; how exact they have to be, the bound alone decides.
A program may use at most 128 MiB of HBM per device.

```python
import math
import jax
import jax.numpy as jnp
import numpy as np
from jax import lax

CS = 64
CA = 32
CR = 128
BB = 128
NBLK = 512
SUBSTEPS = 8
NTILE = 2048
CAP = 16
NS = 256
NAZ = 256
NBT = 16384
N_AZIM = 8
DEVICES = 32


def draw_bubbles(key, part):
    uniform_draw = jax.random.uniform(key, (NBT, 5, BB), jnp.float32)
    lower = jnp.array([0.8, -0.3, 4.0, -1.0, 0.8], jnp.float32)
    upper = jnp.array([1.25, 0.3, CR - 5.0, 1.0, 1.2], jnp.float32)
    return (lower[None, :, None] + (upper - lower)[None, :, None] * uniform_draw).astype(jnp.float32)


def draw_outgoing_block_order(key, part):
    device_keys = jax.random.split(jax.random.fold_in(key, 17), NBT // NBLK)
    orders = jax.vmap(lambda single: jax.random.permutation(single, NBLK))(device_keys)
    return orders.reshape(-1).astype(jnp.int32)


def plant(values, key, least, top_value):
    longest = values.shape.index(max(values.shape))
    spots = []
    for shift in (0, 1):
        where = [jax.random.randint(jax.random.fold_in(key, axis), (), 0, length) for axis, length in enumerate(values.shape)]
        where[longest] = (where[longest] + shift) % values.shape[longest]
        spots.append(tuple(where))
    return values.at[spots[0]].set(least).at[spots[1]].set(top_value)


def steps_of(key, shape, shards, low, largest):
    def one(dim, blocks):
        steps = jax.random.uniform(jax.random.fold_in(jax.random.fold_in(key, 6), dim), (blocks,), jnp.float32, low / len(shards), largest / len(shards))
        return jnp.repeat(jnp.exp(steps), shape[dim] // blocks).reshape((-1,) + (1,) * (len(shape) - dim - 1))

    loudness = one(*shards[0])
    for cut in shards[1:]:
        loudness = loudness * one(*cut)
    return loudness


def rank_bounds(amount, slope):
    weights = [(1 << 20) // math.isqrt(standing ** slope) + 1 for standing in range(1, amount + 1)]
    deviation = 1 + sum(weights) // (1 << 30)
    return np.cumsum(np.array([max(1, weight // deviation) for weight in weights]))


def skewed_ids(own_key, extent, amount, lean):
    table = rank_bounds(amount, lean)
    ticket = jax.random.randint(jax.random.fold_in(own_key, 1), extent, 0, int(table[amount - 1]))
    grade = jnp.searchsorted(jnp.asarray(table, jnp.int32), ticket, side="right")
    return jax.random.permutation(jax.random.fold_in(own_key, 2), amount)[grade].astype(jnp.int32)


def bell_draw(own_key, dims, deviation, bound, shards=(), kind=jnp.bfloat16):
    gain = steps_of(own_key, dims, shards, -0.22, 0.18) if shards else 1.0
    values = jax.random.normal(own_key, dims, jnp.float32) * deviation * gain
    return jnp.minimum(jnp.maximum(values, -bound), bound).astype(kind)


def setup_inputs(seed: int = 0) -> dict:
    key_of = jax.random.split(jax.random.key(seed), 7)
    fluid = bell_draw(key_of[0], (4, NS, NAZ, CR), 1.0, 4.0, ((1, 4), (2, 8)), jnp.float32)
    bubbles = draw_bubbles(jax.random.fold_in(key_of[6], 71), 0)
    counts = plant(jax.random.randint(key_of[2], (DEVICES,), NBLK // 4, NBLK + 1), jax.random.fold_in(key_of[2], 1), NBLK // 4, NBLK).astype(jnp.int32)
    outgoing_block_order = draw_outgoing_block_order(jax.random.fold_in(key_of[6], 71), 0)
    tiles_first_update = plant(skewed_ids(key_of[4], (NBT,), NTILE, 1), jax.random.fold_in(key_of[4], 3), 0, NTILE - 1).astype(jnp.int32)
    tiles_after = plant(skewed_ids(key_of[5], (NBT,), NTILE, 1), jax.random.fold_in(key_of[5], 3), 0, NTILE - 1).astype(jnp.int32)
    return {"fluid": fluid, "bubbles": bubbles, "counts": counts, "outgoing_block_order": outgoing_block_order, "tiles_first_update": tiles_first_update, "tiles_after": tiles_after}


TIME_STEP = 0.25
MEAN_FLOW = 0.5
DIFFUSION = 0.1
KERNEL_WIDTH = 1.5
GAS_INDEX = 4.2
PRESSURE_COUPLING = 0.3
AMBIENT = 1.0
RELAX_TIME = 0.5
VISCOUS = 0.08
SOURCE_GAIN = 0.05
VOID_SCALE = 0.01
FOUR_PI = 12.566370614359172


def kernel_weights(position, cell_centres):
    offset = (position[:, :, None] - cell_centres) / KERNEL_WIDTH
    raw = jnp.exp(-0.5 * offset * offset)
    return raw / jnp.sum(raw, axis=-1, keepdims=True)


def advance_group(packed_blocks):
    bubble_state, tile_row_count, alive_flags = packed_blocks
    cell_centres = jnp.arange(tile_row_count.shape[-1], dtype=jnp.int32).astype(jnp.float32)
    weights = kernel_weights(bubble_state[:, 2], cell_centres)
    sampled = jnp.einsum("gbk,gck->gcb", weights, tile_row_count, precision=lax.Precision.HIGHEST)
    pressure = sampled[:, 0]
    velocity = sampled[:, 1]
    radius = bubble_state[:, 0]
    growth = bubble_state[:, 1]
    position = bubble_state[:, 2]
    bubble_speed = bubble_state[:, 3]
    rest_radius = bubble_state[:, 4]
    substep_size = TIME_STEP / SUBSTEPS
    for substep in range(SUBSTEPS):
        gas = jnp.exp(GAS_INDEX * jnp.log(rest_radius / radius))
        accel = (gas - AMBIENT - PRESSURE_COUPLING * pressure - 1.5 * growth * growth - VISCOUS * growth / radius) / radius
        growth = growth + substep_size * accel
        radius = radius + substep_size * growth
        bubble_speed = bubble_speed + substep_size * (velocity - bubble_speed) / RELAX_TIME
        position = position + substep_size * bubble_speed
    new_state = jnp.stack([radius, growth, position, bubble_speed, rest_radius], axis=1)
    weights = kernel_weights(position, cell_centres)
    source_amounts = jnp.stack([SOURCE_GAIN * FOUR_PI * radius * radius * growth,
                         VOID_SCALE * FOUR_PI / 3.0 * radius * radius * radius], axis=1)
    source_amounts = source_amounts * alive_flags[:, None, None]
    spread_sources = jnp.einsum("gbk,gcb->gck", weights, source_amounts, precision=lax.Precision.HIGHEST)
    return new_state, spread_sources


def advance_every_group(bubble_state, tile_row_count, alive_flags):
    bubble_groups = bubble_state.shape[0] // 64
    new_state, spread_sources = lax.map(advance_group, (bubble_state.reshape((bubble_groups, 64) + bubble_state.shape[1:]),
                                                tile_row_count.reshape((bubble_groups, 64) + tile_row_count.shape[1:]),
                                                alive_flags.reshape(bubble_groups, 64)))
    return new_state.reshape(bubble_state.shape), spread_sources.reshape(tile_row_count.shape)


def fluid_update(flow_field, stream_up, stream_down, azim_up, azim_down, radial_up, radial_down, source):
    d_stream = 0.5 * (stream_up - stream_down)
    d_azim = 0.5 * (azim_up - azim_down)
    d_radial = 0.5 * (radial_up - radial_down)
    pressure_rate = -MEAN_FLOW * d_stream[0] - d_stream[1] - d_azim[2] - d_radial[3] - source
    stream_rate = -MEAN_FLOW * d_stream[1] - d_stream[0]
    azim_rate = -MEAN_FLOW * d_stream[2] - d_azim[0]
    radial_rate = -MEAN_FLOW * d_stream[3] - d_radial[0]
    change = jnp.stack([pressure_rate, stream_rate, azim_rate, radial_rate])
    laplace = stream_up + stream_down + azim_up + azim_down + radial_up + radial_down - 6.0 * flow_field
    return flow_field + TIME_STEP * change + DIFFUSION * laplace


def fluid_step(flow_field, source):
    padded = jnp.pad(flow_field, ((0, 0), (1, 1), (0, 0), (1, 1)))
    return fluid_update(flow_field, padded[:, 2:, :, 1:-1], padded[:, :-2, :, 1:-1],
                        jnp.roll(flow_field, -1, axis=2), jnp.roll(flow_field, 1, axis=2),
                        padded[:, 1:-1, :, 2:], padded[:, 1:-1, :, :-2], source)


def global_update(flow_field, bubble_state, tile_indices, alive_flags):
    slot_index = jnp.arange(NBT, dtype=jnp.int32)
    owner_device = slot_index // NBLK
    stream_cell = (owner_device // N_AZIM) * CS + tile_indices // CA
    azim_cell = (owner_device % N_AZIM) * CA + tile_indices % CA
    selected = jnp.stack([flow_field[0], flow_field[3]])
    tile_row_count = selected[:, stream_cell, azim_cell].transpose(1, 0, 2)
    bubble_state, spread_sources = advance_every_group(bubble_state, tile_row_count, alive_flags)
    grid = jnp.zeros((2,) + flow_field.shape[1:], jnp.float32).at[:, stream_cell, azim_cell].add(spread_sources.transpose(1, 0, 2))
    return fluid_step(flow_field, grid[0]), bubble_state, grid[1]


def reference(fluid, bubbles, counts, outgoing_block_order, tiles_first_update, tiles_after):
    slot_index = jnp.arange(NBT, dtype=jnp.int32)
    owner_device = slot_index // NBLK
    local_slot_index = slot_index % NBLK
    alive_flags = (local_slot_index < counts[owner_device]).astype(jnp.float32)
    flow_field, bubble_state, void_before_update = global_update(fluid, bubbles, tiles_first_update, alive_flags)
    source_device = local_slot_index // CAP
    within = local_slot_index % CAP
    position_sent = source_device * NBLK + owner_device * CAP + within
    sender_slot_index = (source_device * NBLK + outgoing_block_order[position_sent]).astype(jnp.int32)
    moved = bubble_state[sender_slot_index]
    moved_alive_flags = alive_flags[sender_slot_index]
    flow_field, bubble_state, void_field = global_update(flow_field, moved, tiles_after, moved_alive_flags)
    return flow_field, bubble_state * moved_alive_flags[:, None, None], void_field
```

```python
import functools

import jax
import jax.numpy as jnp
from jax import lax
from jax.experimental import pallas as pl
from jax.experimental.pallas import tpu as pltpu
from jax.sharding import PartitionSpec as P

MESH = pl.DeviceIdType.MESH
SUBSTEPS = 8
TIME_STEP = 0.25
MEAN_FLOW = 0.5
DIFFUSION = 0.1
KERNEL_WIDTH = 1.5
GAS_INDEX = 4.2
PRESSURE_COUPLING = 0.3
AMBIENT = 1.0
RELAX_TIME = 0.5
VISCOUS = 0.08
SOURCE_GAIN = 0.05
VOID_SCALE = 0.01
FOUR_PI = 12.566370614359172
LOG2E = 1.4426950408889634
SHARPNESS = 0.5 * LOG2E / (KERNEL_WIDTH * KERNEL_WIDTH)
GROUP = 8
QUAD = 4
CHUNK = 16
STATES = 5
WIDE = 4
VMEM_GRANT = 60 * 2**20
f32, bf16 = jnp.float32, jnp.bfloat16


def cell_columns(cells_n, lanes):
    column = lax.broadcasted_iota(jnp.int32, (8, lanes), 0).astype(f32)
    tiles = cells_n // 8
    return {a: column + float(8 * a) for a in centres(tiles)}


def centres(tiles):
    return [min(start + 1, tiles - 1) for start in range(0, tiles, 3)]


def raw_weights(position, columns, tiles):
    pieces = [None] * tiles
    for start in range(0, tiles, 3):
        width = min(3, tiles - start)
        middle = min(start + 1, tiles - 1)
        offset = columns[middle] - position
        slope = offset * -SHARPNESS
        at = slope * offset
        pieces[middle] = jnp.exp2(at)
        if width > 1:
            near = at - 64.0 * SHARPNESS
            step = slope * 16.0
            pieces[middle - 1] = jnp.exp2(near - step)
            if middle + 1 < start + width:
                pieces[middle + 1] = jnp.exp2(near + step)
    return jnp.concatenate(pieces, axis=0)


def split_bf16(values):
    high = values.astype(bf16)
    low = (values - high.astype(f32)).astype(bf16)
    return high, low


def two_parts(rows):
    high = rows.astype(bf16).astype(f32)
    return jnp.concatenate([high, rows - high], axis=0).astype(bf16)


def clear_lhs(lhs):
    cells_n = lhs.shape[2] // 2
    lhs[...] = jnp.zeros_like(lhs)
    one = jnp.ones((1, cells_n), f32)
    for q in range(lhs.shape[0]):
        lhs[q, 4:5, :cells_n] = one
        lhs[q, 12:13, cells_n:] = one


def sample_quad(q, at, positions, columns, rows_of, lhs, sp, su, sn):
    cells_n = lhs.shape[2] // 2
    weights = []
    for j in range(QUAD):
        p_row, u_row = rows_of(j)
        row, side = 8 * (j // 2) + 2 * (j % 2), slice(cells_n * (j // 2), cells_n * (j // 2 + 1))
        lhs[q, row : row + 1, side] = p_row
        lhs[q, row + 1 : row + 2, side] = u_row
        weights.append(raw_weights(positions[j], columns, cells_n // 8).astype(bf16))
    rhs = jnp.concatenate(
        [jnp.concatenate(weights[:2], axis=1), jnp.concatenate(weights[2:], axis=1)], axis=0
    )
    result = jnp.dot(two_parts(lhs[q]), rhs, preferred_element_type=f32)
    result = result[:16] + result[16:]
    lanes = rhs.shape[1] // 2
    for j in range(QUAD):
        row, part = 8 * (j // 2), result[:, lanes * (j % 2) : lanes * (j % 2 + 1)]
        first = row + 2 * (j % 2)
        sp[pl.ds(at + j, 1), :] = part[first : first + 1]
        su[pl.ds(at + j, 1), :] = part[first + 1 : first + 2]
        sn[pl.ds(at + j, 1), :] = part[row + 4 : row + 5]


def advance_group(state, pressure, velocity, norm):
    radius, growth, position, speed, rest = state
    inverse = 1.0 / norm
    drive = AMBIENT + PRESSURE_COUPLING * (pressure * inverse)
    velocity = velocity * inverse
    h = TIME_STEP / SUBSTEPS
    for _ in range(SUBSTEPS):
        over = 1.0 / radius
        gas = jnp.exp(GAS_INDEX * jnp.log(rest * over))
        accel = (gas - drive - 1.5 * growth * growth - VISCOUS * growth * over) * over
        growth = growth + h * accel
        radius = radius + h * growth
        speed = speed + (h / RELAX_TIME) * (velocity - speed)
        position = position + h * speed
    return radius, growth, position, speed, rest


def source_amount(radius, growth):
    return SOURCE_GAIN * FOUR_PI * radius * radius * growth


def void_amount(radius):
    return VOID_SCALE * FOUR_PI / 3.0 * radius * radius * radius


def spread_pair(pair, positions, amounts, columns, tiles):
    pieces, norms = [], []
    for position in positions:
        raw = raw_weights(position, columns, tiles)
        norms.append(jnp.sum(raw, axis=0, keepdims=True))
        pieces.append(jnp.concatenate(split_bf16(raw), axis=1))
    rhs = jnp.concatenate(pieces, axis=0)
    sublane = lax.broadcasted_iota(jnp.int32, amounts[0].shape, 0)
    inverse = 1.0 / jnp.where(sublane == 2 * pair, norms[0], norms[1])
    rows = jnp.concatenate([a * inverse for a in amounts], axis=0)
    lhs = two_parts(rows)
    lhs = jnp.concatenate([lhs, lhs], axis=1)
    result = lax.dot_general(
        lhs, rhs, (((1,), (1,)), ((), ())), preferred_element_type=f32
    )
    result = result[: rows.shape[0]] + result[rows.shape[0] :]
    cells_n = 8 * tiles
    out = []
    for n in range(len(amounts)):
        for side in range(2):
            row = GROUP * n + 2 * pair + side
            out.append(result[row : row + 1, side * cells_n : (side + 1) * cells_n])
    return out


def lanes_of(rows):
    number, lanes = rows.shape
    pieces = []
    for at in range(0, number, lanes):
        block = rows[at : at + lanes]
        same = lax.broadcasted_iota(jnp.int32, block.shape, 0) == lax.broadcasted_iota(
            jnp.int32, block.shape, 1
        )
        line = jnp.sum(jnp.where(same, block, 0.0), axis=0, keepdims=True)
        pieces.append(line[:, : block.shape[0]])
    return jnp.concatenate(pieces, axis=1)


def scatter(tile_rows, parts, outs):
    tiles = outs[0].shape[0]
    cells_n = outs[0].shape[1]
    ids = lanes_of(tile_rows[...])
    block = min(256, tiles)
    rhs = jnp.concatenate([x for part in parts for x in split_bf16(part[...])], axis=1)

    def some(i, carry):
        at = pl.multiple_of(i * block, block)
        tile = lax.broadcasted_iota(jnp.int32, (block, ids.shape[1]), 0) + at
        hot = jnp.where(tile.astype(f32) == ids, 1.0, 0.0).astype(bf16)
        result = jnp.dot(hot, rhs, preferred_element_type=f32)
        for n, out in enumerate(outs):
            high = result[:, 2 * n * cells_n : (2 * n + 1) * cells_n]
            out[pl.ds(at, block), :] = high + result[:, (2 * n + 1) * cells_n : (2 * n + 2) * cells_n]
        return carry

    lax.fori_loop(0, tiles // block, some, 0)


def flow_plane(s, width, fluid, left, right, source, store):
    comps, _, cells = fluid.shape
    row = lax.broadcasted_iota(jnp.int32, (width, cells), 0)
    lane = lax.broadcasted_iota(jnp.int32, (width, cells), 1)

    def plane(ref, c, n):
        return ref[c, pl.ds(pl.multiple_of(n * width, width), width), :]

    d_s, d_a, d_r, lap, now = [], [], [], [], []
    for c in range(comps):
        x, below, above = (plane(fluid, c, s + n) for n in (1, 0, 2))
        a_down = jnp.where(row == 0, left[c, pl.ds(s, 1), :], pltpu.roll(x, 1, 0))
        a_up = jnp.where(row == width - 1, right[c, pl.ds(s, 1), :], pltpu.roll(x, width - 1, 0))
        r_down = jnp.where(lane == 0, 0.0, pltpu.roll(x, 1, 1))
        r_up = jnp.where(lane == cells - 1, 0.0, pltpu.roll(x, cells - 1, 1))
        now.append(x)
        d_s.append(above - below)
        d_a.append(a_up - a_down)
        d_r.append(r_up - r_down)
        lap.append(above + below + a_up + a_down + r_up + r_down - 6.0 * x)
    half = 0.5 * TIME_STEP
    change = [
        MEAN_FLOW * d_s[0] + d_s[1] + d_a[2] + d_r[3],
        MEAN_FLOW * d_s[1] + d_s[0],
        MEAN_FLOW * d_s[2] + d_a[0],
        MEAN_FLOW * d_s[3] + d_r[0],
    ]
    for c in range(comps):
        new = now[c] - half * change[c] + DIFFUSION * lap[c]
        if c == 0:
            new = new - TIME_STEP * source[pl.ds(pl.multiple_of(s * width, width), width), :]
        store(c, new)


def peer_of(n, streams, azims):
    turn, other = n // streams, n % streams
    step = (turn + 1) // 2 * (2 * (turn % 2) - 1)
    away = (azims // 2 + step + azims) % azims
    stream = (lax.axis_index("stream") + (other + 1) % streams) % streams
    return stream, (lax.axis_index("azim") + away) % azims


def first_kernel(streams, azims, cap, length, width,
                 order_ref, tiles_ref, count_ref, bubbles_hbm, fluid_hbm,
                 fluid_out, arrived, low_out, high_out, left_out, right_out,
                 fluid_v, new_v, low_v, high_v, left_v, right_v, first_v, last_v, zero_v,
                 bubbles_v, now_v, live_v, tile_v, amount_v, place_v, sp, su, sn, send_v, spread_v,
                 source_v, lhs, load_sems, store_sem, own_sem, zero_sems, send_sems, recv_sems,
                 early_send, early_recv, late_send, late_recv):
    devices = streams * azims
    comps, cells_n = fluid_hbm.shape[0], fluid_hbm.shape[2]
    slots, lanes = sp.shape
    stream, azim = lax.axis_index("stream"), lax.axis_index("azim")
    me = stream * azims + azim
    last_stream = streams - 1

    barrier = pltpu.get_barrier_semaphore()

    def greet(n, carry):
        other = (me + n) % devices
        pl.semaphore_signal(
            barrier, inc=1, device_id=(other // azims, other % azims), device_id_type=MESH
        )
        return carry

    lax.fori_loop(1, devices, greet, 0)
    inner = pl.ds(width, length * width)
    loads = [
        pltpu.make_async_copy(fluid_hbm, fluid_v.at[:, inner], load_sems.at[0]),
        pltpu.make_async_copy(bubbles_hbm, bubbles_v, load_sems.at[1]),
    ]
    for load in loads:
        load.start()
    clear_lhs(lhs)
    zero_v[...] = jnp.zeros_like(zero_v)

    @pl.when(stream == 0)
    def _():
        low_v[...] = jnp.zeros_like(low_v)

    @pl.when(stream == last_stream)
    def _():
        high_v[...] = jnp.zeros_like(high_v)

    columns = cell_columns(cells_n, lanes)
    tiles = cells_n // 8
    per = max(1, CHUNK // cap)
    chunk = per * cap
    chunks = slots // chunk
    for load in loads:
        load.wait()

    def sample(i):
        for q in range(chunk // QUAD):
            positions = []

            def rows_of(j, q=q):
                k = q * QUAD + j
                peer_stream, peer_azim = peer_of(i * per + k // cap, streams, azims)
                slot = (peer_stream * azims + peer_azim) * cap + k % cap
                block = order_ref[slot]
                tile = tiles_ref[block]
                at = i * chunk + k
                for c in range(STATES):
                    now_v[c, pl.ds(at, 1), :] = bubbles_v[pl.ds(c * slots + block, 1), :]
                live = jnp.where(block < count_ref[0], 1.0, 0.0)
                live_v[pl.ds(at, 1), :] = jnp.full((1, lanes), live, f32)
                tile_v[pl.ds(at, 1), :] = jnp.full((1, lanes), tile.astype(f32), f32)
                row = tile + width
                positions.append(bubbles_v[pl.ds(2 * slots + block, 1), :])
                return fluid_v[0, pl.ds(row, 1), :], fluid_v[comps - 1, pl.ds(row, 1), :]

            rows = [rows_of(j) for j in range(QUAD)]
            at = i * chunk + q * QUAD
            sample_quad(q, at, positions, columns, lambda j: rows[j], lhs, sp, su, sn)

    def advance(i):
        for g in range(chunk // GROUP):
            at = pl.ds(pl.multiple_of(i * chunk + g * GROUP, GROUP), GROUP)
            live = live_v[at, :] > 0.5
            state = [now_v[c, at, :] for c in range(STATES)]
            state[0] = jnp.where(live, state[0], 1.0)
            state[4] = jnp.where(live, state[4], 1.0)
            new = advance_group(state, sp[at, :], su[at, :], sn[at, :])
            amount_v[at, :] = jnp.where(live, source_amount(new[0], new[1]), 0.0)
            place_v[at, :] = new[2]
            new = (jnp.where(live, new[0], -1.0),) + tuple(new[1:])
            piece = min(cap, GROUP)
            for k in range(0, GROUP, piece):
                n = g * GROUP + k
                for c in range(STATES):
                    send_v[i * per + n // cap, c, n % cap : n % cap + piece, :] = new[c][k : k + piece]

    def spread(i):
        for g in range(chunk // GROUP):
            base = pl.multiple_of(i * chunk + g * GROUP, GROUP)
            amount = amount_v[pl.ds(base, GROUP), :]
            for pair in range(GROUP // 2):
                positions = [place_v[pl.ds(base + 2 * pair + n, 1), :] for n in range(2)]
                rows = spread_pair(pair, positions, [amount], columns, tiles)
                for n in range(2):
                    spread_v[pl.ds(base + 2 * pair + n, 1), :] = rows[n]

    def to_peer(n):
        peer = peer_of(n, streams, azims)
        return pltpu.make_async_remote_copy(
            src_ref=send_v.at[n], dst_ref=arrived.at[me], send_sem=send_sems.at[n],
            recv_sem=recv_sems.at[me], device_id=peer, device_id_type=MESH,
        )

    def from_peer(other):
        return pltpu.make_async_remote_copy(
            src_ref=send_v.at[0], dst_ref=arrived.at[other], send_sem=send_sems.at[0],
            recv_sem=recv_sems.at[other], device_id=(other // azims, other % azims),
            device_id_type=MESH,
        )

    own = pltpu.make_async_copy(send_v.at[devices - 1], arrived.at[me], own_sem)

    def send(i, end=False):
        for q in range(per):
            if end and q == per - 1:
                own.start()
            else:
                to_peer(i * per + q).start()

    def halo_copies(ends, cols, lands, sends, recvs):
        def copy(n, src, dst, peer):
            return pltpu.make_async_remote_copy(
                src_ref=src, dst_ref=dst, send_sem=sends.at[n], recv_sem=recvs.at[n],
                device_id=peer, device_id_type=MESH,
            )

        up, down = (stream + 1) % streams, (stream + streams - 1) % streams
        right, left = (azim + 1) % azims, (azim + azims - 1) % azims
        return (
            copy(0, ends[1], lands[0], (up, azim)),
            copy(1, ends[0], lands[1], (down, azim)),
            copy(2, cols[1], lands[2], (stream, right)),
            copy(3, cols[0], lands[3], (stream, left)),
        )

    def halo_start(copies):
        pl.when(stream < last_stream)(copies[0].start)
        pl.when(stream > 0)(copies[1].start)
        copies[2].start()
        copies[3].start()

    def halo_sent(copies):
        pl.when(stream < last_stream)(copies[0].wait_send)
        pl.when(stream > 0)(copies[1].wait_send)
        copies[2].wait_send()
        copies[3].wait_send()

    def halo_here(copies):
        pl.when(stream > 0)(copies[0].wait_recv)
        pl.when(stream < last_stream)(copies[1].wait_recv)
        copies[2].wait_recv()
        copies[3].wait_recv()

    def ends_of(ref, first):
        return [ref.at[:, pl.ds(width * n, width)] for n in (first, first + length - 1)]

    sample(0)
    def edge(s, carry):
        at = pl.multiple_of((s + 1) * width, width)
        for c in range(comps):
            first_v[c, pl.ds(s, 1), :] = fluid_v[c, pl.ds(at, 1), :]
            last_v[c, pl.ds(s, 1), :] = fluid_v[c, pl.ds(at + width - 1, 1), :]
        return carry

    lax.fori_loop(0, length, edge, 0)
    sample(1)
    advance(0)
    pl.semaphore_wait(barrier, devices - 1)
    early = halo_copies(ends_of(fluid_v, 1), (first_v, last_v), (low_v, high_v, left_v, right_v),
                        early_send, early_recv)
    halo_start(early)

    def steady(i, carry):
        sample(i)
        advance(i - 1)
        spread(i - 2)
        send(i - 2)
        return carry

    lax.fori_loop(2, chunks, steady, 0)
    advance(chunks - 1)
    spread(chunks - 2)
    send(chunks - 2)
    spread(chunks - 1)
    send(chunks - 1, True)
    scatter(tile_v, [spread_v], [source_v])
    halo_here(early)
    halo_sent(early)
    fluid_v[:, pl.ds(0, width), :] = low_v[...]
    fluid_v[:, pl.ds((length + 1) * width, width), :] = high_v[...]

    def flow(s, carry):
        def store(c, new):
            new_v[c, pl.ds(pl.multiple_of(s * width, width), width), :] = new
            first_v[c, pl.ds(s, 1), :] = new[0:1]
            last_v[c, pl.ds(s, 1), :] = new[width - 1 : width]

        flow_plane(s, width, fluid_v, left_v, right_v, source_v, store)
        return carry

    lax.fori_loop(0, length, flow, 0)
    keep = pltpu.make_async_copy(new_v, fluid_out, store_sem)
    keep.start()

    def sent(n, carry):
        to_peer(n).wait_send()
        return carry

    lax.fori_loop(0, devices - 1, sent, 0)
    late = halo_copies(ends_of(new_v, 0), (first_v, last_v), (low_out, high_out, left_out, right_out),
                       late_send, late_recv)
    halo_start(late)
    zeros = [pltpu.make_async_copy(zero_v, out, zero_sems.at[n]) for n, out in enumerate((low_out, high_out))]
    pl.when(stream == 0)(zeros[0].start)
    pl.when(stream == last_stream)(zeros[1].start)
    own.wait()

    def came(n, carry):
        from_peer((me + n) % devices).wait_recv()
        return carry

    lax.fori_loop(1, devices, came, 0)
    halo_here(late)
    halo_sent(late)
    pl.when(stream == 0)(zeros[0].wait)
    pl.when(stream == last_stream)(zeros[1].wait)
    keep.wait()


def first_step(fluid, order, tiles_ids, counts, bubbles, length, width):
    streams, azims = lax.axis_size("stream"), lax.axis_size("azim")
    devices = streams * azims
    comps, tiles, cells = fluid.shape
    slots, lanes = order.shape[0], bubbles.shape[1]
    cap = slots // devices

    def out(*shape):
        return jax.ShapeDtypeStruct(shape, f32)

    def buffer(*shape):
        return pltpu.VMEM(shape, f32)

    def dma(*shape):
        return pltpu.SemaphoreType.DMA(shape)

    end, side = (comps, width, cells), (comps, length, cells)
    per_slot = buffer(slots, lanes)
    anywhere = pl.BlockSpec(memory_space=pl.ANY)
    return pl.pallas_call(
        functools.partial(first_kernel, streams, azims, cap, length, width),
        out_shape=(out(*fluid.shape), out(devices, STATES, cap, lanes),
                   out(*end), out(*end), out(*side), out(*side)),
        in_specs=[pl.BlockSpec(memory_space=pltpu.SMEM)] * 3 + [anywhere] * 2,
        out_specs=(anywhere,) * 6,
        scratch_shapes=[
            buffer(comps, tiles + 2 * width, cells), buffer(*fluid.shape),
            buffer(*end), buffer(*end), buffer(*side), buffer(*side), buffer(*side), buffer(*side),
            buffer(*end), buffer(*bubbles.shape), buffer(STATES, slots, lanes),
            per_slot, per_slot, per_slot, per_slot, per_slot, per_slot, per_slot,
            buffer(devices, STATES, cap, lanes), buffer(slots, cells), buffer(tiles, cells),
            buffer(max(cap, CHUNK) // QUAD, 16, 2 * cells),
            dma(2), dma(), dma(), dma(2), dma(devices), dma(devices), dma(4), dma(4), dma(4), dma(4),
        ],
        compiler_params=pltpu.CompilerParams(
            vmem_limit_bytes=VMEM_GRANT, collective_id=0, has_side_effects=True
        ),
        cost_estimate=pl.CostEstimate(
            flops=slots * lanes * cells * 2000, bytes_accessed=12 * 2**20,
            transcendentals=2 * slots * lanes * cells,
        ),
        name="first_step",
    )(order, tiles_ids, counts, bubbles, fluid)


def second_kernel(live_ref, tiles_ref, arrived_ref, p_ref, u_ref,
                  bubbles_out, source_ref, void_ref,
                  now_v, tile_v, amount_v, volume_v, new_v, sp, su, sn, rows_v, voids_v, lhs, list_ref):
    cells_n, lanes = p_ref.shape[-1], sp.shape[1]
    cap = arrived_ref.shape[2]
    slots = tiles_ref.shape[0]
    columns = cell_columns(cells_n, lanes)
    tiles = cells_n // 8
    clear_lhs(lhs)
    bubbles_out[...] = jnp.zeros_like(bubbles_out)
    tile_v[...] = jnp.full(tile_v.shape, -1.0, f32)
    rows_v[...] = jnp.zeros_like(rows_v)
    voids_v[...] = jnp.zeros_like(voids_v)

    def keep(i, n):
        for k in range(GROUP):
            list_ref[n] = i * GROUP + k
            n = n + live_ref[i * GROUP + k]
        return n

    number = lax.fori_loop(0, slots // GROUP, keep, 0)
    chunks = (number + CHUNK - 1) // CHUNK

    def pad(i, carry):
        list_ref[i] = list_ref[0]
        return carry

    lax.fori_loop(number, jnp.maximum(chunks, 1) * CHUNK, pad, 0)

    def sample(i):
        for q in range(CHUNK // QUAD):
            at = i * CHUNK + q * QUAD
            rows, positions = [], []
            for j in range(QUAD):
                slot = list_ref[at + j]
                tile = tiles_ref[slot]
                for c in range(STATES):
                    now_v[c, pl.ds(at + j, 1), :] = arrived_ref[slot // cap, c, pl.ds(slot % cap, 1), :]
                tile_v[pl.ds(at + j, 1), :] = jnp.full((1, lanes), tile.astype(f32), f32)
                positions.append(arrived_ref[slot // cap, 2, pl.ds(slot % cap, 1), :])
                rows.append((p_ref[0, pl.ds(tile, 1), :], u_ref[0, pl.ds(tile, 1), :]))
            sample_quad(q, at, positions, columns, lambda j: rows[j], lhs, sp, su, sn)

    def advance(i):
        for g in range(CHUNK // GROUP):
            base = pl.multiple_of(i * CHUNK + g * GROUP, GROUP)
            at = pl.ds(base, GROUP)
            state = [now_v[c, at, :] for c in range(STATES)]
            new = advance_group(state, sp[at, :], su[at, :], sn[at, :])
            live = base + lax.broadcasted_iota(jnp.int32, (GROUP, lanes), 0) < number
            amount_v[at, :] = jnp.where(live, source_amount(new[0], new[1]), 0.0)
            volume_v[at, :] = jnp.where(live, void_amount(new[0]), 0.0)
            for c in range(STATES):
                new_v[c, at, :] = new[c]

    def spread(i):
        for g in range(CHUNK // GROUP):
            base = pl.multiple_of(i * CHUNK + g * GROUP, GROUP)
            amounts = [amount_v[pl.ds(base, GROUP), :], volume_v[pl.ds(base, GROUP), :]]
            for pair in range(GROUP // 2):
                positions = [new_v[2, pl.ds(base + 2 * pair + n, 1), :] for n in range(2)]
                rows = spread_pair(pair, positions, amounts, columns, tiles)
                for n in range(2):
                    at = base + 2 * pair + n
                    rows_v[pl.ds(at, 1), :] = rows[n]
                    voids_v[pl.ds(at, 1), :] = rows[2 + n]
                    slot = list_ref[at]
                    for c in range(STATES):
                        bubbles_out[pl.ds(c * slots + slot, 1), :] = new_v[c, pl.ds(at, 1), :]

    @pl.when(number > 0)
    def _():
        sample(0)
        sample(jnp.minimum(1, chunks - 1))
        advance(0)

        def steady(i, carry):
            sample(jnp.minimum(i, chunks - 1))
            advance(i - 1)
            spread(i - 2)
            return carry

        lax.fori_loop(2, chunks + 1, steady, 0)
        spread(chunks - 1)

    scatter(tile_v, [rows_v, voids_v], [source_ref, void_ref])


def whole(shape):
    return pl.BlockSpec(tuple(shape), lambda i: (0,) * len(shape))


def bubbles_second(fluid, live, tiles_ids, arrived):
    comps, tiles, cells = fluid.shape
    slots, lanes = tiles_ids.shape[0], arrived.shape[3]

    def out(*shape):
        return jax.ShapeDtypeStruct(shape, f32)

    def buffer(*shape):
        return pltpu.VMEM(shape, f32)

    per_slot = buffer(slots, lanes)
    outs = (out(STATES * slots, lanes), out(tiles, cells), out(tiles, cells))
    return pl.pallas_call(
        second_kernel,
        grid=(1,),
        out_shape=outs,
        in_specs=[pl.BlockSpec(memory_space=pltpu.SMEM)] * 2 + [
            whole(arrived.shape),
            pl.BlockSpec((1, tiles, cells), lambda i: (0, 0, 0)),
            pl.BlockSpec((1, tiles, cells), lambda i: (comps - 1, 0, 0)),
        ],
        out_specs=tuple(whole(o.shape) for o in outs),
        scratch_shapes=[
            buffer(STATES, slots, lanes), per_slot, per_slot, per_slot, buffer(STATES, slots, lanes),
            per_slot, per_slot, per_slot, buffer(slots, cells), buffer(slots, cells),
            buffer(CHUNK // QUAD, 16, 2 * cells), pltpu.SMEM((slots + CHUNK,), jnp.int32),
        ],
        compiler_params=pltpu.CompilerParams(vmem_limit_bytes=VMEM_GRANT),
        cost_estimate=pl.CostEstimate(
            flops=slots * lanes * cells * 2000, bytes_accessed=6 * 2**20,
            transcendentals=2 * slots * lanes * cells,
        ),
        name="bubbles_second",
    )(live, tiles_ids, arrived, fluid, fluid)


def flow_kernel(f_ref, before_ref, after_ref, low_ref, high_ref, left_ref, right_ref, source_ref, out_ref, window):
    step, steps = pl.program_id(0), pl.num_programs(0)
    comps, rows, cells = f_ref.shape
    width = low_ref.shape[1]
    depth = rows // width
    window[:, pl.ds(0, width), :] = jnp.where(step == 0, low_ref[...], before_ref[...])
    window[:, pl.ds((depth + 1) * width, width), :] = jnp.where(step == steps - 1, high_ref[...], after_ref[...])
    window[:, pl.ds(width, rows), :] = f_ref[...]

    def flow(s, carry):
        def store(c, new):
            out_ref[c, pl.ds(pl.multiple_of(s * width, width), width), :] = new

        flow_plane(s, width, window, left_ref, right_ref, source_ref, store)
        return carry

    lax.fori_loop(0, depth, flow, 0)


def flow_second(fluid, low, high, left, right, source):
    comps, tiles, cells = fluid.shape
    width, length = low.shape[1], left.shape[1]
    depth = 16
    rows = depth * width
    side = pl.BlockSpec((comps, depth, cells), lambda i: (0, i, 0))
    main = pl.BlockSpec((comps, rows, cells), lambda i: (0, i, 0))
    plane = (comps, width, cells)
    return pl.pallas_call(
        flow_kernel,
        grid=(length // depth,),
        out_shape=jax.ShapeDtypeStruct(fluid.shape, f32),
        in_specs=[
            main,
            pl.BlockSpec(plane, lambda i: (0, jnp.maximum(i * depth - 1, 0), 0)),
            pl.BlockSpec(plane, lambda i: (0, jnp.minimum(i * depth + depth, length - 1), 0)),
            whole(plane), whole(plane), side, side,
            pl.BlockSpec((rows, cells), lambda i: (i, 0)),
        ],
        out_specs=main,
        scratch_shapes=[pltpu.VMEM((comps, rows + 2 * width, cells), f32)],
        compiler_params=pltpu.CompilerParams(vmem_limit_bytes=VMEM_GRANT),
        cost_estimate=pl.CostEstimate(
            flops=fluid.size * 30, bytes_accessed=10 * 2**20, transcendentals=0
        ),
        name="flow_second",
    )(fluid, fluid, fluid, low, high, left, right, source)


def on_device(fluid, bubbles, counts, outgoing_block_order, tiles_first_update, tiles_after):
    comps, length, width, cells = fluid.shape
    slots, states, lanes = bubbles.shape
    flat = (comps, length * width, cells)
    bubbles = bubbles.transpose(1, 0, 2).reshape(states * slots, lanes)
    fluid, arrived, low, high, left, right = first_step(
        fluid.reshape(flat), outgoing_block_order, tiles_first_update, counts, bubbles, length, width
    )
    live = (arrived[:, 0, :, 0] * arrived[:, 4, :, 0] >= 0.0).astype(jnp.int32).reshape(slots)
    bubbles, source, void = bubbles_second(fluid, live, tiles_after, arrived)
    fluid = flow_second(fluid, low, high, left, right, source)
    bubbles = bubbles.reshape(states, slots, lanes).transpose(1, 0, 2)
    return fluid.reshape(comps, length, width, cells), bubbles, void.reshape(length, width, cells)


def solution(mesh):
    return jax.shard_map(
        on_device,
        mesh=mesh,
        in_specs=(
            P(None, "stream", "azim", None),
            P(("stream", "azim"), None, None),
            P(("stream", "azim")),
            P(("stream", "azim")),
            P(("stream", "azim")),
            P(("stream", "azim")),
        ),
        out_specs=(
            P(None, "stream", "azim", None),
            P(("stream", "azim"), None, None),
            P("stream", "azim", None),
        ),
        check_vma=False,
    )
```

```python
import functools

import jax
import jax.numpy as jnp
from jax import lax
from jax.experimental import pallas as pl
from jax.experimental.pallas import tpu as pltpu
from jax.sharding import PartitionSpec as P

MESH = pl.DeviceIdType.MESH
SUBSTEPS = 8
TIME_STEP = 0.25
MEAN_FLOW = 0.5
DIFFUSION = 0.1
KERNEL_WIDTH = 1.5
GAS_INDEX = 4.2
PRESSURE_COUPLING = 0.3
AMBIENT = 1.0
RELAX_TIME = 0.5
VISCOUS = 0.08
SOURCE_GAIN = 0.05
VOID_SCALE = 0.01
FOUR_PI = 12.566370614359172
LOG2E = 1.4426950408889634
SHARPNESS = 0.5 * LOG2E / (KERNEL_WIDTH * KERNEL_WIDTH)
GROUP = 8
QUAD = 4
CHUNK = 16
STATES = 5
WIDE = 4
VMEM_GRANT = 60 * 2**20
f32, bf16 = jnp.float32, jnp.bfloat16


SAMPLE_SPANS = (7, 9)
SPREAD_SPANS = (5, 5, 6)


def runs(spans, tiles):
    out, start = [], 0
    while start < tiles:
        end = min(start + spans[len(out) % len(spans)], tiles)
        out.append((start, (start + end - 1) // 2, end))
        start = end
    return out


def cell_columns(cells_n, lanes):
    column = lax.broadcasted_iota(jnp.int32, (8, lanes), 0).astype(f32)
    tiles = cells_n // 8
    middles = sorted({m for spans in (SAMPLE_SPANS, SPREAD_SPANS) for _, m, _ in runs(spans, tiles)})
    return {m: column + float(8 * m) for m in middles}


def raw_weights(position, columns, tiles, spans):
    pieces = [None] * tiles
    for start, middle, end in runs(spans, tiles):
        offset = columns[middle] - position
        slope = offset * -SHARPNESS
        at = slope * offset
        pieces[middle] = jnp.exp2(at)
        for n in range(1, max(end - middle, middle - start + 1)):
            near = at - 64.0 * SHARPNESS * n * n
            step = slope * (16.0 * n)
            if middle - n >= start:
                pieces[middle - n] = jnp.exp2(near - step)
            if middle + n < end:
                pieces[middle + n] = jnp.exp2(near + step)
    return jnp.concatenate(pieces, axis=0)


def split_bf16(values):
    high = values.astype(bf16)
    low = (values - high.astype(f32)).astype(bf16)
    return high, low


def two_parts(rows):
    high = rows.astype(bf16).astype(f32)
    return jnp.concatenate([high, rows - high], axis=0).astype(bf16)


def clear_lhs(lhs):
    cells_n = lhs.shape[2] // 2
    lhs[...] = jnp.zeros_like(lhs)
    one = jnp.ones((1, cells_n), f32)
    for q in range(lhs.shape[0]):
        lhs[q, 4:5, :cells_n] = one
        lhs[q, 12:13, cells_n:] = one


def sample_quad(q, at, positions, columns, rows_of, lhs, sp, su, sn):
    cells_n = lhs.shape[2] // 2
    weights = []
    for j in range(QUAD):
        p_row, u_row = rows_of(j)
        row, side = 8 * (j // 2) + 2 * (j % 2), slice(cells_n * (j // 2), cells_n * (j // 2 + 1))
        lhs[q, row : row + 1, side] = p_row
        lhs[q, row + 1 : row + 2, side] = u_row
        weights.append(raw_weights(positions[j], columns, cells_n // 8, SAMPLE_SPANS).astype(bf16))
    rhs = jnp.concatenate(
        [jnp.concatenate(weights[:2], axis=1), jnp.concatenate(weights[2:], axis=1)], axis=0
    )
    result = jnp.dot(two_parts(lhs[q]), rhs, preferred_element_type=f32)
    result = result[:16] + result[16:]
    lanes = rhs.shape[1] // 2
    for j in range(QUAD):
        row, part = 8 * (j // 2), result[:, lanes * (j % 2) : lanes * (j % 2 + 1)]
        first = row + 2 * (j % 2)
        sp[pl.ds(at + j, 1), :] = part[first : first + 1]
        su[pl.ds(at + j, 1), :] = part[first + 1 : first + 2]
        sn[pl.ds(at + j, 1), :] = part[row + 4 : row + 5]


def drive_of(pressure, velocity, norm):
    inverse = 1.0 / norm
    return AMBIENT + PRESSURE_COUPLING * (pressure * inverse), velocity * inverse


def advance_group(radius, growth, rest, drive, substeps):
    h = TIME_STEP / SUBSTEPS
    for _ in range(substeps):
        over = 1.0 / radius
        gas = jnp.exp2((GAS_INDEX * LOG2E) * jnp.log(rest * over))
        damping = growth * (1.5 * growth + VISCOUS * over)
        growth = growth + (gas - drive - damping) * (h * over)
        radius = radius + h * growth
    return radius, growth


def travel(position, speed, velocity):
    h = TIME_STEP / SUBSTEPS
    keep = 1.0 - h / RELAX_TIME
    lag = speed - velocity
    path = h * sum(keep ** n for n in range(1, SUBSTEPS + 1))
    return position + TIME_STEP * velocity + path * lag, velocity + keep**SUBSTEPS * lag


def source_amount(radius, growth):
    return SOURCE_GAIN * FOUR_PI * radius * radius * growth


def void_amount(radius):
    return VOID_SCALE * FOUR_PI / 3.0 * radius * radius * radius


def spread_pair(pair, positions, amounts, columns, tiles):
    pieces, norms = [], []
    for position in positions:
        raw = raw_weights(position, columns, tiles, SPREAD_SPANS)
        norms.append(jnp.sum(raw, axis=0, keepdims=True))
        pieces.append(jnp.concatenate(split_bf16(raw), axis=1))
    rhs = jnp.concatenate(pieces, axis=0)
    sublane = lax.broadcasted_iota(jnp.int32, amounts[0].shape, 0)
    inverse = 1.0 / jnp.where(sublane == 2 * pair, norms[0], norms[1])
    rows = jnp.concatenate([a * inverse for a in amounts], axis=0)
    lhs = two_parts(rows)
    lhs = jnp.concatenate([lhs, lhs], axis=1)
    result = lax.dot_general(
        lhs, rhs, (((1,), (1,)), ((), ())), preferred_element_type=f32
    )
    result = result[: rows.shape[0]] + result[rows.shape[0] :]
    cells_n = 8 * tiles
    out = []
    for n in range(len(amounts)):
        for side in range(2):
            row = GROUP * n + 2 * pair + side
            out.append(result[row : row + 1, side * cells_n : (side + 1) * cells_n])
    return out


def lanes_of(rows):
    number, lanes = rows.shape
    pieces = []
    for at in range(0, number, lanes):
        block = rows[at : at + lanes]
        same = lax.broadcasted_iota(jnp.int32, block.shape, 0) == lax.broadcasted_iota(
            jnp.int32, block.shape, 1
        )
        line = jnp.sum(jnp.where(same, block, 0.0), axis=0, keepdims=True)
        pieces.append(line[:, : block.shape[0]])
    return jnp.concatenate(pieces, axis=1)


def scatter(tile_rows, parts, tiles, store):
    cells_n = parts[0].shape[1]
    ids = lanes_of(tile_rows[...])
    block = min(256, tiles)
    rhs = jnp.concatenate([x for part in parts for x in split_bf16(part[...])], axis=1)

    def some(i, carry):
        at = pl.multiple_of(i * block, block)
        tile = lax.broadcasted_iota(jnp.int32, (block, ids.shape[1]), 0) + at
        hot = jnp.where(tile.astype(f32) == ids, 1.0, 0.0).astype(bf16)
        result = jnp.dot(hot, rhs, preferred_element_type=f32)
        sums = []
        for n in range(len(parts)):
            high = result[:, 2 * n * cells_n : (2 * n + 1) * cells_n]
            sums.append(high + result[:, (2 * n + 1) * cells_n : (2 * n + 2) * cells_n])
        store(at, block, sums)
        return carry

    lax.fori_loop(0, tiles // block, some, 0)


def flow_plane(s, width, fluid, left, right, new_ref):
    comps, _, cells = fluid.shape
    row = lax.broadcasted_iota(jnp.int32, (width, cells), 0)
    lane = lax.broadcasted_iota(jnp.int32, (width, cells), 1)

    def plane(ref, c, n):
        return ref[c, pl.ds(pl.multiple_of(n * width, width), width), :]

    d_s, d_a, d_r, lap, now = [], [], [], [], []
    for c in range(comps):
        x, below, above = (plane(fluid, c, s + n) for n in (1, 0, 2))
        before = 0.0 if left is None else left[c, pl.ds(s, 1), :]
        after = 0.0 if right is None else right[c, pl.ds(s, 1), :]
        a_down = jnp.where(row == 0, before, pltpu.roll(x, 1, 0))
        a_up = jnp.where(row == width - 1, after, pltpu.roll(x, width - 1, 0))
        r_down = jnp.where(lane == 0, 0.0, pltpu.roll(x, 1, 1))
        r_up = jnp.where(lane == cells - 1, 0.0, pltpu.roll(x, cells - 1, 1))
        now.append(x)
        d_s.append(above - below)
        d_a.append(a_up - a_down)
        d_r.append(r_up - r_down)
        lap.append(above + below + a_up + a_down + r_up + r_down - 6.0 * x)
    half = 0.5 * TIME_STEP
    change = [
        MEAN_FLOW * d_s[0] + d_s[1] + d_a[2] + d_r[3],
        MEAN_FLOW * d_s[1] + d_s[0],
        MEAN_FLOW * d_s[2] + d_a[0],
        MEAN_FLOW * d_s[3] + d_r[0],
    ]
    for c in range(comps):
        at = pl.multiple_of((s + 1) * width, width)
        new_ref[c, pl.ds(at, width), :] = now[c] - half * change[c] + DIFFUSION * lap[c]


def halo_terms(side, sign, stream):
    half = sign * 0.5 * TIME_STEP
    own = DIFFUSION + (half * MEAN_FLOW if stream else 0.0)
    terms = [own * x for x in side]
    other = 1 if stream else 2
    terms[0] = terms[0] + half * side[other]
    terms[other] = terms[other] + half * side[0]
    return terms


def peer_of(n, streams, azims):
    turn, other = n // streams, n % streams
    half = azims // 2
    azim, near = lax.axis_index("azim"), turn // half
    side = (azim // half + 1 + near) % 2
    stream = (lax.axis_index("stream") + (other + 1) % streams) % streams
    return stream, side * half + (azim + turn % half + near) % half


def first_kernel(streams, azims, cap, length, width,
                 order_ref, tiles_ref, count_ref, bubbles_hbm, fluid_hbm,
                 fluid_out, rows_out, arrived, low_2, high_2, left_2, right_2,
                 fluid_v, new_v, rows_in, low_v, high_v, left_v, right_v, first_v, last_v,
                 zero_v, bubbles_v, now_v, mid_v, live_v, tile_v, amount_v, place_v, sp, su, sn, send_v, spread_v,
                 lhs, load_sems, store_sems, own_sem, send_sems, recv_sems,
                 early_send, early_recv, late_send, late_recv, zero_sems):
    devices = streams * azims
    comps, area, cells_n = fluid_hbm.shape
    slots, lanes = sp.shape
    stream, azim = lax.axis_index("stream"), lax.axis_index("azim")
    me = stream * azims + azim
    last_stream = streams - 1

    barrier = pltpu.get_barrier_semaphore()

    def greet(n, carry):
        other = (me + n) % devices
        pl.semaphore_signal(
            barrier, inc=1, device_id=(other // azims, other % azims), device_id_type=MESH
        )
        return carry

    lax.fori_loop(1, devices, greet, 0)
    inner = pl.ds(width, area)
    loads = [
        pltpu.make_async_copy(bubbles_hbm, bubbles_v, load_sems.at[0]),
        pltpu.make_async_copy(fluid_hbm.at[0], rows_in.at[0], load_sems.at[1]),
        pltpu.make_async_copy(fluid_hbm.at[comps - 1], rows_in.at[1], load_sems.at[2]),
        pltpu.make_async_copy(fluid_hbm, fluid_v.at[:, inner], load_sems.at[3]),
    ]
    for load in loads:
        load.start()
    clear_lhs(lhs)
    zero_v[...] = jnp.zeros_like(zero_v)

    @pl.when(stream == 0)
    def _():
        low_v[...] = jnp.zeros_like(low_v)

    @pl.when(stream == last_stream)
    def _():
        high_v[...] = jnp.zeros_like(high_v)

    columns = cell_columns(cells_n, lanes)
    tiles = cells_n // 8
    per = max(1, CHUNK // cap)
    chunk = per * cap
    chunks = slots // chunk
    for load in loads[:3]:
        load.wait()

    def groups(i):
        for g in range(chunk // GROUP):
            yield g, pl.ds(pl.multiple_of(i * chunk + g * GROUP, GROUP), GROUP)

    def sample(i):
        for q in range(chunk // QUAD):
            positions = []

            def rows_of(j, q=q):
                k = q * QUAD + j
                peer_stream, peer_azim = peer_of(i * per + k // cap, streams, azims)
                slot = (peer_stream * azims + peer_azim) * cap + k % cap
                block = order_ref[slot]
                tile = tiles_ref[block]
                at = i * chunk + k
                for c in range(STATES):
                    now_v[c, pl.ds(at, 1), :] = bubbles_v[pl.ds(c * slots + block, 1), :]
                live = jnp.where(block < count_ref[0], 1.0, 0.0)
                live_v[pl.ds(at, 1), :] = jnp.full((1, lanes), live, f32)
                tile_v[pl.ds(at, 1), :] = jnp.full((1, lanes), tile.astype(f32), f32)
                positions.append(bubbles_v[pl.ds(2 * slots + block, 1), :])
                return rows_in[0, pl.ds(tile, 1), :], rows_in[1, pl.ds(tile, 1), :]

            rows = [rows_of(j) for j in range(QUAD)]
            at = i * chunk + q * QUAD
            sample_quad(q, at, positions, columns, lambda j: rows[j], lhs, sp, su, sn)

    def advance_start(i):
        for g, at in groups(i):
            live = live_v[at, :] > 0.5
            state = [now_v[c, at, :] for c in range(STATES)]
            state[0] = jnp.where(live, state[0], 1.0)
            state[4] = jnp.where(live, state[4], 1.0)
            drive, velocity = drive_of(sp[at, :], su[at, :], sn[at, :])
            place, speed = travel(state[2], state[3], velocity)
            radius, growth = advance_group(state[0], state[1], state[4], drive, SUBSTEPS // 2)
            for c, x in enumerate((radius, growth, place, speed, state[4], drive)):
                mid_v[c, at, :] = x

    def advance_end(i):
        for g, at in groups(i):
            live = live_v[at, :] > 0.5
            state = [mid_v[c, at, :] for c in range(STATES + 1)]
            new = advance_group(state[0], state[1], state[4], state[5], SUBSTEPS - SUBSTEPS // 2)
            new = new + tuple(state[2:STATES])
            amount_v[at, :] = jnp.where(live, source_amount(new[0], new[1]), 0.0)
            place_v[at, :] = new[2]
            new = (jnp.where(live, new[0], -1.0),) + tuple(new[1:])
            piece = min(cap, GROUP)
            for k in range(0, GROUP, piece):
                n = g * GROUP + k
                for c in range(STATES):
                    send_v[i * per + n // cap, c, n % cap : n % cap + piece, :] = new[c][k : k + piece]

    def spread(i):
        for g in range(chunk // GROUP):
            base = pl.multiple_of(i * chunk + g * GROUP, GROUP)
            amount = amount_v[pl.ds(base, GROUP), :]
            for pair in range(GROUP // 2):
                positions = [place_v[pl.ds(base + 2 * pair + n, 1), :] for n in range(2)]
                rows = spread_pair(pair, positions, [amount], columns, tiles)
                for n in range(2):
                    spread_v[pl.ds(base + 2 * pair + n, 1), :] = rows[n]

    def to_peer(n):
        peer = peer_of(n, streams, azims)
        return pltpu.make_async_remote_copy(
            src_ref=send_v.at[n], dst_ref=arrived.at[me], send_sem=send_sems.at[n],
            recv_sem=recv_sems.at[me], device_id=peer, device_id_type=MESH,
        )

    def from_peer(other):
        return pltpu.make_async_remote_copy(
            src_ref=send_v.at[0], dst_ref=arrived.at[other], send_sem=send_sems.at[0],
            recv_sem=recv_sems.at[other], device_id=(other // azims, other % azims),
            device_id_type=MESH,
        )

    own = pltpu.make_async_copy(send_v.at[devices - 1], arrived.at[me], own_sem)

    def send(i, end=False):
        for q in range(per):
            if end and q == per - 1:
                own.start()
            else:
                to_peer(i * per + q).start()

    def halo_copies(ref, lands, sends, recvs):
        def copy(n, src, dst, peer):
            return pltpu.make_async_remote_copy(
                src_ref=src, dst_ref=dst, send_sem=sends.at[n], recv_sem=recvs.at[n],
                device_id=peer, device_id_type=MESH,
            )

        up, down = (stream + 1) % streams, (stream + streams - 1) % streams
        right, left = (azim + 1) % azims, (azim + azims - 1) % azims
        return (
            copy(0, ref.at[:, pl.ds(width * length, width)], lands[0], (up, azim)),
            copy(1, ref.at[:, pl.ds(width, width)], lands[1], (down, azim)),
            copy(2, last_v, lands[2], (stream, right)),
            copy(3, first_v, lands[3], (stream, left)),
        )

    def halo_start(copies):
        pl.when(stream < last_stream)(copies[0].start)
        pl.when(stream > 0)(copies[1].start)
        copies[2].start()
        copies[3].start()

    def halo_sent(copies):
        pl.when(stream < last_stream)(copies[0].wait_send)
        pl.when(stream > 0)(copies[1].wait_send)
        copies[2].wait_send()
        copies[3].wait_send()

    def halo_here(copies):
        pl.when(stream > 0)(copies[0].wait_recv)
        pl.when(stream < last_stream)(copies[1].wait_recv)
        copies[2].wait_recv()
        copies[3].wait_recv()

    def set_ends(ref, low, high):
        ref[:, pl.ds(0, width), :] = low
        ref[:, pl.ds((length + 1) * width, width), :] = high

    def edges(ref):
        many = 4

        def edge(n, carry):
            for k in range(many):
                s = n * many + k
                at = pl.multiple_of((s + 1) * width, width)
                for c in range(comps):
                    first_v[c, pl.ds(s, 1), :] = ref[c, pl.ds(at, 1), :]
                    last_v[c, pl.ds(s, 1), :] = ref[c, pl.ds(at + width - 1, 1), :]
            return carry

        lax.fori_loop(0, length // many, edge, 0)

    sample(0)
    loads[3].wait()
    edges(fluid_v)
    advance_start(0)
    sample(1)
    pl.semaphore_wait(barrier, devices - 1)
    early = halo_copies(fluid_v, (low_v, high_v, left_v, right_v), early_send, early_recv)
    halo_start(early)
    advance_end(0)
    advance_start(1)
    sample(2)

    def steady(i):
        spread(i - 3)
        advance_end(i - 2)
        advance_start(i - 1)
        sample(i)
        send(i - 3)

    def plain(i, carry):
        steady(i)
        return carry

    planes = 3
    begin = max(3, chunks - pl.cdiv(length, planes))
    planes = pl.cdiv(length, max(1, chunks - begin))

    def with_flow(i, carry):
        for n in range(planes):
            s = jnp.minimum((i - begin) * planes + n, length - 1)
            flow_plane(s, width, fluid_v, left_v, right_v, new_v)
        steady(i)
        return carry

    lax.fori_loop(3, begin, plain, 0)
    halo_here(early)
    set_ends(fluid_v, low_v[...], high_v[...])
    halo_sent(early)
    lax.fori_loop(begin, chunks, with_flow, 0)
    send(chunks - 3)
    spread(chunks - 3)
    advance_end(chunks - 2)
    advance_start(chunks - 1)
    send(chunks - 2)
    spread(chunks - 2)
    advance_end(chunks - 1)
    spread(chunks - 1)
    send(chunks - 1, True)

    def subtract(at, block, parts):
        rows = pl.ds(at + width, block)
        new_v[0, rows, :] = new_v[0, rows, :] - TIME_STEP * parts[0]

    scatter(tile_v, [spread_v], area, subtract)
    edges(new_v)
    late = halo_copies(new_v, (low_2, high_2, left_2, right_2), late_send, late_recv)
    keeps = [
        pltpu.make_async_copy(new_v.at[0, inner], rows_out.at[0], store_sems.at[0]),
        pltpu.make_async_copy(new_v.at[comps - 1, inner], rows_out.at[1], store_sems.at[1]),
    ]
    for keep in keeps:
        keep.start()
    halo_start(late)

    def sent(n, carry):
        to_peer(n).wait_send()
        return carry

    zeros = [pltpu.make_async_copy(zero_v, out, zero_sems.at[n]) for n, out in enumerate((low_2, high_2))]
    pl.when(stream == 0)(zeros[0].start)
    pl.when(stream == last_stream)(zeros[1].start)
    set_ends(new_v, zero_v[...], zero_v[...])
    pieces = 4
    part = length // pieces
    outs = []
    for p in range(pieces):
        def flow(n, carry, p=p):
            for k in range(4):
                flow_plane(p * part + 4 * n + k, width, new_v, None, None, fluid_v)
            return carry

        lax.fori_loop(0, part // 4, flow, 0)
        outs.append(pltpu.make_async_copy(
            fluid_v.at[:, pl.ds((p * part + 1) * width, part * width)],
            fluid_out.at[:, pl.ds(p * part * width, part * width)], store_sems.at[2 + p],
        ))
        outs[p].start()
    lax.fori_loop(0, devices - 1, sent, 0)
    own.wait()

    def came(n, carry):
        from_peer((me + n) % devices).wait_recv()
        return carry

    lax.fori_loop(1, devices, came, 0)
    halo_here(late)
    halo_sent(late)
    pl.when(stream == 0)(zeros[0].wait)
    pl.when(stream == last_stream)(zeros[1].wait)
    for copy in keeps + outs:
        copy.wait()


def shaped(*shape):
    return jax.ShapeDtypeStruct(shape, f32)


def buffer(*shape):
    return pltpu.VMEM(shape, f32)


def dma(*shape):
    return pltpu.SemaphoreType.DMA(shape)


ANYWHERE = pl.BlockSpec(memory_space=pl.ANY)
SCALARS = pl.BlockSpec(memory_space=pltpu.SMEM)


def first_step(fluid, order, tiles_ids, counts, bubbles, length, width):
    streams, azims = lax.axis_size("stream"), lax.axis_size("azim")
    devices = streams * azims
    comps, tiles, cells = fluid.shape
    slots, lanes = order.shape[0], bubbles.shape[1]
    cap = slots // devices
    end, side = buffer(comps, width, cells), buffer(comps, length, cells)
    padded = buffer(comps, tiles + 2 * width, cells)
    per_slot = buffer(slots, lanes)
    return pl.pallas_call(
        functools.partial(first_kernel, streams, azims, cap, length, width),
        out_shape=(shaped(*fluid.shape), shaped(2, tiles, cells), shaped(devices, STATES, cap, lanes),
                   *[shaped(*x.shape) for x in (end, end, side, side)]),
        in_specs=[SCALARS] * 3 + [ANYWHERE] * 2,
        out_specs=(ANYWHERE,) * 7,
        scratch_shapes=[
            padded, padded, buffer(2, tiles, cells), end, end, side, side, side, side,
            end, buffer(*bubbles.shape), buffer(STATES, slots, lanes), buffer(STATES + 1, slots, lanes),
            per_slot, per_slot, per_slot, per_slot, per_slot, per_slot, per_slot,
            buffer(devices, STATES, cap, lanes), buffer(slots, cells),
            buffer(max(cap, CHUNK) // QUAD, 16, 2 * cells),
            dma(4), dma(6), dma(), dma(devices), dma(devices), dma(4), dma(4), dma(4), dma(4), dma(2),
        ],
        compiler_params=pltpu.CompilerParams(
            vmem_limit_bytes=VMEM_GRANT, collective_id=0, has_side_effects=True
        ),
        cost_estimate=pl.CostEstimate(
            flops=slots * lanes * cells * 2000, bytes_accessed=12 * 2**20,
            transcendentals=2 * slots * lanes * cells,
        ),
        name="first_step",
    )(order, tiles_ids, counts, bubbles, fluid)


def live_list(arrived_v, devices, live_v, slots_v, rows_v):
    slots, lanes = live_v.shape
    cap = slots // devices
    for d in range(devices):
        at = d * STATES * cap
        live = arrived_v[at : at + cap, :] * arrived_v[at + 4 * cap : at + 5 * cap, :] >= 0.0
        live_v[d * cap : (d + 1) * cap, :] = jnp.where(live, 1.0, 0.0)
    live = live_v[...]
    row = lax.broadcasted_iota(jnp.int32, (slots, slots), 0)
    column = lax.broadcasted_iota(jnp.int32, (slots, slots), 1)
    before = jnp.where(column < row, 1.0, 0.0).astype(bf16)
    rank = jnp.dot(before, live.astype(bf16), preferred_element_type=f32)
    number = jnp.dot(jnp.ones((16, slots), bf16), live.astype(bf16), preferred_element_type=f32)
    rank = jnp.where(live > 0.5, rank, -1.0)
    place = lax.broadcasted_iota(jnp.int32, (slots, lanes), 1).astype(f32)
    hot = [
        jnp.where(rank - float(at) == place, 1.0, 0.0).astype(bf16)[:, : min(lanes, slots - at)]
        for at in range(0, slots, lanes)
    ]
    which = lax.broadcasted_iota(jnp.int32, (16, slots), 0)
    slot = lax.broadcasted_iota(jnp.int32, (16, slots), 1)
    digits = jnp.where(which == 0, slot // cap, slot % cap).astype(f32).astype(bf16)
    found = jnp.dot(digits, jnp.concatenate(hot, axis=1), preferred_element_type=f32)
    entry = lax.broadcasted_iota(jnp.int32, (1, slots), 1).astype(f32)
    for ref, stride in ((slots_v, cap), (rows_v, STATES * cap)):
        line = float(stride) * found[0:1] + found[1:2]
        line = jnp.where(entry < number[0:1, 0:1], line, line[:, 0:1])
        ref[:, :slots] = line.astype(jnp.int32)
        ref[:, slots:] = number[0:1].astype(jnp.int32)


def second_kernel(devices, length, tiles_ref, arrived_hbm, rows_hbm, flow_hbm, low_hbm, high_hbm, left_hbm, right_hbm, fluid_out, bubbles_out, void_out,
                  arrived_v, rows_in, flow_v, low_v, high_v, left_v, right_v, bubbles_v, void_v,
                  now_v, mid_v, fin_v, live_v, tile_v, amount_v, volume_v, sp, su, sn, rows_v, voids_v,
                  lhs, slots_v, places_v, slots_ref, places_ref, load_sems, list_sems, store_sems):
    comps, area, cells_n = flow_hbm.shape
    slots, lanes = sp.shape
    cap = slots // devices
    width = area // length
    loads = [
        pltpu.make_async_copy(arrived_hbm, arrived_v, load_sems.at[0]),
        pltpu.make_async_copy(rows_hbm, rows_in, load_sems.at[1]),
        pltpu.make_async_copy(flow_hbm, flow_v, load_sems.at[2]),
        pltpu.make_async_copy(low_hbm, low_v, load_sems.at[3]),
        pltpu.make_async_copy(high_hbm, high_v, load_sems.at[4]),
        pltpu.make_async_copy(left_hbm, left_v, load_sems.at[5]),
        pltpu.make_async_copy(right_hbm, right_v, load_sems.at[6]),
    ]
    for load in loads:
        load.start()
    columns = cell_columns(cells_n, lanes)
    tiles = cells_n // 8
    clear_lhs(lhs)
    loads[0].wait()
    live_list(arrived_v, devices, live_v, slots_v, places_v)
    lists = [
        pltpu.make_async_copy(slots_v, slots_ref, list_sems.at[0]),
        pltpu.make_async_copy(places_v, places_ref, list_sems.at[1]),
    ]
    for copy in lists:
        copy.start()
    bubbles_v[...] = jnp.zeros_like(bubbles_v)
    tile_v[...] = jnp.full(tile_v.shape, -1.0, f32)
    rows_v[...] = jnp.zeros_like(rows_v)
    voids_v[...] = jnp.zeros_like(voids_v)
    loads[1].wait()
    for copy in lists:
        copy.wait()
    number = slots_ref[0, slots]
    chunks = (number + CHUNK - 1) // CHUNK

    def groups(i):
        for g in range(CHUNK // GROUP):
            base = pl.multiple_of(i * CHUNK + g * GROUP, GROUP)
            yield base, pl.ds(base, GROUP)

    def sample(i):
        for q in range(CHUNK // QUAD):
            at = i * CHUNK + q * QUAD
            rows, positions = [], []
            for j in range(QUAD):
                place = places_ref[0, at + j]
                tile = tiles_ref[slots_ref[0, at + j]]
                for c in range(STATES):
                    now_v[c, pl.ds(at + j, 1), :] = arrived_v[pl.ds(place + c * cap, 1), :]
                tile_v[pl.ds(at + j, 1), :] = jnp.full((1, lanes), tile.astype(f32), f32)
                positions.append(arrived_v[pl.ds(place + 2 * cap, 1), :])
                rows.append((rows_in[0, pl.ds(tile, 1), :], rows_in[1, pl.ds(tile, 1), :]))
            sample_quad(q, at, positions, columns, lambda j: rows[j], lhs, sp, su, sn)

    def advance_start(i):
        for _, at in groups(i):
            state = [now_v[c, at, :] for c in range(STATES)]
            drive, velocity = drive_of(sp[at, :], su[at, :], sn[at, :])
            place, speed = travel(state[2], state[3], velocity)
            radius, growth = advance_group(state[0], state[1], state[4], drive, SUBSTEPS // 2)
            for c, x in enumerate((radius, growth, place, speed, state[4], drive)):
                mid_v[c, at, :] = x

    def advance_end(i):
        for base, at in groups(i):
            state = [mid_v[c, at, :] for c in range(STATES + 1)]
            new = advance_group(state[0], state[1], state[4], state[5], SUBSTEPS - SUBSTEPS // 2)
            new = new + tuple(state[2:STATES])
            live = base + lax.broadcasted_iota(jnp.int32, (GROUP, lanes), 0) < number
            amount_v[at, :] = jnp.where(live, source_amount(new[0], new[1]), 0.0)
            volume_v[at, :] = jnp.where(live, void_amount(new[0]), 0.0)
            for c in range(STATES):
                fin_v[c, at, :] = new[c]

    def spread(i):
        for base, rows_at in groups(i):
            amounts = [amount_v[rows_at, :], volume_v[rows_at, :]]
            for pair in range(GROUP // 2):
                positions = [fin_v[2, pl.ds(base + 2 * pair + n, 1), :] for n in range(2)]
                rows = spread_pair(pair, positions, amounts, columns, tiles)
                for n in range(2):
                    at = base + 2 * pair + n
                    rows_v[pl.ds(at, 1), :] = rows[n]
                    voids_v[pl.ds(at, 1), :] = rows[2 + n]
                    slot = slots_ref[0, at]
                    for c in range(STATES):
                        bubbles_v[pl.ds(c * slots + slot, 1), :] = fin_v[c, pl.ds(at, 1), :]

    @pl.when(number > 0)
    def _():
        def at_most(i):
            return jnp.minimum(i, chunks - 1)

        def before_end(n):
            return jnp.maximum(chunks - n, 0)

        sample(0)
        advance_start(0)
        sample(at_most(1))
        advance_end(0)
        advance_start(at_most(1))
        sample(at_most(2))

        def steady(i, carry):
            spread(i - 3)
            advance_end(i - 2)
            advance_start(i - 1)
            sample(i)
            return carry

        lax.fori_loop(3, chunks, steady, 0)
        spread(before_end(3))
        advance_end(before_end(2))
        advance_start(before_end(1))
        spread(before_end(2))
        advance_end(before_end(1))
        spread(before_end(1))

    def store(n, src, dst):
        copy = pltpu.make_async_copy(src, dst, store_sems.at[n])
        copy.start()
        return copy

    for load in loads[2:]:
        load.wait()
    first, last = pl.ds(0, width), pl.ds(area - width, width)
    begin, end = pl.ds(0, length, stride=width), pl.ds(width - 1, length, stride=width)
    for rows, ref, sign, stream in (
        (first, low_v, 1, True), (last, high_v, -1, True), (begin, left_v, 1, False), (end, right_v, -1, False)
    ):
        for c, term in enumerate(halo_terms([ref[c] for c in range(comps)], sign, stream)):
            flow_v[c, rows, :] = flow_v[c, rows, :] + term
    rest = pl.ds(1, comps - 1)
    stores = [store(0, bubbles_v, bubbles_out), store(1, flow_v.at[rest], fluid_out.at[rest])]

    def finish(at, block, parts):
        rows = pl.ds(at, block)
        flow_v[0, rows, :] = flow_v[0, rows, :] - TIME_STEP * parts[0]
        void_v[rows, :] = parts[1]

    scatter(tile_v, [rows_v, voids_v], area, finish)
    stores += [store(2, flow_v.at[0], fluid_out.at[0]), store(3, void_v, void_out)]
    for copy in stores:
        copy.wait()


def second_step(tiles_ids, arrived, rows, flow, halos):
    comps, tiles, cells = flow.shape
    slots, lanes = tiles_ids.shape[0], arrived.shape[3]
    devices, length = arrived.shape[0], halos[2].shape[1]
    arrived = arrived.reshape(slots * STATES, lanes)
    per_slot = buffer(slots, lanes)
    return pl.pallas_call(
        functools.partial(second_kernel, devices, length),
        out_shape=(shaped(*flow.shape), shaped(STATES * slots, lanes), shaped(tiles, cells)),
        in_specs=[SCALARS] + [ANYWHERE] * 7,
        out_specs=(ANYWHERE,) * 3,
        scratch_shapes=[
            buffer(*arrived.shape), buffer(*rows.shape), buffer(*flow.shape),
            *[buffer(*x.shape) for x in halos],
            buffer(STATES * slots, lanes), buffer(tiles, cells),
            buffer(STATES, slots, lanes), buffer(STATES + 1, slots, lanes), buffer(STATES, slots, lanes),
            per_slot, per_slot, per_slot, per_slot, per_slot, per_slot, per_slot,
            buffer(slots, cells), buffer(slots, cells),
            buffer(CHUNK // QUAD, 16, 2 * cells),
            *[space((1, slots + lanes), jnp.int32) for space in (pltpu.VMEM, pltpu.VMEM, pltpu.SMEM, pltpu.SMEM)],
            dma(7), dma(2), dma(4),
        ],
        compiler_params=pltpu.CompilerParams(vmem_limit_bytes=VMEM_GRANT),
        cost_estimate=pl.CostEstimate(
            flops=slots * lanes * cells * 2000, bytes_accessed=6 * 2**20,
            transcendentals=2 * slots * lanes * cells,
        ),
        name="second_step",
    )(tiles_ids, arrived, rows, flow, *halos)


def on_device(fluid, bubbles, counts, outgoing_block_order, tiles_first_update, tiles_after):
    comps, length, width, cells = fluid.shape
    slots, states, lanes = bubbles.shape
    flat = (comps, length * width, cells)
    bubbles = bubbles.transpose(1, 0, 2).reshape(states * slots, lanes)
    flow, rows, arrived, *halos = first_step(
        fluid.reshape(flat), outgoing_block_order, tiles_first_update, counts, bubbles, length, width
    )
    fluid, bubbles, void = second_step(tiles_after, arrived, rows, flow, halos)
    bubbles = bubbles.reshape(states, slots, lanes).transpose(1, 0, 2)
    return fluid.reshape(comps, length, width, cells), bubbles, void.reshape(length, width, cells)


def solution(mesh):
    return jax.shard_map(
        on_device,
        mesh=mesh,
        in_specs=(
            P(None, "stream", "azim", None),
            P(("stream", "azim"), None, None),
            P(("stream", "azim")),
            P(("stream", "azim")),
            P(("stream", "azim")),
            P(("stream", "azim")),
        ),
        out_specs=(
            P(None, "stream", "azim", None),
            P(("stream", "azim"), None, None),
            P("stream", "azim", None),
        ),
        check_vma=False,
    )
```

```python
import functools

import jax
import jax.numpy as jnp
from jax import lax
from jax.experimental import pallas as pl
from jax.experimental.pallas import tpu as pltpu
from jax.sharding import PartitionSpec as P

MESH = pl.DeviceIdType.MESH
SUBSTEPS = 8
TIME_STEP = 0.25
MEAN_FLOW = 0.5
DIFFUSION = 0.1
KERNEL_WIDTH = 1.5
GAS_INDEX = 4.2
PRESSURE_COUPLING = 0.3
AMBIENT = 1.0
RELAX_TIME = 0.5
VISCOUS = 0.08
SOURCE_GAIN = 0.05
VOID_SCALE = 0.01
FOUR_PI = 12.566370614359172
LOG2E = 1.4426950408889634
SHARPNESS = 0.5 * LOG2E / (KERNEL_WIDTH * KERNEL_WIDTH)
GROUP = 8
QUAD = 4
CHUNK = 16
STATES = 5
WIDE = 4
VMEM_GRANT = 60 * 2**20
f32, bf16 = jnp.float32, jnp.bfloat16


SAMPLE_SPANS = (7, 9)
SPREAD_SPANS = (5, 5, 6)


def runs(spans, tiles):
    out, start = [], 0
    while start < tiles:
        end = min(start + spans[len(out) % len(spans)], tiles)
        out.append((start, (start + end - 1) // 2, end))
        start = end
    return out


def cell_columns(cells_n, lanes):
    column = lax.broadcasted_iota(jnp.int32, (8, lanes), 0).astype(f32)
    tiles = cells_n // 8
    middles = sorted({m for spans in (SAMPLE_SPANS, SPREAD_SPANS) for _, m, _ in runs(spans, tiles)})
    return {m: column + float(8 * m) for m in middles}


def raw_weights(position, columns, tiles, spans):
    pieces = [None] * tiles
    for start, middle, end in runs(spans, tiles):
        offset = columns[middle] - position
        slope = offset * -SHARPNESS
        at = slope * offset
        pieces[middle] = jnp.exp2(at)
        for n in range(1, max(end - middle, middle - start + 1)):
            near = at - 64.0 * SHARPNESS * n * n
            step = slope * (16.0 * n)
            if middle - n >= start:
                pieces[middle - n] = jnp.exp2(near - step)
            if middle + n < end:
                pieces[middle + n] = jnp.exp2(near + step)
    return jnp.concatenate(pieces, axis=0)


def split_bf16(values):
    high = values.astype(bf16)
    low = (values - high.astype(f32)).astype(bf16)
    return high, low


def two_parts(rows):
    high = rows.astype(bf16).astype(f32)
    return jnp.concatenate([high, rows - high], axis=0).astype(bf16)


def clear_lhs(lhs):
    cells_n = lhs.shape[2] // 2
    lhs[...] = jnp.zeros_like(lhs)
    one = jnp.ones((1, cells_n), f32)
    for q in range(lhs.shape[0]):
        lhs[q, 4:5, :cells_n] = one
        lhs[q, 12:13, cells_n:] = one


def sample_quad(q, at, positions, columns, rows_of, lhs, sp, su, sn):
    cells_n = lhs.shape[2] // 2
    weights = []
    for j in range(QUAD):
        p_row, u_row = rows_of(j)
        row, side = 8 * (j // 2) + 2 * (j % 2), slice(cells_n * (j // 2), cells_n * (j // 2 + 1))
        lhs[q, row : row + 1, side] = p_row
        lhs[q, row + 1 : row + 2, side] = u_row
        weights.append(raw_weights(positions[j], columns, cells_n // 8, SAMPLE_SPANS).astype(bf16))
    rhs = jnp.concatenate(
        [jnp.concatenate(weights[:2], axis=1), jnp.concatenate(weights[2:], axis=1)], axis=0
    )
    result = jnp.dot(two_parts(lhs[q]), rhs, preferred_element_type=f32)
    result = result[:16] + result[16:]
    lanes = rhs.shape[1] // 2
    for j in range(QUAD):
        row, part = 8 * (j // 2), result[:, lanes * (j % 2) : lanes * (j % 2 + 1)]
        first = row + 2 * (j % 2)
        sp[pl.ds(at + j, 1), :] = part[first : first + 1]
        su[pl.ds(at + j, 1), :] = part[first + 1 : first + 2]
        sn[pl.ds(at + j, 1), :] = part[row + 4 : row + 5]


def drive_of(pressure, velocity, norm):
    inverse = 1.0 / norm
    return AMBIENT + PRESSURE_COUPLING * (pressure * inverse), velocity * inverse


def advance_group(radius, growth, rest, drive, substeps):
    h = TIME_STEP / SUBSTEPS
    for _ in range(substeps):
        over = 1.0 / radius
        gas = jnp.exp2((GAS_INDEX * LOG2E) * jnp.log(rest * over))
        damping = growth * (1.5 * growth + VISCOUS * over)
        growth = growth + (gas - drive - damping) * (h * over)
        radius = radius + h * growth
    return radius, growth


def travel(position, speed, velocity):
    h = TIME_STEP / SUBSTEPS
    keep = 1.0 - h / RELAX_TIME
    lag = speed - velocity
    path = h * sum(keep ** n for n in range(1, SUBSTEPS + 1))
    return position + TIME_STEP * velocity + path * lag, velocity + keep**SUBSTEPS * lag


def source_amount(radius, growth):
    return SOURCE_GAIN * FOUR_PI * radius * radius * growth


def void_amount(radius):
    return VOID_SCALE * FOUR_PI / 3.0 * radius * radius * radius


def spread_pair(pair, positions, amounts, columns, tiles):
    pieces, norms = [], []
    for position in positions:
        raw = raw_weights(position, columns, tiles, SPREAD_SPANS)
        norms.append(jnp.sum(raw, axis=0, keepdims=True))
        pieces.append(jnp.concatenate(split_bf16(raw), axis=1))
    rhs = jnp.concatenate(pieces, axis=0)
    sublane = lax.broadcasted_iota(jnp.int32, amounts[0].shape, 0)
    inverse = 1.0 / jnp.where(sublane == 2 * pair, norms[0], norms[1])
    rows = jnp.concatenate([a * inverse for a in amounts], axis=0)
    lhs = two_parts(rows)
    lhs = jnp.concatenate([lhs, lhs], axis=1)
    result = lax.dot_general(
        lhs, rhs, (((1,), (1,)), ((), ())), preferred_element_type=f32
    )
    result = result[: rows.shape[0]] + result[rows.shape[0] :]
    cells_n = 8 * tiles
    out = []
    for n in range(len(amounts)):
        for side in range(2):
            row = GROUP * n + 2 * pair + side
            out.append(result[row : row + 1, side * cells_n : (side + 1) * cells_n])
    return out


def spread_quad(quad, positions, amounts, columns, tiles):
    weights, norms = [], []
    for position in positions:
        raw = raw_weights(position, columns, tiles, SPREAD_SPANS)
        norms.append(jnp.sum(raw, axis=0, keepdims=True))
        weights.append(raw.astype(bf16))
    rhs = jnp.concatenate(
        [jnp.concatenate(weights[0::2], axis=1), jnp.concatenate(weights[1::2], axis=1)], axis=0
    )
    row = lax.broadcasted_iota(jnp.int32, amounts.shape, 0) % QUAD
    norm = jnp.where(
        row < 2, jnp.where(row == 0, norms[0], norms[1]), jnp.where(row == 2, norms[2], norms[3])
    )
    parts = two_parts(amounts / norm)
    none = jnp.zeros_like(parts)
    lhs = jnp.concatenate(
        [jnp.concatenate([parts, none], axis=1), jnp.concatenate([none, parts], axis=1)], axis=0
    )
    result = lax.dot_general(
        lhs, rhs, (((1,), (1,)), ((), ())), preferred_element_type=f32
    )
    size, cells_n = amounts.shape[0], 8 * tiles
    out = []
    for j in range(QUAD):
        first = (j // 2) * 2 * size + QUAD * quad + j
        side = slice((j % 2) * cells_n, (j % 2 + 1) * cells_n)
        out.append(result[first : first + 1, side] + result[first + size : first + size + 1, side])
    return out


def lanes_of(rows):
    number, lanes = rows.shape
    pieces = []
    for at in range(0, number, lanes):
        block = rows[at : at + lanes]
        same = lax.broadcasted_iota(jnp.int32, block.shape, 0) == lax.broadcasted_iota(
            jnp.int32, block.shape, 1
        )
        line = jnp.sum(jnp.where(same, block, 0.0), axis=0, keepdims=True)
        pieces.append(line[:, : block.shape[0]])
    return jnp.concatenate(pieces, axis=1)


def scatter(tile_rows, parts, tiles, store):
    cells_n = parts[0].shape[1]
    ids = lanes_of(tile_rows[...])
    block = min(256, tiles)
    rhs = jnp.concatenate([x for part in parts for x in split_bf16(part[...])], axis=1)

    def some(i, carry):
        at = pl.multiple_of(i * block, block)
        tile = lax.broadcasted_iota(jnp.int32, (block, ids.shape[1]), 0) + at
        hot = jnp.where(tile.astype(f32) == ids, 1.0, 0.0).astype(bf16)
        result = jnp.dot(hot, rhs, preferred_element_type=f32)
        sums = []
        for n in range(len(parts)):
            high = result[:, 2 * n * cells_n : (2 * n + 1) * cells_n]
            sums.append(high + result[:, (2 * n + 1) * cells_n : (2 * n + 2) * cells_n])
        store(at, block, sums)
        return carry

    lax.fori_loop(0, tiles // block, some, 0)


def flow_plane(s, width, fluid, new_ref):
    comps, _, cells = fluid.shape
    row = lax.broadcasted_iota(jnp.int32, (width, cells), 0)
    lane = lax.broadcasted_iota(jnp.int32, (width, cells), 1)

    def plane(ref, c, n):
        return ref[c, pl.ds(pl.multiple_of(n * width, width), width), :]

    d_s, d_a, d_r, lap, now = [], [], [], [], []
    for c in range(comps):
        x, below, above = (plane(fluid, c, s + n) for n in (1, 0, 2))
        a_down = jnp.where(row == 0, 0.0, pltpu.roll(x, 1, 0))
        a_up = jnp.where(row == width - 1, 0.0, pltpu.roll(x, width - 1, 0))
        r_down = jnp.where(lane == 0, 0.0, pltpu.roll(x, 1, 1))
        r_up = jnp.where(lane == cells - 1, 0.0, pltpu.roll(x, cells - 1, 1))
        now.append(x)
        d_s.append(above - below)
        d_a.append(a_up - a_down)
        d_r.append(r_up - r_down)
        lap.append(above + below + a_up + a_down + r_up + r_down - 6.0 * x)
    half = 0.5 * TIME_STEP
    change = [
        MEAN_FLOW * d_s[0] + d_s[1] + d_a[2] + d_r[3],
        MEAN_FLOW * d_s[1] + d_s[0],
        MEAN_FLOW * d_s[2] + d_a[0],
        MEAN_FLOW * d_s[3] + d_r[0],
    ]
    for c in range(comps):
        at = pl.multiple_of((s + 1) * width, width)
        new_ref[c, pl.ds(at, width), :] = now[c] - half * change[c] + DIFFUSION * lap[c]


def halo_terms(side, sign, stream):
    half = sign * 0.5 * TIME_STEP
    own = DIFFUSION + (half * MEAN_FLOW if stream else 0.0)
    terms = [own * x for x in side]
    other = 1 if stream else 2
    terms[0] = terms[0] + half * side[other]
    terms[other] = terms[other] + half * side[0]
    return terms


def add_halos(ref, start, length, width, low, high, left, right):
    comps = ref.shape[0]
    for at, number, stride, side, sign in (
        (start, width, 1, low, 1), (start + (length - 1) * width, width, 1, high, -1),
        (start, length, width, left, 1), (start + width - 1, length, width, right, -1),
    ):
        rows = pl.ds(at, number) if stride == 1 else pl.ds(at, number, stride=stride)
        terms = halo_terms([side[c] for c in range(comps)], sign, stride == 1)
        terms = [ref[c, rows, :] + term for c, term in enumerate(terms)]
        for c, term in enumerate(terms):
            ref[c, rows, :] = term


def peer_of(n, streams, azims):
    turn, other = n // streams, n % streams
    step = (turn + 1) // 2 * (2 * (turn % 2) - 1)
    away = (azims // 2 + step + azims) % azims
    stream = (lax.axis_index("stream") + (other + 1) % streams) % streams
    return stream, (lax.axis_index("azim") + away) % azims


def source_of(n, streams, azims):
    turn, other = n // streams, n % streams
    step = (turn + 1) // 2 * (2 * (turn % 2) - 1)
    away = (azims // 2 + step + azims) % azims
    stream = (lax.axis_index("stream") + streams - (other + 1) % streams) % streams
    return stream * azims + (lax.axis_index("azim") + azims - away) % azims


def first_kernel(streams, azims, cap, length, width, soon,
                 order_ref, tiles_ref, after_ref, count_ref, bubbles_hbm, fluid_hbm,
                 fluid_out, rows_out, arrived, low_2, high_2, left_2, right_2,
                 bubbles_out, spread_out, void_out, tile_out,
                 fluid_v, new_v, rows_in, low_v, high_v, left_v, right_v, first_v, last_v,
                 zero_v, bubbles_v, now_v, mid_v, live_v, tile_v, amount_v, place_v, sp, su, sn, send_v, spread_v,
                 soon_v, dead_v, fin_v, volume_v, void_v,
                 lhs, load_sems, store_sems, own_sem, dead_sems, send_sems, recv_sems,
                 early_send, early_recv, late_send, late_recv, zero_sems):
    devices = streams * azims
    comps, area, cells_n = fluid_hbm.shape
    slots, lanes = sp.shape
    stream, azim = lax.axis_index("stream"), lax.axis_index("azim")
    me = stream * azims + azim
    last_stream = streams - 1

    barrier = pltpu.get_barrier_semaphore()

    def greet(n, carry):
        other = (me + n) % devices
        pl.semaphore_signal(
            barrier, inc=1, device_id=(other // azims, other % azims), device_id_type=MESH
        )
        return carry

    lax.fori_loop(1, devices, greet, 0)
    inner = pl.ds(width, area)
    loads = [
        pltpu.make_async_copy(bubbles_hbm, bubbles_v, load_sems.at[0]),
        pltpu.make_async_copy(fluid_hbm.at[0], rows_in.at[0], load_sems.at[1]),
        pltpu.make_async_copy(fluid_hbm.at[comps - 1], rows_in.at[1], load_sems.at[2]),
        pltpu.make_async_copy(fluid_hbm, fluid_v.at[:, inner], load_sems.at[3]),
    ]
    for load in loads[:3]:
        load.start()
    clear_lhs(lhs)
    zero_v[...] = jnp.zeros_like(zero_v)

    @pl.when(stream == 0)
    def _():
        low_v[...] = jnp.zeros_like(low_v)

    @pl.when(stream == last_stream)
    def _():
        high_v[...] = jnp.zeros_like(high_v)

    columns = cell_columns(cells_n, lanes)
    tiles = cells_n // 8
    per = max(1, CHUNK // cap)
    chunk = per * cap
    chunks = slots // chunk
    for load in loads[:3]:
        load.wait()
    loads[3].start()

    def groups(i):
        for g in range(chunk // GROUP):
            yield g, pl.ds(pl.multiple_of(i * chunk + g * GROUP, GROUP), GROUP)

    def sample(i):
        for q in range(chunk // QUAD):
            positions = []

            def rows_of(j, q=q):
                k = q * QUAD + j
                peer_stream, peer_azim = peer_of(i * per + k // cap, streams, azims)
                slot = (peer_stream * azims + peer_azim) * cap + k % cap
                block = order_ref[slot]
                tile = tiles_ref[block]
                at = i * chunk + k
                for c in range(STATES):
                    now_v[c, pl.ds(at, 1), :] = bubbles_v[pl.ds(c * slots + block, 1), :]
                live = jnp.where(block < count_ref[0], 1.0, 0.0)
                live_v[pl.ds(at, 1), :] = jnp.full((1, lanes), live, f32)
                tile_v[pl.ds(at, 1), :] = jnp.full((1, lanes), tile.astype(f32), f32)
                positions.append(bubbles_v[pl.ds(2 * slots + block, 1), :])
                return rows_in[0, pl.ds(tile, 1), :], rows_in[1, pl.ds(tile, 1), :]

            rows = [rows_of(j) for j in range(QUAD)]
            at = i * chunk + q * QUAD
            sample_quad(q, at, positions, columns, lambda j: rows[j], lhs, sp, su, sn)

    def advance_start(i):
        for g, at in groups(i):
            live = live_v[at, :] > 0.5
            state = [now_v[c, at, :] for c in range(STATES)]
            state[0] = jnp.where(live, state[0], 1.0)
            state[4] = jnp.where(live, state[4], 1.0)
            drive, velocity = drive_of(sp[at, :], su[at, :], sn[at, :])
            place, speed = travel(state[2], state[3], velocity)
            radius, growth = advance_group(state[0], state[1], state[4], drive, SUBSTEPS // 2)
            for c, x in enumerate((radius, growth, place, speed, state[4], drive)):
                mid_v[c, at, :] = x

    def advance_end(i):
        for g, at in groups(i):
            live = live_v[at, :] > 0.5
            state = [mid_v[c, at, :] for c in range(STATES + 1)]
            new = advance_group(state[0], state[1], state[4], state[5], SUBSTEPS - SUBSTEPS // 2)
            new = new + tuple(state[2:STATES])
            amount_v[at, :] = jnp.where(live, source_amount(new[0], new[1]), 0.0)
            place_v[at, :] = new[2]
            new = (jnp.where(live, new[0], -1.0),) + tuple(new[1:])
            piece = min(cap, GROUP)
            for k in range(0, GROUP, piece):
                n = g * GROUP + k
                for c in range(STATES):
                    send_v[i * per + n // cap, c, n % cap : n % cap + piece, :] = new[c][k : k + piece]

    def spread(i):
        for g in range(chunk // GROUP):
            base = pl.multiple_of(i * chunk + g * GROUP, GROUP)
            amount = amount_v[pl.ds(base, GROUP), :]
            for quad in range(GROUP // QUAD):
                positions = [place_v[pl.ds(base + QUAD * quad + n, 1), :] for n in range(QUAD)]
                rows = spread_quad(quad, positions, amount, columns, tiles)
                for n in range(QUAD):
                    spread_v[pl.ds(base + QUAD * quad + n, 1), :] = rows[n]

    def to_peer(n, place):
        peer = peer_of(n, streams, azims)
        return pltpu.make_async_remote_copy(
            src_ref=send_v.at[n], dst_ref=place, send_sem=send_sems.at[n],
            recv_sem=recv_sems.at[n], device_id=peer, device_id_type=MESH,
        )

    def start_to(n):
        pl.when(n < soon)(to_peer(n, soon_v.at[jnp.minimum(n, soon - 1)]).start)
        pl.when(n >= soon)(to_peer(n, arrived.at[me]).start)

    def dead(n):
        return pltpu.make_async_copy(dead_v, arrived.at[source_of(n, streams, azims)], dead_sems.at[n])

    def wait_soon(n):
        to_peer(n, soon_v.at[n]).wait_recv()

    def wait_late(n):
        to_peer(n, arrived.at[source_of(n, streams, azims)]).wait_recv()

    own = pltpu.make_async_copy(send_v.at[devices - 1], arrived.at[me], own_sem)

    def send(i, end=False):
        for q in range(per):
            if end and q == per - 1:
                own.start()
            else:
                start_to(i * per + q)

    def halo_copies(ref, lands, sends, recvs):
        def copy(n, src, dst, peer):
            return pltpu.make_async_remote_copy(
                src_ref=src, dst_ref=dst, send_sem=sends.at[n], recv_sem=recvs.at[n],
                device_id=peer, device_id_type=MESH,
            )

        up, down = (stream + 1) % streams, (stream + streams - 1) % streams
        right, left = (azim + 1) % azims, (azim + azims - 1) % azims
        return (
            copy(0, ref.at[:, pl.ds(width * length, width)], lands[0], (up, azim)),
            copy(1, ref.at[:, pl.ds(width, width)], lands[1], (down, azim)),
            copy(2, last_v, lands[2], (stream, right)),
            copy(3, first_v, lands[3], (stream, left)),
        )

    def halo_start(copies):
        pl.when(stream < last_stream)(copies[0].start)
        pl.when(stream > 0)(copies[1].start)
        copies[2].start()
        copies[3].start()

    def halo_sent(copies):
        pl.when(stream < last_stream)(copies[0].wait_send)
        pl.when(stream > 0)(copies[1].wait_send)
        copies[2].wait_send()
        copies[3].wait_send()

    def halo_here(copies):
        pl.when(stream > 0)(copies[0].wait_recv)
        pl.when(stream < last_stream)(copies[1].wait_recv)
        copies[2].wait_recv()
        copies[3].wait_recv()

    def set_ends(ref, low, high):
        ref[:, pl.ds(0, width), :] = low
        ref[:, pl.ds((length + 1) * width, width), :] = high

    def edges(ref):
        many = 4

        def edge(n, carry):
            for k in range(many):
                s = n * many + k
                at = pl.multiple_of((s + 1) * width, width)
                for c in range(comps):
                    first_v[c, pl.ds(s, 1), :] = ref[c, pl.ds(at, 1), :]
                    last_v[c, pl.ds(s, 1), :] = ref[c, pl.ds(at + width - 1, 1), :]
            return carry

        lax.fori_loop(0, length // many, edge, 0)

    state_row = lax.broadcasted_iota(jnp.int32, dead_v.shape, 0)
    dead_v[...] = jnp.where(state_row == 0, -1.0, 1.0)
    fin_v[...] = jnp.zeros_like(fin_v)
    sample(0)
    loads[3].wait()
    edges(fluid_v)
    advance_start(0)
    sample(1)
    pl.semaphore_wait(barrier, devices - 1)
    early = halo_copies(fluid_v, (low_v, high_v, left_v, right_v), early_send, early_recv)
    halo_start(early)

    def bury(n, carry):
        dead(n).start()
        return carry

    lax.fori_loop(0, soon, bury, 0)
    advance_end(0)
    advance_start(1)
    sample(2)

    def steady(i):
        spread(i - 3)
        advance_end(i - 2)
        advance_start(i - 1)
        sample(i)
        send(i - 3)

    def plain(i, carry):
        steady(i)
        return carry

    planes = 3
    begin = max(3, chunks - pl.cdiv(length, planes))
    planes = pl.cdiv(length, max(1, chunks - begin))

    def with_flow(i, carry):
        for n in range(planes):
            s = jnp.minimum((i - begin) * planes + n, length - 1)
            flow_plane(s, width, fluid_v, new_v)
        steady(i)
        return carry

    set_ends(fluid_v, zero_v[...], zero_v[...])
    lax.fori_loop(3, begin, plain, 0)
    lax.fori_loop(begin, chunks, with_flow, 0)
    send(chunks - 3)
    spread(chunks - 3)
    advance_end(chunks - 2)
    advance_start(chunks - 1)
    send(chunks - 2)
    spread(chunks - 2)
    advance_end(chunks - 1)
    spread(chunks - 1)
    send(chunks - 1, True)

    halo_here(early)
    halo_sent(early)
    add_halos(new_v, width, length, width, low_v, high_v, left_v, right_v)

    def subtract(at, block, parts):
        rows = pl.ds(at + width, block)
        new_v[0, rows, :] = new_v[0, rows, :] - TIME_STEP * parts[0]

    scatter(tile_v, [spread_v], area, subtract)
    edges(new_v)
    late = halo_copies(new_v, (low_2, high_2, left_2, right_2), late_send, late_recv)
    keeps = [
        pltpu.make_async_copy(new_v.at[0, inner], rows_out.at[0], store_sems.at[0]),
        pltpu.make_async_copy(new_v.at[comps - 1, inner], rows_out.at[1], store_sems.at[1]),
    ]
    for keep in keeps:
        keep.start()
    halo_start(late)

    def sent(n, carry):
        to_peer(n, soon_v.at[0]).wait_send()
        return carry

    zeros = [pltpu.make_async_copy(zero_v, out, zero_sems.at[n]) for n, out in enumerate((low_2, high_2))]
    pl.when(stream == 0)(zeros[0].start)
    pl.when(stream == last_stream)(zeros[1].start)
    set_ends(new_v, zero_v[...], zero_v[...])
    pieces = 4
    part = length // pieces
    outs = []
    for p in range(pieces):
        def flow(n, carry, p=p):
            for k in range(4):
                flow_plane(p * part + 4 * n + k, width, new_v, fluid_v)
            return carry

        lax.fori_loop(0, part // 4, flow, 0)
        outs.append(pltpu.make_async_copy(
            fluid_v.at[:, pl.ds((p * part + 1) * width, part * width)],
            fluid_out.at[:, pl.ds(p * part * width, part * width)], store_sems.at[2 + p],
        ))
        outs[p].start()
    def peers(i):
        for q in range(per):
            yield q, i * per + q

    def arrive(i):
        for _, n in peers(i):
            wait_soon(n)

    def sample_2(i):
        for q in range(chunk // QUAD):
            rows, positions = [], []
            for j in range(QUAD):
                k = q * QUAD + j
                n = i * per + k // cap
                tile = after_ref[source_of(n, streams, azims) * cap + k % cap]
                tile_v[pl.ds(i * chunk + k, 1), :] = jnp.full((1, lanes), tile.astype(f32), f32)
                positions.append(soon_v[n, 2, pl.ds(k % cap, 1), :])
                row = pl.ds(tile + width, 1)
                rows.append((new_v[0, row, :], new_v[comps - 1, row, :]))
            sample_quad(q, i * chunk + q * QUAD, positions, columns, lambda j: rows[j], lhs, sp, su, sn)

    def state_2(i, g):
        piece = min(cap, GROUP)
        parts = []
        for k in range(g * GROUP, (g + 1) * GROUP, piece):
            parts.append([soon_v[i * per + k // cap, c, k % cap : k % cap + piece, :] for c in range(STATES)])
        state = [x[0] if len(parts) == 1 else jnp.concatenate(x, axis=0) for x in zip(*parts)]
        return state, state[0] * state[4] >= 0.0

    def advance_start_2(i):
        for g, at in groups(i):
            state, live = state_2(i, g)
            radius, rest = (jnp.where(live, x, 1.0) for x in (state[0], state[4]))
            drive, velocity = drive_of(sp[at, :], su[at, :], sn[at, :])
            place, speed = travel(state[2], state[3], velocity)
            radius, growth = advance_group(radius, state[1], rest, drive, SUBSTEPS // 2)
            for c, x in enumerate((radius, growth, place, speed, rest, drive)):
                mid_v[c, at, :] = x

    def advance_end_2(i):
        for g, at in groups(i):
            live = state_2(i, g)[1]
            state = [mid_v[c, at, :] for c in range(STATES + 1)]
            new = advance_group(state[0], state[1], state[4], state[5], SUBSTEPS - SUBSTEPS // 2)
            new = new + tuple(state[2:STATES])
            amount_v[at, :] = jnp.where(live, source_amount(new[0], new[1]), 0.0)
            volume_v[at, :] = jnp.where(live, void_amount(new[0]), 0.0)
            place_v[at, :] = new[2]
            piece = min(cap, GROUP)
            for k in range(0, GROUP, piece):
                m = g * GROUP + k
                source = source_of(i * per + m // cap, streams, azims)
                for c in range(STATES):
                    fin_v[c, source, m % cap : m % cap + piece, :] = jnp.where(live, new[c], 0.0)[k : k + piece]

    def spread_2(i):
        for g, at in groups(i):
            base = i * chunk + g * GROUP
            amounts = [amount_v[at, :], volume_v[at, :]]
            for pair in range(GROUP // 2):
                positions = [place_v[pl.ds(base + 2 * pair + n, 1), :] for n in range(2)]
                rows = spread_pair(pair, positions, amounts, columns, tiles)
                for n in range(2):
                    spread_v[pl.ds(base + 2 * pair + n, 1), :] = rows[n]
                    void_v[pl.ds(base + 2 * pair + n, 1), :] = rows[2 + n]

    count = soon // per
    arrive(0)
    sample_2(0)
    arrive(1)
    advance_start_2(0)
    sample_2(1)
    arrive(2)
    advance_end_2(0)
    advance_start_2(1)
    sample_2(2)

    def steady_2(i, carry):
        arrive(i)
        spread_2(i - 3)
        advance_end_2(i - 2)
        advance_start_2(i - 1)
        sample_2(i)
        return carry

    lax.fori_loop(3, count, steady_2, 0)
    spread_2(count - 3)
    advance_end_2(count - 2)
    advance_start_2(count - 1)
    spread_2(count - 2)
    advance_end_2(count - 1)
    spread_2(count - 1)
    done = pl.ds(0, soon * cap)
    for n, (src, dst) in enumerate((
        (fin_v, bubbles_out), (spread_v.at[done], spread_out), (void_v, void_out), (tile_v.at[done], tile_out)
    )):
        outs.append(pltpu.make_async_copy(src, dst, store_sems.at[2 + pieces + n]))
        outs[-1].start()
    lax.fori_loop(0, devices - 1, sent, 0)
    own.wait()

    def came(n, carry):
        wait_late(n)
        return carry

    lax.fori_loop(soon, devices - 1, came, 0)

    def buried(n, carry):
        dead(n).wait()
        return carry

    lax.fori_loop(0, soon, buried, 0)
    halo_here(late)
    halo_sent(late)
    pl.when(stream == 0)(zeros[0].wait)
    pl.when(stream == last_stream)(zeros[1].wait)
    for copy in keeps + outs:
        copy.wait()


def shaped(*shape):
    return jax.ShapeDtypeStruct(shape, f32)


def buffer(*shape):
    return pltpu.VMEM(shape, f32)


def dma(*shape):
    return pltpu.SemaphoreType.DMA(shape)


ANYWHERE = pl.BlockSpec(memory_space=pl.ANY)
SCALARS = pl.BlockSpec(memory_space=pltpu.SMEM)


def first_step(fluid, order, tiles_ids, after_ids, counts, bubbles, length, width):
    streams, azims = lax.axis_size("stream"), lax.axis_size("azim")
    devices = streams * azims
    comps, tiles, cells = fluid.shape
    slots, lanes = order.shape[0], bubbles.shape[1]
    cap = slots // devices
    soon = 3 * devices // 8
    end, side = buffer(comps, width, cells), buffer(comps, length, cells)
    padded = buffer(comps, tiles + 2 * width, cells)
    per_slot = buffer(slots, lanes)
    return pl.pallas_call(
        functools.partial(first_kernel, streams, azims, cap, length, width, soon),
        out_shape=(shaped(*fluid.shape), shaped(2, tiles, cells), shaped(devices, STATES, cap, lanes),
                   *[shaped(*x.shape) for x in (end, end, side, side)],
                   shaped(STATES, devices, cap, lanes), *[shaped(soon * cap, cells)] * 2, shaped(soon * cap, lanes)),
        in_specs=[SCALARS] * 4 + [ANYWHERE] * 2,
        out_specs=(ANYWHERE,) * 11,
        scratch_shapes=[
            padded, padded, buffer(2, tiles, cells), end, end, side, side, side, side,
            end, buffer(*bubbles.shape), buffer(STATES, slots, lanes), buffer(STATES + 1, slots, lanes),
            per_slot, per_slot, per_slot, per_slot, per_slot, per_slot, per_slot,
            buffer(devices, STATES, cap, lanes), buffer(slots, cells),
            buffer(soon, STATES, cap, lanes), buffer(STATES, cap, lanes), buffer(STATES, devices, cap, lanes),
            per_slot, buffer(soon * cap, cells),
            buffer(max(cap, CHUNK) // QUAD, 16, 2 * cells),
            dma(4), dma(10), dma(), dma(soon), dma(devices), dma(devices), dma(4), dma(4), dma(4), dma(4), dma(2),
        ],
        compiler_params=pltpu.CompilerParams(
            vmem_limit_bytes=VMEM_GRANT, collective_id=0, has_side_effects=True
        ),
        cost_estimate=pl.CostEstimate(
            flops=slots * lanes * cells * 2000, bytes_accessed=12 * 2**20,
            transcendentals=2 * slots * lanes * cells,
        ),
        name="first_step",
    )(order, tiles_ids, after_ids, counts, bubbles, fluid)


def live_list(arrived_v, devices, live_v, slots_v, rows_v):
    slots, lanes = live_v.shape
    cap = slots // devices
    for d in range(devices):
        at = d * STATES * cap
        live = arrived_v[at : at + cap, :] * arrived_v[at + 4 * cap : at + 5 * cap, :] >= 0.0
        live_v[d * cap : (d + 1) * cap, :] = jnp.where(live, 1.0, 0.0)
    live = live_v[...]
    row = lax.broadcasted_iota(jnp.int32, (slots, slots), 0)
    column = lax.broadcasted_iota(jnp.int32, (slots, slots), 1)
    before = jnp.where(column < row, 1.0, 0.0).astype(bf16)
    rank = jnp.dot(before, live.astype(bf16), preferred_element_type=f32)
    number = jnp.dot(jnp.ones((16, slots), bf16), live.astype(bf16), preferred_element_type=f32)
    rank = jnp.where(live > 0.5, rank, -1.0)
    place = lax.broadcasted_iota(jnp.int32, (slots, lanes), 1).astype(f32)
    hot = [
        jnp.where(rank - float(at) == place, 1.0, 0.0).astype(bf16)[:, : min(lanes, slots - at)]
        for at in range(0, slots, lanes)
    ]
    which = lax.broadcasted_iota(jnp.int32, (16, slots), 0)
    slot = lax.broadcasted_iota(jnp.int32, (16, slots), 1)
    digits = jnp.where(which == 0, slot // cap, slot % cap).astype(f32).astype(bf16)
    found = jnp.dot(digits, jnp.concatenate(hot, axis=1), preferred_element_type=f32)
    entry = lax.broadcasted_iota(jnp.int32, (1, slots), 1).astype(f32)
    for ref, stride in ((slots_v, cap), (rows_v, STATES * cap)):
        line = float(stride) * found[0:1] + found[1:2]
        line = jnp.where(entry < number[0:1, 0:1], line, line[:, 0:1])
        ref[:, :slots] = line.astype(jnp.int32)
        ref[:, slots:] = number[0:1].astype(jnp.int32)


def second_kernel(devices, length, tiles_ref, arrived_hbm, rows_hbm, flow_hbm, low_hbm, high_hbm, left_hbm, right_hbm,
                  bubbles_hbm, spread_hbm, spread_void_hbm, spread_tile_hbm, fluid_out, bubbles_out, void_out,
                  arrived_v, rows_in, flow_v, low_v, high_v, left_v, right_v, bubbles_v, void_v,
                  now_v, mid_v, fin_v, live_v, tile_v, amount_v, volume_v, sp, su, sn, rows_v, voids_v,
                  lhs, slots_v, places_v, slots_ref, places_ref, load_sems, list_sems, store_sems):
    comps, area, cells_n = flow_hbm.shape
    slots, lanes = sp.shape
    cap = slots // devices
    width = area // length
    ahead = slots - spread_hbm.shape[0]
    behind = pl.ds(ahead, slots - ahead)
    loads = [
        pltpu.make_async_copy(arrived_hbm, arrived_v, load_sems.at[0]),
        pltpu.make_async_copy(rows_hbm, rows_in, load_sems.at[1]),
        pltpu.make_async_copy(flow_hbm, flow_v, load_sems.at[2]),
        pltpu.make_async_copy(low_hbm, low_v, load_sems.at[3]),
        pltpu.make_async_copy(high_hbm, high_v, load_sems.at[4]),
        pltpu.make_async_copy(left_hbm, left_v, load_sems.at[5]),
        pltpu.make_async_copy(right_hbm, right_v, load_sems.at[6]),
        pltpu.make_async_copy(bubbles_hbm, bubbles_v, load_sems.at[7]),
        pltpu.make_async_copy(spread_hbm, rows_v.at[behind], load_sems.at[8]),
        pltpu.make_async_copy(spread_void_hbm, voids_v.at[behind], load_sems.at[9]),
        pltpu.make_async_copy(spread_tile_hbm, tile_v.at[behind], load_sems.at[10]),
    ]
    for load in loads:
        load.start()
    columns = cell_columns(cells_n, lanes)
    tiles = cells_n // 8
    clear_lhs(lhs)
    loads[0].wait()
    live_list(arrived_v, devices, live_v, slots_v, places_v)
    lists = [
        pltpu.make_async_copy(slots_v, slots_ref, list_sems.at[0]),
        pltpu.make_async_copy(places_v, places_ref, list_sems.at[1]),
    ]
    for copy in lists:
        copy.start()
    tile_v[:ahead, :] = jnp.full((ahead, lanes), -1.0, f32)
    rows_v[:ahead, :] = jnp.zeros((ahead, cells_n), f32)
    voids_v[:ahead, :] = jnp.zeros((ahead, cells_n), f32)
    for load in (loads[1], *loads[7:]):
        load.wait()
    for copy in lists:
        copy.wait()
    number = slots_ref[0, slots]
    chunks = (number + CHUNK - 1) // CHUNK

    def groups(i):
        for g in range(CHUNK // GROUP):
            base = pl.multiple_of(i * CHUNK + g * GROUP, GROUP)
            yield base, pl.ds(base, GROUP)

    def sample(i):
        for q in range(CHUNK // QUAD):
            at = i * CHUNK + q * QUAD
            rows, positions = [], []
            for j in range(QUAD):
                place = places_ref[0, at + j]
                tile = tiles_ref[slots_ref[0, at + j]]
                for c in range(STATES):
                    now_v[c, pl.ds(at + j, 1), :] = arrived_v[pl.ds(place + c * cap, 1), :]
                tile_v[pl.ds(at + j, 1), :] = jnp.full((1, lanes), tile.astype(f32), f32)
                positions.append(arrived_v[pl.ds(place + 2 * cap, 1), :])
                rows.append((rows_in[0, pl.ds(tile, 1), :], rows_in[1, pl.ds(tile, 1), :]))
            sample_quad(q, at, positions, columns, lambda j: rows[j], lhs, sp, su, sn)

    def advance_start(i):
        for _, at in groups(i):
            state = [now_v[c, at, :] for c in range(STATES)]
            drive, velocity = drive_of(sp[at, :], su[at, :], sn[at, :])
            place, speed = travel(state[2], state[3], velocity)
            radius, growth = advance_group(state[0], state[1], state[4], drive, SUBSTEPS // 2)
            for c, x in enumerate((radius, growth, place, speed, state[4], drive)):
                mid_v[c, at, :] = x

    def advance_end(i):
        for base, at in groups(i):
            state = [mid_v[c, at, :] for c in range(STATES + 1)]
            new = advance_group(state[0], state[1], state[4], state[5], SUBSTEPS - SUBSTEPS // 2)
            new = new + tuple(state[2:STATES])
            live = base + lax.broadcasted_iota(jnp.int32, (GROUP, lanes), 0) < number
            amount_v[at, :] = jnp.where(live, source_amount(new[0], new[1]), 0.0)
            volume_v[at, :] = jnp.where(live, void_amount(new[0]), 0.0)
            for c in range(STATES):
                fin_v[c, at, :] = new[c]

    def spread(i):
        for base, rows_at in groups(i):
            amounts = [amount_v[rows_at, :], volume_v[rows_at, :]]
            for pair in range(GROUP // 2):
                positions = [fin_v[2, pl.ds(base + 2 * pair + n, 1), :] for n in range(2)]
                rows = spread_pair(pair, positions, amounts, columns, tiles)
                for n in range(2):
                    at = base + 2 * pair + n
                    rows_v[pl.ds(at, 1), :] = rows[n]
                    voids_v[pl.ds(at, 1), :] = rows[2 + n]
                    slot = slots_ref[0, at]
                    for c in range(STATES):
                        bubbles_v[pl.ds(c * slots + slot, 1), :] = fin_v[c, pl.ds(at, 1), :]

    @pl.when(number > 0)
    def _():
        def at_most(i):
            return jnp.minimum(i, chunks - 1)

        def before_end(n):
            return jnp.maximum(chunks - n, 0)

        sample(0)
        advance_start(0)
        sample(at_most(1))
        advance_end(0)
        advance_start(at_most(1))
        sample(at_most(2))

        def steady(i, carry):
            spread(i - 3)
            advance_end(i - 2)
            advance_start(i - 1)
            sample(i)
            return carry

        lax.fori_loop(3, chunks, steady, 0)
        spread(before_end(3))
        advance_end(before_end(2))
        advance_start(before_end(1))
        spread(before_end(2))
        advance_end(before_end(1))
        spread(before_end(1))

    def store(n, src, dst):
        copy = pltpu.make_async_copy(src, dst, store_sems.at[n])
        copy.start()
        return copy

    for load in loads[2:7]:
        load.wait()
    add_halos(flow_v, 0, length, width, low_v, high_v, left_v, right_v)
    rest = pl.ds(1, comps - 1)
    stores = [store(0, bubbles_v, bubbles_out), store(1, flow_v.at[rest], fluid_out.at[rest])]

    def finish(at, block, parts):
        rows = pl.ds(at, block)
        flow_v[0, rows, :] = flow_v[0, rows, :] - TIME_STEP * parts[0]
        void_v[rows, :] = parts[1]

    scatter(tile_v, [rows_v, voids_v], area, finish)
    stores += [store(2, flow_v.at[0], fluid_out.at[0]), store(3, void_v, void_out)]
    for copy in stores:
        copy.wait()


def second_step(tiles_ids, arrived, rows, flow, halos, bubbles, parts):
    comps, tiles, cells = flow.shape
    slots, lanes = tiles_ids.shape[0], arrived.shape[3]
    devices, length = arrived.shape[0], halos[2].shape[1]
    arrived = arrived.reshape(slots * STATES, lanes)
    per_slot = buffer(slots, lanes)
    return pl.pallas_call(
        functools.partial(second_kernel, devices, length),
        out_shape=(shaped(*flow.shape), shaped(STATES * slots, lanes), shaped(tiles, cells)),
        in_specs=[SCALARS] + [ANYWHERE] * 11,
        out_specs=(ANYWHERE,) * 3,
        scratch_shapes=[
            buffer(*arrived.shape), buffer(*rows.shape), buffer(*flow.shape),
            *[buffer(*x.shape) for x in halos],
            buffer(STATES * slots, lanes), buffer(tiles, cells),
            buffer(STATES, slots, lanes), buffer(STATES + 1, slots, lanes), buffer(STATES, slots, lanes),
            per_slot, per_slot, per_slot, per_slot, per_slot, per_slot, per_slot,
            buffer(slots, cells), buffer(slots, cells),
            buffer(CHUNK // QUAD, 16, 2 * cells),
            *[space((1, slots + lanes), jnp.int32) for space in (pltpu.VMEM, pltpu.VMEM, pltpu.SMEM, pltpu.SMEM)],
            dma(11), dma(2), dma(4),
        ],
        compiler_params=pltpu.CompilerParams(vmem_limit_bytes=VMEM_GRANT),
        cost_estimate=pl.CostEstimate(
            flops=slots * lanes * cells * 2000, bytes_accessed=6 * 2**20,
            transcendentals=2 * slots * lanes * cells,
        ),
        name="second_step",
    )(tiles_ids, arrived, rows, flow, *halos, bubbles.reshape(STATES * slots, lanes), *parts)


def on_device(fluid, bubbles, counts, outgoing_block_order, tiles_first_update, tiles_after):
    comps, length, width, cells = fluid.shape
    slots, states, lanes = bubbles.shape
    flat = (comps, length * width, cells)
    bubbles = bubbles.transpose(1, 0, 2).reshape(states * slots, lanes)
    flow, rows, arrived, *rest = first_step(
        fluid.reshape(flat), outgoing_block_order, tiles_first_update, tiles_after, counts, bubbles, length, width
    )
    fluid, bubbles, void = second_step(tiles_after, arrived, rows, flow, rest[:4], rest[4], rest[5:])
    bubbles = bubbles.reshape(states, slots, lanes).transpose(1, 0, 2)
    return fluid.reshape(comps, length, width, cells), bubbles, void.reshape(length, width, cells)


def solution(mesh):
    return jax.shard_map(
        on_device,
        mesh=mesh,
        in_specs=(
            P(None, "stream", "azim", None),
            P(("stream", "azim"), None, None),
            P(("stream", "azim")),
            P(("stream", "azim")),
            P(("stream", "azim")),
            P(("stream", "azim")),
        ),
        out_specs=(
            P(None, "stream", "azim", None),
            P(("stream", "azim"), None, None),
            P("stream", "azim", None),
        ),
        check_vma=False,
    )
```

```python
import functools

import jax
import jax.numpy as jnp
from jax import lax
from jax.experimental import pallas as pl
from jax.experimental.pallas import tpu as pltpu
from jax.sharding import PartitionSpec as P

MESH = pl.DeviceIdType.MESH
SUBSTEPS = 8
TIME_STEP = 0.25
MEAN_FLOW = 0.5
DIFFUSION = 0.1
KERNEL_WIDTH = 1.5
GAS_INDEX = 4.2
PRESSURE_COUPLING = 0.3
AMBIENT = 1.0
RELAX_TIME = 0.5
VISCOUS = 0.08
SOURCE_GAIN = 0.05
VOID_SCALE = 0.01
FOUR_PI = 12.566370614359172
LOG2E = 1.4426950408889634
SHARPNESS = 0.5 * LOG2E / (KERNEL_WIDTH * KERNEL_WIDTH)
GROUP = 8
QUAD = 4
CHUNK = 16
STATES = 5
WIDE = 4
VMEM_GRANT = 60 * 2**20
f32, bf16 = jnp.float32, jnp.bfloat16


SAMPLE_SPANS = (7, 9)
SPREAD_SPANS = (5, 5, 6)


def runs(spans, tiles):
    out, start = [], 0
    while start < tiles:
        end = min(start + spans[len(out) % len(spans)], tiles)
        out.append((start, (start + end - 1) // 2, end))
        start = end
    return out


def cell_columns(cells_n, lanes):
    column = lax.broadcasted_iota(jnp.int32, (8, lanes), 0).astype(f32)
    tiles = cells_n // 8
    middles = sorted({m for spans in (SAMPLE_SPANS, SPREAD_SPANS) for _, m, _ in runs(spans, tiles)})
    return {m: column + float(8 * m) for m in middles}


def raw_weights(position, columns, tiles, spans):
    pieces = [None] * tiles
    for start, middle, end in runs(spans, tiles):
        offset = columns[middle] - position
        slope = offset * -SHARPNESS
        at = slope * offset
        pieces[middle] = jnp.exp2(at)
        for n in range(1, max(end - middle, middle - start + 1)):
            near = at - 64.0 * SHARPNESS * n * n
            step = slope * (16.0 * n)
            if middle - n >= start:
                pieces[middle - n] = jnp.exp2(near - step)
            if middle + n < end:
                pieces[middle + n] = jnp.exp2(near + step)
    return jnp.concatenate(pieces, axis=0)


def split_bf16(values):
    high = values.astype(bf16)
    low = (values - high.astype(f32)).astype(bf16)
    return high, low


def two_parts(rows):
    high = rows.astype(bf16).astype(f32)
    return jnp.concatenate([high, rows - high], axis=0).astype(bf16)


def clear_lhs(lhs):
    cells_n = lhs.shape[2] // 2
    lhs[...] = jnp.zeros_like(lhs)
    one = jnp.ones((1, cells_n), f32)
    for q in range(lhs.shape[0]):
        lhs[q, 4:5, :cells_n] = one
        lhs[q, 12:13, cells_n:] = one


def sample_quad(q, at, positions, columns, rows_of, lhs, sp, su, sn):
    cells_n = lhs.shape[2] // 2
    weights = []
    for j in range(QUAD):
        p_row, u_row = rows_of(j)
        row, side = 8 * (j // 2) + 2 * (j % 2), slice(cells_n * (j // 2), cells_n * (j // 2 + 1))
        lhs[q, row : row + 1, side] = p_row
        lhs[q, row + 1 : row + 2, side] = u_row
        weights.append(raw_weights(positions[j], columns, cells_n // 8, SAMPLE_SPANS).astype(bf16))
    rhs = jnp.concatenate(
        [jnp.concatenate(weights[:2], axis=1), jnp.concatenate(weights[2:], axis=1)], axis=0
    )
    result = jnp.dot(two_parts(lhs[q]), rhs, preferred_element_type=f32)
    result = result[:16] + result[16:]
    lanes = rhs.shape[1] // 2
    for j in range(QUAD):
        row, part = 8 * (j // 2), result[:, lanes * (j % 2) : lanes * (j % 2 + 1)]
        first = row + 2 * (j % 2)
        sp[pl.ds(at + j, 1), :] = part[first : first + 1]
        su[pl.ds(at + j, 1), :] = part[first + 1 : first + 2]
        sn[pl.ds(at + j, 1), :] = part[row + 4 : row + 5]


def drive_of(pressure, velocity, norm):
    inverse = 1.0 / norm
    return AMBIENT + PRESSURE_COUPLING * (pressure * inverse), velocity * inverse


def advance_group(radius, growth, rest, drive, substeps):
    h = TIME_STEP / SUBSTEPS
    for _ in range(substeps):
        over = 1.0 / radius
        gas = jnp.exp2((GAS_INDEX * LOG2E) * jnp.log(rest * over))
        damping = growth * (1.5 * growth + VISCOUS * over)
        growth = growth + (gas - drive - damping) * (h * over)
        radius = radius + h * growth
    return radius, growth


def travel(position, speed, velocity):
    h = TIME_STEP / SUBSTEPS
    keep = 1.0 - h / RELAX_TIME
    lag = speed - velocity
    path = h * sum(keep ** n for n in range(1, SUBSTEPS + 1))
    return position + TIME_STEP * velocity + path * lag, velocity + keep**SUBSTEPS * lag


def source_amount(radius, growth):
    return SOURCE_GAIN * FOUR_PI * radius * radius * growth


def void_amount(radius):
    return VOID_SCALE * FOUR_PI / 3.0 * radius * radius * radius


def spread_pair(pair, positions, amounts, columns, tiles):
    pieces, norms = [], []
    for position in positions:
        raw = raw_weights(position, columns, tiles, SPREAD_SPANS)
        norms.append(jnp.sum(raw, axis=0, keepdims=True))
        pieces.append(jnp.concatenate(split_bf16(raw), axis=1))
    rhs = jnp.concatenate(pieces, axis=0)
    sublane = lax.broadcasted_iota(jnp.int32, amounts[0].shape, 0)
    inverse = 1.0 / jnp.where(sublane == 2 * pair, norms[0], norms[1])
    rows = jnp.concatenate([a * inverse for a in amounts], axis=0)
    lhs = two_parts(rows)
    lhs = jnp.concatenate([lhs, lhs], axis=1)
    result = lax.dot_general(
        lhs, rhs, (((1,), (1,)), ((), ())), preferred_element_type=f32
    )
    result = result[: rows.shape[0]] + result[rows.shape[0] :]
    cells_n = 8 * tiles
    out = []
    for n in range(len(amounts)):
        for side in range(2):
            row = GROUP * n + 2 * pair + side
            out.append(result[row : row + 1, side * cells_n : (side + 1) * cells_n])
    return out


def spread_quad(quad, positions, amounts, columns, tiles):
    weights, norms = [], []
    for position in positions:
        raw = raw_weights(position, columns, tiles, SPREAD_SPANS)
        norms.append(jnp.sum(raw, axis=0, keepdims=True))
        weights.append(raw.astype(bf16))
    rhs = jnp.concatenate(
        [jnp.concatenate(weights[0::2], axis=1), jnp.concatenate(weights[1::2], axis=1)], axis=0
    )
    row = lax.broadcasted_iota(jnp.int32, amounts.shape, 0) % QUAD
    norm = jnp.where(
        row < 2, jnp.where(row == 0, norms[0], norms[1]), jnp.where(row == 2, norms[2], norms[3])
    )
    parts = two_parts(amounts / norm)
    none = jnp.zeros_like(parts)
    lhs = jnp.concatenate(
        [jnp.concatenate([parts, none], axis=1), jnp.concatenate([none, parts], axis=1)], axis=0
    )
    result = lax.dot_general(
        lhs, rhs, (((1,), (1,)), ((), ())), preferred_element_type=f32
    )
    size, cells_n = amounts.shape[0], 8 * tiles
    out = []
    for j in range(QUAD):
        first = (j // 2) * 2 * size + QUAD * quad + j
        side = slice((j % 2) * cells_n, (j % 2 + 1) * cells_n)
        out.append(result[first : first + 1, side] + result[first + size : first + size + 1, side])
    return out


def lanes_of(rows):
    number, lanes = rows.shape
    pieces = []
    for at in range(0, number, lanes):
        block = rows[at : at + lanes]
        same = lax.broadcasted_iota(jnp.int32, block.shape, 0) == lax.broadcasted_iota(
            jnp.int32, block.shape, 1
        )
        line = jnp.sum(jnp.where(same, block, 0.0), axis=0, keepdims=True)
        pieces.append(line[:, : block.shape[0]])
    return jnp.concatenate(pieces, axis=1)


def scatter(tile_rows, parts, tiles, store):
    cells_n = parts[0].shape[1]
    ids = lanes_of(tile_rows[...])
    block = min(1024, tiles)
    rhs = jnp.concatenate([x for part in parts for x in split_bf16(part[...])], axis=1)

    def some(i, carry):
        at = pl.multiple_of(i * block, block)
        tile = lax.broadcasted_iota(jnp.int32, (block, ids.shape[1]), 0) + at
        hot = jnp.where(tile.astype(f32) == ids, 1.0, 0.0).astype(bf16)
        result = jnp.dot(hot, rhs, preferred_element_type=f32)
        sums = []
        for n in range(len(parts)):
            high = result[:, 2 * n * cells_n : (2 * n + 1) * cells_n]
            sums.append(high + result[:, (2 * n + 1) * cells_n : (2 * n + 2) * cells_n])
        store(at, block, sums)
        return carry

    lax.fori_loop(0, tiles // block, some, 0)


def flow_plane(s, width, fluid, new_ref):
    comps, _, cells = fluid.shape
    row = lax.broadcasted_iota(jnp.int32, (width, cells), 0)
    lane = lax.broadcasted_iota(jnp.int32, (width, cells), 1)

    def plane(ref, c, n):
        return ref[c, pl.ds(pl.multiple_of(n * width, width), width), :]

    d_s, d_a, d_r, lap, now = [], [], [], [], []
    for c in range(comps):
        x, below, above = (plane(fluid, c, s + n) for n in (1, 0, 2))
        a_down = jnp.where(row == 0, 0.0, pltpu.roll(x, 1, 0))
        a_up = jnp.where(row == width - 1, 0.0, pltpu.roll(x, width - 1, 0))
        r_down = jnp.where(lane == 0, 0.0, pltpu.roll(x, 1, 1))
        r_up = jnp.where(lane == cells - 1, 0.0, pltpu.roll(x, cells - 1, 1))
        now.append(x)
        d_s.append(above - below)
        d_a.append(a_up - a_down)
        d_r.append(r_up - r_down)
        lap.append(above + below + a_up + a_down + r_up + r_down - 6.0 * x)
    half = 0.5 * TIME_STEP
    change = [
        MEAN_FLOW * d_s[0] + d_s[1] + d_a[2] + d_r[3],
        MEAN_FLOW * d_s[1] + d_s[0],
        MEAN_FLOW * d_s[2] + d_a[0],
        MEAN_FLOW * d_s[3] + d_r[0],
    ]
    for c in range(comps):
        at = pl.multiple_of((s + 1) * width, width)
        new_ref[c, pl.ds(at, width), :] = now[c] - half * change[c] + DIFFUSION * lap[c]


def halo_terms(side, sign, stream):
    half = sign * 0.5 * TIME_STEP
    own = DIFFUSION + (half * MEAN_FLOW if stream else 0.0)
    terms = [own * x for x in side]
    other = 1 if stream else 2
    terms[0] = terms[0] + half * side[other]
    terms[other] = terms[other] + half * side[0]
    return terms


def add_halos(ref, start, length, width, low, high, left, right):
    comps = ref.shape[0]
    for at, number, stride, side, sign in (
        (start, width, 1, low, 1), (start + (length - 1) * width, width, 1, high, -1),
        (start, length, width, left, 1), (start + width - 1, length, width, right, -1),
    ):
        rows = pl.ds(at, number) if stride == 1 else pl.ds(at, number, stride=stride)
        terms = halo_terms([side[c] for c in range(comps)], sign, stride == 1)
        terms = [ref[c, rows, :] + term for c, term in enumerate(terms)]
        for c, term in enumerate(terms):
            ref[c, rows, :] = term


def peer_of(n, streams, azims):
    turn, other = n // streams, n % streams
    step = (turn + 1) // 2 * (2 * (turn % 2) - 1)
    away = (azims // 2 + step + azims) % azims
    stream = (lax.axis_index("stream") + (other + 1) % streams) % streams
    return stream, (lax.axis_index("azim") + away) % azims


def source_of(n, streams, azims):
    turn, other = n // streams, n % streams
    step = (turn + 1) // 2 * (2 * (turn % 2) - 1)
    away = (azims // 2 + step + azims) % azims
    stream = (lax.axis_index("stream") + streams - (other + 1) % streams) % streams
    return stream * azims + (lax.axis_index("azim") + azims - away) % azims


def first_kernel(streams, azims, cap, length, width, soon,
                 order_ref, tiles_ref, after_ref, count_ref, bubbles_hbm, fluid_hbm,
                 fluid_out, rows_out, arrived, low_2, high_2, left_2, right_2,
                 bubbles_out, spread_out, void_out, tile_out,
                 fluid_v, new_v, rows_in, low_v, high_v, left_v, right_v, first_v, last_v,
                 zero_v, bubbles_v, now_v, mid_v, live_v, tile_v, amount_v, place_v, sp, su, sn, send_v, spread_v,
                 soon_v, dead_v, fin_v, volume_v, void_v,
                 lhs, load_sems, store_sems, own_sem, dead_sems, send_sems, recv_sems,
                 early_send, early_recv, late_send, late_recv, zero_sems):
    devices = streams * azims
    comps, area, cells_n = fluid_hbm.shape
    slots, lanes = sp.shape
    stream, azim = lax.axis_index("stream"), lax.axis_index("azim")
    me = stream * azims + azim
    last_stream = streams - 1

    barrier = pltpu.get_barrier_semaphore()

    def greet(n, carry):
        other = (me + n) % devices
        pl.semaphore_signal(
            barrier, inc=1, device_id=(other // azims, other % azims), device_id_type=MESH
        )
        return carry

    lax.fori_loop(1, devices, greet, 0)
    inner = pl.ds(width, area)
    loads = [
        pltpu.make_async_copy(bubbles_hbm, bubbles_v, load_sems.at[0]),
        pltpu.make_async_copy(fluid_hbm.at[0], rows_in.at[0], load_sems.at[1]),
        pltpu.make_async_copy(fluid_hbm.at[comps - 1], rows_in.at[1], load_sems.at[2]),
        pltpu.make_async_copy(fluid_hbm, fluid_v.at[:, inner], load_sems.at[3]),
    ]
    for load in loads[:3]:
        load.start()
    clear_lhs(lhs)
    zero_v[...] = jnp.zeros_like(zero_v)

    @pl.when(stream == 0)
    def _():
        low_v[...] = jnp.zeros_like(low_v)

    @pl.when(stream == last_stream)
    def _():
        high_v[...] = jnp.zeros_like(high_v)

    columns = cell_columns(cells_n, lanes)
    tiles = cells_n // 8
    per = max(1, CHUNK // cap)
    chunk = per * cap
    chunks = slots // chunk
    for load in loads[:3]:
        load.wait()
    loads[3].start()

    def groups(i):
        for g in range(chunk // GROUP):
            yield g, pl.ds(pl.multiple_of(i * chunk + g * GROUP, GROUP), GROUP)

    def sample(i):
        for q in range(chunk // QUAD):
            positions = []

            def rows_of(j, q=q):
                k = q * QUAD + j
                peer_stream, peer_azim = peer_of(i * per + k // cap, streams, azims)
                slot = (peer_stream * azims + peer_azim) * cap + k % cap
                block = order_ref[slot]
                tile = tiles_ref[block]
                at = i * chunk + k
                for c in range(STATES):
                    now_v[c, pl.ds(at, 1), :] = bubbles_v[pl.ds(c * slots + block, 1), :]
                live = jnp.where(block < count_ref[0], 1.0, 0.0)
                live_v[pl.ds(at, 1), :] = jnp.full((1, lanes), live, f32)
                tile_v[pl.ds(at, 1), :] = jnp.full((1, lanes), tile.astype(f32), f32)
                positions.append(bubbles_v[pl.ds(2 * slots + block, 1), :])
                return rows_in[0, pl.ds(tile, 1), :], rows_in[1, pl.ds(tile, 1), :]

            rows = [rows_of(j) for j in range(QUAD)]
            at = i * chunk + q * QUAD
            sample_quad(q, at, positions, columns, lambda j: rows[j], lhs, sp, su, sn)

    def advance_start(i):
        for g, at in groups(i):
            live = live_v[at, :] > 0.5
            state = [now_v[c, at, :] for c in range(STATES)]
            state[0] = jnp.where(live, state[0], 1.0)
            state[4] = jnp.where(live, state[4], 1.0)
            drive, velocity = drive_of(sp[at, :], su[at, :], sn[at, :])
            place, speed = travel(state[2], state[3], velocity)
            radius, growth = advance_group(state[0], state[1], state[4], drive, SUBSTEPS // 2)
            for c, x in enumerate((radius, growth, place, speed, state[4], drive)):
                mid_v[c, at, :] = x

    def advance_end(i):
        for g, at in groups(i):
            live = live_v[at, :] > 0.5
            state = [mid_v[c, at, :] for c in range(STATES + 1)]
            new = advance_group(state[0], state[1], state[4], state[5], SUBSTEPS - SUBSTEPS // 2)
            new = new + tuple(state[2:STATES])
            amount_v[at, :] = jnp.where(live, source_amount(new[0], new[1]), 0.0)
            place_v[at, :] = new[2]
            new = (jnp.where(live, new[0], -1.0),) + tuple(new[1:])
            piece = min(cap, GROUP)
            for k in range(0, GROUP, piece):
                n = g * GROUP + k
                for c in range(STATES):
                    send_v[i * per + n // cap, c, n % cap : n % cap + piece, :] = new[c][k : k + piece]

    def spread(i):
        for g in range(chunk // GROUP):
            base = pl.multiple_of(i * chunk + g * GROUP, GROUP)
            amount = amount_v[pl.ds(base, GROUP), :]
            for quad in range(GROUP // QUAD):
                positions = [place_v[pl.ds(base + QUAD * quad + n, 1), :] for n in range(QUAD)]
                rows = spread_quad(quad, positions, amount, columns, tiles)
                for n in range(QUAD):
                    spread_v[pl.ds(base + QUAD * quad + n, 1), :] = rows[n]

    def to_peer(n, place):
        peer = peer_of(n, streams, azims)
        return pltpu.make_async_remote_copy(
            src_ref=send_v.at[n], dst_ref=place, send_sem=send_sems.at[n],
            recv_sem=recv_sems.at[n], device_id=peer, device_id_type=MESH,
        )

    def start_to(n):
        pl.when(n < soon)(to_peer(n, soon_v.at[jnp.minimum(n, soon - 1)]).start)
        pl.when(n >= soon)(to_peer(n, arrived.at[me]).start)

    def dead(n):
        return pltpu.make_async_copy(dead_v, arrived.at[source_of(n, streams, azims)], dead_sems.at[n])

    def wait_soon(n):
        to_peer(n, soon_v.at[n]).wait_recv()

    def wait_late(n):
        to_peer(n, arrived.at[source_of(n, streams, azims)]).wait_recv()

    own = pltpu.make_async_copy(send_v.at[devices - 1], arrived.at[me], own_sem)

    def send(i, end=False):
        for q in range(per):
            if end and q == per - 1:
                own.start()
            else:
                start_to(i * per + q)

    def halo_copies(ref, lands, sends, recvs):
        def copy(n, src, dst, peer):
            return pltpu.make_async_remote_copy(
                src_ref=src, dst_ref=dst, send_sem=sends.at[n], recv_sem=recvs.at[n],
                device_id=peer, device_id_type=MESH,
            )

        up, down = (stream + 1) % streams, (stream + streams - 1) % streams
        right, left = (azim + 1) % azims, (azim + azims - 1) % azims
        return (
            copy(0, ref.at[:, pl.ds(width * length, width)], lands[0], (up, azim)),
            copy(1, ref.at[:, pl.ds(width, width)], lands[1], (down, azim)),
            copy(2, last_v, lands[2], (stream, right)),
            copy(3, first_v, lands[3], (stream, left)),
        )

    def halo_start(copies):
        pl.when(stream < last_stream)(copies[0].start)
        pl.when(stream > 0)(copies[1].start)
        copies[2].start()
        copies[3].start()

    def halo_sent(copies):
        pl.when(stream < last_stream)(copies[0].wait_send)
        pl.when(stream > 0)(copies[1].wait_send)
        copies[2].wait_send()
        copies[3].wait_send()

    def halo_here(copies):
        pl.when(stream > 0)(copies[0].wait_recv)
        pl.when(stream < last_stream)(copies[1].wait_recv)
        copies[2].wait_recv()
        copies[3].wait_recv()

    def set_ends(ref, low, high):
        ref[:, pl.ds(0, width), :] = low
        ref[:, pl.ds((length + 1) * width, width), :] = high

    def edges(ref):
        many = 4

        def edge(n, carry):
            for k in range(many):
                s = n * many + k
                at = pl.multiple_of((s + 1) * width, width)
                for c in range(comps):
                    first_v[c, pl.ds(s, 1), :] = ref[c, pl.ds(at, 1), :]
                    last_v[c, pl.ds(s, 1), :] = ref[c, pl.ds(at + width - 1, 1), :]
            return carry

        lax.fori_loop(0, length // many, edge, 0)

    state_row = lax.broadcasted_iota(jnp.int32, dead_v.shape, 0)
    dead_v[...] = jnp.where(state_row == 0, -1.0, 1.0)
    fin_v[...] = jnp.zeros_like(fin_v)
    sample(0)
    loads[3].wait()
    edges(fluid_v)
    advance_start(0)
    sample(1)
    pl.semaphore_wait(barrier, devices - 1)
    early = halo_copies(fluid_v, (low_v, high_v, left_v, right_v), early_send, early_recv)
    halo_start(early)

    def bury(n, carry):
        dead(n).start()
        return carry

    lax.fori_loop(0, soon, bury, 0)
    advance_end(0)
    advance_start(1)
    sample(2)

    def steady(i):
        spread(i - 3)
        advance_end(i - 2)
        advance_start(i - 1)
        sample(i)
        send(i - 3)

    def plain(i, carry):
        steady(i)
        return carry

    planes = 3
    begin = max(3, chunks - pl.cdiv(length, planes))
    planes = pl.cdiv(length, max(1, chunks - begin))

    def with_flow(i, carry):
        for n in range(planes):
            s = jnp.minimum((i - begin) * planes + n, length - 1)
            flow_plane(s, width, fluid_v, new_v)
        steady(i)
        return carry

    set_ends(fluid_v, zero_v[...], zero_v[...])
    lax.fori_loop(3, begin, plain, 0)
    lax.fori_loop(begin, chunks, with_flow, 0)
    send(chunks - 3)
    spread(chunks - 3)
    advance_end(chunks - 2)
    advance_start(chunks - 1)
    send(chunks - 2)
    spread(chunks - 2)
    advance_end(chunks - 1)
    spread(chunks - 1)
    send(chunks - 1, True)

    halo_here(early)
    halo_sent(early)
    add_halos(new_v, width, length, width, low_v, high_v, left_v, right_v)

    def subtract(at, block, parts):
        rows = pl.ds(at + width, block)
        new_v[0, rows, :] = new_v[0, rows, :] - TIME_STEP * parts[0]

    scatter(tile_v, [spread_v], area, subtract)
    edges(new_v)
    late = halo_copies(new_v, (low_2, high_2, left_2, right_2), late_send, late_recv)
    keeps = [
        pltpu.make_async_copy(new_v.at[0, inner], rows_out.at[0], store_sems.at[0]),
        pltpu.make_async_copy(new_v.at[comps - 1, inner], rows_out.at[1], store_sems.at[1]),
    ]
    for keep in keeps:
        keep.start()
    halo_start(late)

    def sent(n, carry):
        to_peer(n, soon_v.at[0]).wait_send()
        return carry

    zeros = [pltpu.make_async_copy(zero_v, out, zero_sems.at[n]) for n, out in enumerate((low_2, high_2))]
    pl.when(stream == 0)(zeros[0].start)
    pl.when(stream == last_stream)(zeros[1].start)
    set_ends(new_v, zero_v[...], zero_v[...])
    pieces = 4
    part = length // pieces
    outs = []
    for p in range(pieces):
        def flow(n, carry, p=p):
            for k in range(4):
                flow_plane(p * part + 4 * n + k, width, new_v, fluid_v)
            return carry

        lax.fori_loop(0, part // 4, flow, 0)
        outs.append(pltpu.make_async_copy(
            fluid_v.at[:, pl.ds((p * part + 1) * width, part * width)],
            fluid_out.at[:, pl.ds(p * part * width, part * width)], store_sems.at[2 + p],
        ))
        outs[p].start()
    def peers(i):
        for q in range(per):
            yield q, i * per + q

    def arrive(i):
        for _, n in peers(i):
            wait_soon(n)

    def sample_2(i):
        for q in range(chunk // QUAD):
            rows, positions = [], []
            for j in range(QUAD):
                k = q * QUAD + j
                n = i * per + k // cap
                tile = after_ref[source_of(n, streams, azims) * cap + k % cap]
                tile_v[pl.ds(i * chunk + k, 1), :] = jnp.full((1, lanes), tile.astype(f32), f32)
                positions.append(soon_v[n, 2, pl.ds(k % cap, 1), :])
                row = pl.ds(tile + width, 1)
                rows.append((new_v[0, row, :], new_v[comps - 1, row, :]))
            sample_quad(q, i * chunk + q * QUAD, positions, columns, lambda j: rows[j], lhs, sp, su, sn)

    def state_2(i, g):
        piece = min(cap, GROUP)
        parts = []
        for k in range(g * GROUP, (g + 1) * GROUP, piece):
            parts.append([soon_v[i * per + k // cap, c, k % cap : k % cap + piece, :] for c in range(STATES)])
        state = [x[0] if len(parts) == 1 else jnp.concatenate(x, axis=0) for x in zip(*parts)]
        return state, state[0] * state[4] >= 0.0

    def advance_start_2(i):
        for g, at in groups(i):
            state, live = state_2(i, g)
            radius, rest = (jnp.where(live, x, 1.0) for x in (state[0], state[4]))
            drive, velocity = drive_of(sp[at, :], su[at, :], sn[at, :])
            place, speed = travel(state[2], state[3], velocity)
            radius, growth = advance_group(radius, state[1], rest, drive, SUBSTEPS // 2)
            for c, x in enumerate((radius, growth, place, speed, rest, drive)):
                mid_v[c, at, :] = x

    def advance_end_2(i):
        for g, at in groups(i):
            live = state_2(i, g)[1]
            state = [mid_v[c, at, :] for c in range(STATES + 1)]
            new = advance_group(state[0], state[1], state[4], state[5], SUBSTEPS - SUBSTEPS // 2)
            new = new + tuple(state[2:STATES])
            amount_v[at, :] = jnp.where(live, source_amount(new[0], new[1]), 0.0)
            volume_v[at, :] = jnp.where(live, void_amount(new[0]), 0.0)
            place_v[at, :] = new[2]
            piece = min(cap, GROUP)
            for k in range(0, GROUP, piece):
                m = g * GROUP + k
                source = source_of(i * per + m // cap, streams, azims)
                for c in range(STATES):
                    fin_v[c, source, m % cap : m % cap + piece, :] = jnp.where(live, new[c], 0.0)[k : k + piece]

    def spread_2(i):
        for g, at in groups(i):
            base = i * chunk + g * GROUP
            amounts = [amount_v[at, :], volume_v[at, :]]
            for pair in range(GROUP // 2):
                positions = [place_v[pl.ds(base + 2 * pair + n, 1), :] for n in range(2)]
                rows = spread_pair(pair, positions, amounts, columns, tiles)
                for n in range(2):
                    spread_v[pl.ds(base + 2 * pair + n, 1), :] = rows[n]
                    void_v[pl.ds(base + 2 * pair + n, 1), :] = rows[2 + n]

    count = soon // per
    arrive(0)
    sample_2(0)
    arrive(1)
    advance_start_2(0)
    sample_2(1)
    arrive(2)
    advance_end_2(0)
    advance_start_2(1)
    sample_2(2)

    def steady_2(i, carry):
        arrive(i)
        spread_2(i - 3)
        advance_end_2(i - 2)
        advance_start_2(i - 1)
        sample_2(i)
        return carry

    lax.fori_loop(3, count, steady_2, 0)
    spread_2(count - 3)
    advance_end_2(count - 2)
    advance_start_2(count - 1)
    spread_2(count - 2)
    advance_end_2(count - 1)
    spread_2(count - 1)
    done = pl.ds(0, soon * cap)
    for n, (src, dst) in enumerate((
        (fin_v, bubbles_out), (spread_v.at[done], spread_out), (void_v, void_out), (tile_v.at[done], tile_out)
    )):
        outs.append(pltpu.make_async_copy(src, dst, store_sems.at[2 + pieces + n]))
        outs[-1].start()
    lax.fori_loop(0, devices - 1, sent, 0)
    own.wait()

    def came(n, carry):
        wait_late(n)
        return carry

    lax.fori_loop(soon, devices - 1, came, 0)

    def buried(n, carry):
        dead(n).wait()
        return carry

    lax.fori_loop(0, soon, buried, 0)
    halo_here(late)
    halo_sent(late)
    pl.when(stream == 0)(zeros[0].wait)
    pl.when(stream == last_stream)(zeros[1].wait)
    for copy in keeps + outs:
        copy.wait()


def shaped(*shape):
    return jax.ShapeDtypeStruct(shape, f32)


def buffer(*shape):
    return pltpu.VMEM(shape, f32)


def dma(*shape):
    return pltpu.SemaphoreType.DMA(shape)


ANYWHERE = pl.BlockSpec(memory_space=pl.ANY)
SCALARS = pl.BlockSpec(memory_space=pltpu.SMEM)


def first_step(fluid, order, tiles_ids, after_ids, counts, bubbles, length, width):
    streams, azims = lax.axis_size("stream"), lax.axis_size("azim")
    devices = streams * azims
    comps, tiles, cells = fluid.shape
    slots, lanes = order.shape[0], bubbles.shape[1]
    cap = slots // devices
    soon = 3 * devices // 8
    end, side = buffer(comps, width, cells), buffer(comps, length, cells)
    padded = buffer(comps, tiles + 2 * width, cells)
    per_slot = buffer(slots, lanes)
    return pl.pallas_call(
        functools.partial(first_kernel, streams, azims, cap, length, width, soon),
        out_shape=(shaped(*fluid.shape), shaped(2, tiles, cells), shaped(devices, STATES, cap, lanes),
                   *[shaped(*x.shape) for x in (end, end, side, side)],
                   shaped(STATES, devices, cap, lanes), *[shaped(soon * cap, cells)] * 2, shaped(soon * cap, lanes)),
        in_specs=[SCALARS] * 4 + [ANYWHERE] * 2,
        out_specs=(ANYWHERE,) * 11,
        scratch_shapes=[
            padded, padded, buffer(2, tiles, cells), end, end, side, side, side, side,
            end, buffer(*bubbles.shape), buffer(STATES, slots, lanes), buffer(STATES + 1, slots, lanes),
            per_slot, per_slot, per_slot, per_slot, per_slot, per_slot, per_slot,
            buffer(devices, STATES, cap, lanes), buffer(slots, cells),
            buffer(soon, STATES, cap, lanes), buffer(STATES, cap, lanes), buffer(STATES, devices, cap, lanes),
            per_slot, buffer(soon * cap, cells),
            buffer(max(cap, CHUNK) // QUAD, 16, 2 * cells),
            dma(4), dma(10), dma(), dma(soon), dma(devices), dma(devices), dma(4), dma(4), dma(4), dma(4), dma(2),
        ],
        compiler_params=pltpu.CompilerParams(
            vmem_limit_bytes=VMEM_GRANT, collective_id=0, has_side_effects=True
        ),
        cost_estimate=pl.CostEstimate(
            flops=slots * lanes * cells * 2000, bytes_accessed=12 * 2**20,
            transcendentals=2 * slots * lanes * cells,
        ),
        name="first_step",
    )(order, tiles_ids, after_ids, counts, bubbles, fluid)


def live_list(arrived_v, devices, live_v, slots_v, rows_v):
    slots, lanes = live_v.shape
    cap = slots // devices
    for d in range(devices):
        at = d * STATES * cap
        live = arrived_v[at : at + cap, :] * arrived_v[at + 4 * cap : at + 5 * cap, :] >= 0.0
        live_v[d * cap : (d + 1) * cap, :] = jnp.where(live, 1.0, 0.0)
    live = live_v[...]
    row = lax.broadcasted_iota(jnp.int32, (slots, slots), 0)
    column = lax.broadcasted_iota(jnp.int32, (slots, slots), 1)
    before = jnp.where(column < row, 1.0, 0.0).astype(bf16)
    rank = jnp.dot(before, live.astype(bf16), preferred_element_type=f32)
    number = jnp.dot(jnp.ones((16, slots), bf16), live.astype(bf16), preferred_element_type=f32)
    rank = jnp.where(live > 0.5, rank, -1.0)
    place = lax.broadcasted_iota(jnp.int32, (slots, lanes), 1).astype(f32)
    hot = [
        jnp.where(rank - float(at) == place, 1.0, 0.0).astype(bf16)[:, : min(lanes, slots - at)]
        for at in range(0, slots, lanes)
    ]
    which = lax.broadcasted_iota(jnp.int32, (16, slots), 0)
    slot = lax.broadcasted_iota(jnp.int32, (16, slots), 1)
    digits = jnp.where(which == 0, slot // cap, slot % cap).astype(f32).astype(bf16)
    found = jnp.dot(digits, jnp.concatenate(hot, axis=1), preferred_element_type=f32)
    entry = lax.broadcasted_iota(jnp.int32, (1, slots), 1).astype(f32)
    for ref, stride in ((slots_v, cap), (rows_v, STATES * cap)):
        line = float(stride) * found[0:1] + found[1:2]
        line = jnp.where(entry < number[0:1, 0:1], line, line[:, 0:1])
        ref[:, :slots] = line.astype(jnp.int32)
        ref[:, slots:] = number[0:1].astype(jnp.int32)


def second_kernel(devices, length, tiles_ref, arrived_hbm, rows_hbm, flow_hbm, low_hbm, high_hbm, left_hbm, right_hbm,
                  bubbles_hbm, spread_hbm, spread_void_hbm, spread_tile_hbm, fluid_out, bubbles_out, void_out,
                  arrived_v, rows_in, flow_v, low_v, high_v, left_v, right_v, bubbles_v, void_v,
                  now_v, mid_v, fin_v, live_v, tile_v, amount_v, volume_v, sp, su, sn, rows_v, voids_v,
                  lhs, slots_v, places_v, slots_ref, places_ref, load_sems, list_sems, store_sems):
    comps, area, cells_n = flow_hbm.shape
    slots, lanes = sp.shape
    cap = slots // devices
    width = area // length
    ahead = slots - spread_hbm.shape[0]
    behind = pl.ds(ahead, slots - ahead)
    loads = [
        pltpu.make_async_copy(arrived_hbm, arrived_v, load_sems.at[0]),
        pltpu.make_async_copy(rows_hbm, rows_in, load_sems.at[1]),
        pltpu.make_async_copy(flow_hbm, flow_v, load_sems.at[2]),
        pltpu.make_async_copy(low_hbm, low_v, load_sems.at[3]),
        pltpu.make_async_copy(high_hbm, high_v, load_sems.at[4]),
        pltpu.make_async_copy(left_hbm, left_v, load_sems.at[5]),
        pltpu.make_async_copy(right_hbm, right_v, load_sems.at[6]),
        pltpu.make_async_copy(bubbles_hbm, bubbles_v, load_sems.at[7]),
        pltpu.make_async_copy(spread_hbm, rows_v.at[behind], load_sems.at[8]),
        pltpu.make_async_copy(spread_void_hbm, voids_v.at[behind], load_sems.at[9]),
        pltpu.make_async_copy(spread_tile_hbm, tile_v.at[behind], load_sems.at[10]),
    ]
    for load in loads:
        load.start()
    columns = cell_columns(cells_n, lanes)
    tiles = cells_n // 8
    clear_lhs(lhs)
    loads[0].wait()
    live_list(arrived_v, devices, live_v, slots_v, places_v)
    lists = [
        pltpu.make_async_copy(slots_v, slots_ref, list_sems.at[0]),
        pltpu.make_async_copy(places_v, places_ref, list_sems.at[1]),
    ]
    for copy in lists:
        copy.start()
    tile_v[:ahead, :] = jnp.full((ahead, lanes), -1.0, f32)
    rows_v[:ahead, :] = jnp.zeros((ahead, cells_n), f32)
    voids_v[:ahead, :] = jnp.zeros((ahead, cells_n), f32)
    def store(n, src, dst):
        copy = pltpu.make_async_copy(src, dst, store_sems.at[n])
        copy.start()
        return copy

    for load in loads[1:]:
        load.wait()
    add_halos(flow_v, 0, length, width, low_v, high_v, left_v, right_v)
    for copy in lists:
        copy.wait()
    rest = pl.ds(1, comps - 1)
    stores = [store(0, flow_v.at[rest], fluid_out.at[rest])]
    number = slots_ref[0, slots]
    chunks = (number + CHUNK - 1) // CHUNK

    def groups(i):
        for g in range(CHUNK // GROUP):
            base = pl.multiple_of(i * CHUNK + g * GROUP, GROUP)
            yield base, pl.ds(base, GROUP)

    def sample(i):
        for q in range(CHUNK // QUAD):
            at = i * CHUNK + q * QUAD
            rows, positions = [], []
            for j in range(QUAD):
                place = places_ref[0, at + j]
                tile = tiles_ref[slots_ref[0, at + j]]
                for c in range(STATES):
                    now_v[c, pl.ds(at + j, 1), :] = arrived_v[pl.ds(place + c * cap, 1), :]
                tile_v[pl.ds(at + j, 1), :] = jnp.full((1, lanes), tile.astype(f32), f32)
                positions.append(arrived_v[pl.ds(place + 2 * cap, 1), :])
                rows.append((rows_in[0, pl.ds(tile, 1), :], rows_in[1, pl.ds(tile, 1), :]))
            sample_quad(q, at, positions, columns, lambda j: rows[j], lhs, sp, su, sn)

    def ready(i):
        return [
            ([now_v[c, at, :] for c in range(STATES)], (sp[at, :], su[at, :], sn[at, :]))
            for _, at in groups(i)
        ]

    def advance_start(i, loaded=None):
        for (_, at), (state, sums) in zip(groups(i), loaded or ready(i)):
            drive, velocity = drive_of(*sums)
            place, speed = travel(state[2], state[3], velocity)
            radius, growth = advance_group(state[0], state[1], state[4], drive, SUBSTEPS // 2)
            for c, x in enumerate((radius, growth, place, speed, state[4], drive)):
                mid_v[c, at, :] = x

    def advance_end(i):
        for base, at in groups(i):
            state = [mid_v[c, at, :] for c in range(STATES + 1)]
            new = advance_group(state[0], state[1], state[4], state[5], SUBSTEPS - SUBSTEPS // 2)
            new = new + tuple(state[2:STATES])
            live = base + lax.broadcasted_iota(jnp.int32, (GROUP, lanes), 0) < number
            amount_v[at, :] = jnp.where(live, source_amount(new[0], new[1]), 0.0)
            volume_v[at, :] = jnp.where(live, void_amount(new[0]), 0.0)
            for c in range(STATES):
                fin_v[c, at, :] = new[c]

    def spread(i):
        for base, rows_at in groups(i):
            amounts = [amount_v[rows_at, :], volume_v[rows_at, :]]
            for pair in range(GROUP // 2):
                positions = [fin_v[2, pl.ds(base + 2 * pair + n, 1), :] for n in range(2)]
                rows = spread_pair(pair, positions, amounts, columns, tiles)
                for n in range(2):
                    at = base + 2 * pair + n
                    rows_v[pl.ds(at, 1), :] = rows[n]
                    voids_v[pl.ds(at, 1), :] = rows[2 + n]
                    slot = slots_ref[0, at]
                    for c in range(STATES):
                        bubbles_v[pl.ds(c * slots + slot, 1), :] = fin_v[c, pl.ds(at, 1), :]

    @pl.when(number > 0)
    def _():
        def at_most(i):
            return jnp.minimum(i, chunks - 1)

        def before_end(n):
            return jnp.maximum(chunks - n, 0)

        sample(0)
        advance_start(0)
        sample(at_most(1))
        advance_end(0)
        advance_start(at_most(1))
        sample(at_most(2))

        def steady(i, carry):
            loaded = ready(i - 1)
            sample(i)
            spread(i - 3)
            advance_end(i - 2)
            advance_start(i - 1, loaded)
            return carry

        lax.fori_loop(3, chunks, steady, 0)
        spread(before_end(3))
        advance_end(before_end(2))
        advance_start(before_end(1))
        spread(before_end(2))
        advance_end(before_end(1))
        spread(before_end(1))

    stores.append(store(1, bubbles_v, bubbles_out))

    def finish(at, block, parts):
        rows = pl.ds(at, block)
        flow_v[0, rows, :] = flow_v[0, rows, :] - TIME_STEP * parts[0]
        void_v[rows, :] = parts[1]

    scatter(tile_v, [rows_v, voids_v], area, finish)
    stores += [store(2, flow_v.at[0], fluid_out.at[0]), store(3, void_v, void_out)]
    for copy in stores:
        copy.wait()


def second_step(tiles_ids, arrived, rows, flow, halos, bubbles, parts):
    comps, tiles, cells = flow.shape
    slots, lanes = tiles_ids.shape[0], arrived.shape[3]
    devices, length = arrived.shape[0], halos[2].shape[1]
    arrived = arrived.reshape(slots * STATES, lanes)
    per_slot = buffer(slots, lanes)
    return pl.pallas_call(
        functools.partial(second_kernel, devices, length),
        out_shape=(shaped(*flow.shape), shaped(STATES * slots, lanes), shaped(tiles, cells)),
        in_specs=[SCALARS] + [ANYWHERE] * 11,
        out_specs=(ANYWHERE,) * 3,
        scratch_shapes=[
            buffer(*arrived.shape), buffer(*rows.shape), buffer(*flow.shape),
            *[buffer(*x.shape) for x in halos],
            buffer(STATES * slots, lanes), buffer(tiles, cells),
            buffer(STATES, slots, lanes), buffer(STATES + 1, slots, lanes), buffer(STATES, slots, lanes),
            per_slot, per_slot, per_slot, per_slot, per_slot, per_slot, per_slot,
            buffer(slots, cells), buffer(slots, cells),
            buffer(CHUNK // QUAD, 16, 2 * cells),
            *[space((1, slots + lanes), jnp.int32) for space in (pltpu.VMEM, pltpu.VMEM, pltpu.SMEM, pltpu.SMEM)],
            dma(11), dma(2), dma(4),
        ],
        compiler_params=pltpu.CompilerParams(vmem_limit_bytes=VMEM_GRANT),
        cost_estimate=pl.CostEstimate(
            flops=slots * lanes * cells * 2000, bytes_accessed=6 * 2**20,
            transcendentals=2 * slots * lanes * cells,
        ),
        name="second_step",
    )(tiles_ids, arrived, rows, flow, *halos, bubbles.reshape(STATES * slots, lanes), *parts)


def on_device(fluid, bubbles, counts, outgoing_block_order, tiles_first_update, tiles_after):
    comps, length, width, cells = fluid.shape
    slots, states, lanes = bubbles.shape
    flat = (comps, length * width, cells)
    bubbles = bubbles.transpose(1, 0, 2).reshape(states * slots, lanes)
    flow, rows, arrived, *rest = first_step(
        fluid.reshape(flat), outgoing_block_order, tiles_first_update, tiles_after, counts, bubbles, length, width
    )
    fluid, bubbles, void = second_step(tiles_after, arrived, rows, flow, rest[:4], rest[4], rest[5:])
    bubbles = bubbles.reshape(states, slots, lanes).transpose(1, 0, 2)
    return fluid.reshape(comps, length, width, cells), bubbles, void.reshape(length, width, cells)


def solution(mesh):
    return jax.shard_map(
        on_device,
        mesh=mesh,
        in_specs=(
            P(None, "stream", "azim", None),
            P(("stream", "azim"), None, None),
            P(("stream", "azim")),
            P(("stream", "azim")),
            P(("stream", "azim")),
            P(("stream", "azim")),
        ),
        out_specs=(
            P(None, "stream", "azim", None),
            P(("stream", "azim"), None, None),
            P("stream", "azim", None),
        ),
        check_vma=False,
    )
```

```python
import functools

import jax
import jax.numpy as jnp
from jax import lax
from jax.experimental import pallas as pl
from jax.experimental.pallas import tpu as pltpu
from jax.sharding import PartitionSpec as P

MESH = pl.DeviceIdType.MESH
SUBSTEPS = 8
TIME_STEP = 0.25
MEAN_FLOW = 0.5
DIFFUSION = 0.1
KERNEL_WIDTH = 1.5
GAS_INDEX = 4.2
PRESSURE_COUPLING = 0.3
AMBIENT = 1.0
RELAX_TIME = 0.5
VISCOUS = 0.08
SOURCE_GAIN = 0.05
VOID_SCALE = 0.01
FOUR_PI = 12.566370614359172
LOG2E = 1.4426950408889634
SHARPNESS = 0.5 * LOG2E / (KERNEL_WIDTH * KERNEL_WIDTH)
GROUP = 8
QUAD = 4
CHUNK = 16
STATES = 5
WIDE = 4
VMEM_GRANT = 60 * 2**20
f32, bf16 = jnp.float32, jnp.bfloat16


SAMPLE_SPANS = (7, 9)
SPREAD_SPANS = (5, 5, 6)


def runs(spans, tiles):
    out, start = [], 0
    while start < tiles:
        end = min(start + spans[len(out) % len(spans)], tiles)
        out.append((start, (start + end - 1) // 2, end))
        start = end
    return out


def cell_columns(cells_n, lanes):
    column = lax.broadcasted_iota(jnp.int32, (8, lanes), 0).astype(f32)
    tiles = cells_n // 8
    middles = sorted({m for spans in (SAMPLE_SPANS, SPREAD_SPANS) for _, m, _ in runs(spans, tiles)})
    return {m: column + float(8 * m) for m in middles}


def raw_weights(position, columns, tiles, spans):
    pieces = [None] * tiles
    for start, middle, end in runs(spans, tiles):
        offset = columns[middle] - position
        slope = offset * -SHARPNESS
        at = slope * offset
        pieces[middle] = jnp.exp2(at)
        for n in range(1, max(end - middle, middle - start + 1)):
            near = at - 64.0 * SHARPNESS * n * n
            step = slope * (16.0 * n)
            if middle - n >= start:
                pieces[middle - n] = jnp.exp2(near - step)
            if middle + n < end:
                pieces[middle + n] = jnp.exp2(near + step)
    return jnp.concatenate(pieces, axis=0)


def split_bf16(values):
    high = values.astype(bf16)
    low = (values - high.astype(f32)).astype(bf16)
    return high, low


def two_parts(rows):
    high = rows.astype(bf16).astype(f32)
    return jnp.concatenate([high, rows - high], axis=0).astype(bf16)


def clear_lhs(lhs):
    cells_n = lhs.shape[2] // 2
    lhs[...] = jnp.zeros_like(lhs)
    one = jnp.ones((1, cells_n), f32)
    for q in range(lhs.shape[0]):
        lhs[q, 4:5, :cells_n] = one
        lhs[q, 12:13, cells_n:] = one


def sample_quad(q, at, positions, columns, rows_of, lhs, sp, su, sn):
    cells_n = lhs.shape[2] // 2
    weights = []
    for j in range(QUAD):
        p_row, u_row = rows_of(j)
        row, side = 8 * (j // 2) + 2 * (j % 2), slice(cells_n * (j // 2), cells_n * (j // 2 + 1))
        lhs[q, row : row + 1, side] = p_row
        lhs[q, row + 1 : row + 2, side] = u_row
        weights.append(raw_weights(positions[j], columns, cells_n // 8, SAMPLE_SPANS).astype(bf16))
    rhs = jnp.concatenate(
        [jnp.concatenate(weights[:2], axis=1), jnp.concatenate(weights[2:], axis=1)], axis=0
    )
    result = jnp.dot(two_parts(lhs[q]), rhs, preferred_element_type=f32)
    result = result[:16] + result[16:]
    lanes = rhs.shape[1] // 2
    for j in range(QUAD):
        row, part = 8 * (j // 2), result[:, lanes * (j % 2) : lanes * (j % 2 + 1)]
        first = row + 2 * (j % 2)
        sp[pl.ds(at + j, 1), :] = part[first : first + 1]
        su[pl.ds(at + j, 1), :] = part[first + 1 : first + 2]
        sn[pl.ds(at + j, 1), :] = part[row + 4 : row + 5]


def drive_of(pressure, velocity, norm):
    inverse = 1.0 / norm
    return AMBIENT + PRESSURE_COUPLING * (pressure * inverse), velocity * inverse


def advance_group(radius, growth, rest, drive, substeps):
    h = TIME_STEP / SUBSTEPS
    for _ in range(substeps):
        over = 1.0 / radius
        gas = jnp.exp2((GAS_INDEX * LOG2E) * jnp.log(rest * over))
        damping = growth * (1.5 * growth + VISCOUS * over)
        growth = growth + (gas - drive - damping) * (h * over)
        radius = radius + h * growth
    return radius, growth


def travel(position, speed, velocity):
    h = TIME_STEP / SUBSTEPS
    keep = 1.0 - h / RELAX_TIME
    lag = speed - velocity
    path = h * sum(keep ** n for n in range(1, SUBSTEPS + 1))
    return position + TIME_STEP * velocity + path * lag, velocity + keep**SUBSTEPS * lag


def source_amount(radius, growth):
    return SOURCE_GAIN * FOUR_PI * radius * radius * growth


def void_amount(radius):
    return VOID_SCALE * FOUR_PI / 3.0 * radius * radius * radius


def spread_pair(pair, positions, amounts, columns, tiles):
    pieces, norms = [], []
    for position in positions:
        raw = raw_weights(position, columns, tiles, SPREAD_SPANS)
        norms.append(jnp.sum(raw, axis=0, keepdims=True))
        pieces.append(jnp.concatenate(split_bf16(raw), axis=1))
    rhs = jnp.concatenate(pieces, axis=0)
    sublane = lax.broadcasted_iota(jnp.int32, amounts[0].shape, 0)
    inverse = 1.0 / jnp.where(sublane == 2 * pair, norms[0], norms[1])
    rows = jnp.concatenate([a * inverse for a in amounts], axis=0)
    lhs = two_parts(rows)
    lhs = jnp.concatenate([lhs, lhs], axis=1)
    result = lax.dot_general(
        lhs, rhs, (((1,), (1,)), ((), ())), preferred_element_type=f32
    )
    result = result[: rows.shape[0]] + result[rows.shape[0] :]
    cells_n = 8 * tiles
    out = []
    for n in range(len(amounts)):
        for side in range(2):
            row = GROUP * n + 2 * pair + side
            out.append(result[row : row + 1, side * cells_n : (side + 1) * cells_n])
    return out


def spread_quad(quad, positions, amounts, columns, tiles):
    weights, norms = [], []
    for position in positions:
        raw = raw_weights(position, columns, tiles, SPREAD_SPANS)
        norms.append(jnp.sum(raw, axis=0, keepdims=True))
        weights.append(raw.astype(bf16))
    rhs = jnp.concatenate(
        [jnp.concatenate(weights[0::2], axis=1), jnp.concatenate(weights[1::2], axis=1)], axis=0
    )
    row = lax.broadcasted_iota(jnp.int32, amounts.shape, 0) % QUAD
    norm = jnp.where(
        row < 2, jnp.where(row == 0, norms[0], norms[1]), jnp.where(row == 2, norms[2], norms[3])
    )
    parts = two_parts(amounts / norm)
    none = jnp.zeros_like(parts)
    lhs = jnp.concatenate(
        [jnp.concatenate([parts, none], axis=1), jnp.concatenate([none, parts], axis=1)], axis=0
    )
    result = lax.dot_general(
        lhs, rhs, (((1,), (1,)), ((), ())), preferred_element_type=f32
    )
    size, cells_n = amounts.shape[0], 8 * tiles
    out = []
    for j in range(QUAD):
        first = (j // 2) * 2 * size + QUAD * quad + j
        side = slice((j % 2) * cells_n, (j % 2 + 1) * cells_n)
        out.append(result[first : first + 1, side] + result[first + size : first + size + 1, side])
    return out


def lanes_of(rows):
    number, lanes = rows.shape
    pieces = []
    for at in range(0, number, lanes):
        block = rows[at : at + lanes]
        same = lax.broadcasted_iota(jnp.int32, block.shape, 0) == lax.broadcasted_iota(
            jnp.int32, block.shape, 1
        )
        line = jnp.sum(jnp.where(same, block, 0.0), axis=0, keepdims=True)
        pieces.append(line[:, : block.shape[0]])
    return jnp.concatenate(pieces, axis=1)


def scatter(tile_rows, parts, tiles, store):
    cells_n = parts[0].shape[1]
    ids = lanes_of(tile_rows[...])
    block = min(1024, tiles)
    rhs = jnp.concatenate([x for part in parts for x in split_bf16(part[...])], axis=1)

    def some(i, carry):
        at = pl.multiple_of(i * block, block)
        tile = lax.broadcasted_iota(jnp.int32, (block, ids.shape[1]), 0) + at
        hot = jnp.where(tile.astype(f32) == ids, 1.0, 0.0).astype(bf16)
        result = jnp.dot(hot, rhs, preferred_element_type=f32)
        sums = []
        for n in range(len(parts)):
            high = result[:, 2 * n * cells_n : (2 * n + 1) * cells_n]
            sums.append(high + result[:, (2 * n + 1) * cells_n : (2 * n + 2) * cells_n])
        store(at, block, sums)
        return carry

    lax.fori_loop(0, tiles // block, some, 0)


def flow_plane(s, width, fluid, new_ref):
    comps, _, cells = fluid.shape
    row = lax.broadcasted_iota(jnp.int32, (width, cells), 0)
    lane = lax.broadcasted_iota(jnp.int32, (width, cells), 1)

    def plane(ref, c, n):
        return ref[c, pl.ds(pl.multiple_of(n * width, width), width), :]

    d_s, d_a, d_r, lap, now = [], [], [], [], []
    for c in range(comps):
        x, below, above = (plane(fluid, c, s + n) for n in (1, 0, 2))
        a_down = jnp.where(row == 0, 0.0, pltpu.roll(x, 1, 0))
        a_up = jnp.where(row == width - 1, 0.0, pltpu.roll(x, width - 1, 0))
        r_down = jnp.where(lane == 0, 0.0, pltpu.roll(x, 1, 1))
        r_up = jnp.where(lane == cells - 1, 0.0, pltpu.roll(x, cells - 1, 1))
        now.append(x)
        d_s.append(above - below)
        d_a.append(a_up - a_down)
        d_r.append(r_up - r_down)
        lap.append(above + below + a_up + a_down + r_up + r_down - 6.0 * x)
    half = 0.5 * TIME_STEP
    change = [
        MEAN_FLOW * d_s[0] + d_s[1] + d_a[2] + d_r[3],
        MEAN_FLOW * d_s[1] + d_s[0],
        MEAN_FLOW * d_s[2] + d_a[0],
        MEAN_FLOW * d_s[3] + d_r[0],
    ]
    for c in range(comps):
        at = pl.multiple_of((s + 1) * width, width)
        new_ref[c, pl.ds(at, width), :] = now[c] - half * change[c] + DIFFUSION * lap[c]


def halo_terms(side, sign, stream):
    half = sign * 0.5 * TIME_STEP
    own = DIFFUSION + (half * MEAN_FLOW if stream else 0.0)
    terms = [own * x for x in side]
    other = 1 if stream else 2
    terms[0] = terms[0] + half * side[other]
    terms[other] = terms[other] + half * side[0]
    return terms


def add_halos(ref, start, length, width, low, high, left, right):
    comps = ref.shape[0]
    for at, number, stride, side, sign in (
        (start, width, 1, low, 1), (start + (length - 1) * width, width, 1, high, -1),
        (start, length, width, left, 1), (start + width - 1, length, width, right, -1),
    ):
        rows = pl.ds(at, number) if stride == 1 else pl.ds(at, number, stride=stride)
        terms = halo_terms([side[c] for c in range(comps)], sign, stride == 1)
        terms = [ref[c, rows, :] + term for c, term in enumerate(terms)]
        for c, term in enumerate(terms):
            ref[c, rows, :] = term


def peer_of(n, streams, azims):
    turn, other = n // streams, n % streams
    step = (turn + 1) // 2 * (2 * (turn % 2) - 1)
    away = (azims // 2 + step + azims) % azims
    stream = (lax.axis_index("stream") + (other + 1) % streams) % streams
    return stream, (lax.axis_index("azim") + away) % azims


def source_of(n, streams, azims):
    turn, other = n // streams, n % streams
    step = (turn + 1) // 2 * (2 * (turn % 2) - 1)
    away = (azims // 2 + step + azims) % azims
    stream = (lax.axis_index("stream") + streams - (other + 1) % streams) % streams
    return stream * azims + (lax.axis_index("azim") + azims - away) % azims


def first_kernel(streams, azims, cap, length, width, soon,
                 order_ref, tiles_ref, after_ref, count_ref, bubbles_hbm, fluid_hbm,
                 fluid_out, rows_out, arrived, low_2, high_2, left_2, right_2,
                 bubbles_out, spread_out, void_out, tile_out,
                 fluid_v, new_v, rows_in, low_v, high_v, left_v, right_v, first_v, last_v,
                 zero_v, bubbles_v, now_v, mid_v, live_v, tile_v, amount_v, place_v, sp, su, sn, send_v, spread_v,
                 soon_v, dead_v, fin_v, volume_v, void_v,
                 lhs, load_sems, store_sems, own_sem, dead_sems, send_sems, recv_sems,
                 early_send, early_recv, late_send, late_recv, zero_sems):
    devices = streams * azims
    comps, area, cells_n = fluid_hbm.shape
    slots, lanes = sp.shape
    stream, azim = lax.axis_index("stream"), lax.axis_index("azim")
    me = stream * azims + azim
    last_stream = streams - 1

    barrier = pltpu.get_barrier_semaphore()

    def greet(n, carry):
        other = (me + n) % devices
        pl.semaphore_signal(
            barrier, inc=1, device_id=(other // azims, other % azims), device_id_type=MESH
        )
        return carry

    lax.fori_loop(1, devices, greet, 0)
    inner = pl.ds(width, area)
    loads = [
        pltpu.make_async_copy(bubbles_hbm, bubbles_v, load_sems.at[0]),
        pltpu.make_async_copy(fluid_hbm.at[0], rows_in.at[0], load_sems.at[1]),
        pltpu.make_async_copy(fluid_hbm.at[comps - 1], rows_in.at[1], load_sems.at[2]),
        pltpu.make_async_copy(fluid_hbm, fluid_v.at[:, inner], load_sems.at[3]),
    ]
    for load in loads[:3]:
        load.start()
    clear_lhs(lhs)
    zero_v[...] = jnp.zeros_like(zero_v)

    @pl.when(stream == 0)
    def _():
        low_v[...] = jnp.zeros_like(low_v)

    @pl.when(stream == last_stream)
    def _():
        high_v[...] = jnp.zeros_like(high_v)

    columns = cell_columns(cells_n, lanes)
    tiles = cells_n // 8
    per = max(1, CHUNK // cap)
    chunk = per * cap
    chunks = slots // chunk
    for load in loads[:3]:
        load.wait()
    loads[3].start()

    def groups(i):
        for g in range(chunk // GROUP):
            yield g, pl.ds(pl.multiple_of(i * chunk + g * GROUP, GROUP), GROUP)

    def sample(i):
        for q in range(chunk // QUAD):
            positions = []

            def rows_of(j, q=q):
                k = q * QUAD + j
                peer_stream, peer_azim = peer_of(i * per + k // cap, streams, azims)
                slot = (peer_stream * azims + peer_azim) * cap + k % cap
                block = order_ref[slot]
                tile = tiles_ref[block]
                at = i * chunk + k
                for c in range(STATES):
                    now_v[c, pl.ds(at, 1), :] = bubbles_v[pl.ds(c * slots + block, 1), :]
                live = jnp.where(block < count_ref[0], 1.0, 0.0)
                live_v[pl.ds(at, 1), :] = jnp.full((1, lanes), live, f32)
                tile_v[pl.ds(at, 1), :] = jnp.full((1, lanes), tile.astype(f32), f32)
                positions.append(bubbles_v[pl.ds(2 * slots + block, 1), :])
                return rows_in[0, pl.ds(tile, 1), :], rows_in[1, pl.ds(tile, 1), :]

            rows = [rows_of(j) for j in range(QUAD)]
            at = i * chunk + q * QUAD
            sample_quad(q, at, positions, columns, lambda j: rows[j], lhs, sp, su, sn)

    def advance_start(i):
        for g, at in groups(i):
            live = live_v[at, :] > 0.5
            state = [now_v[c, at, :] for c in range(STATES)]
            state[0] = jnp.where(live, state[0], 1.0)
            state[4] = jnp.where(live, state[4], 1.0)
            drive, velocity = drive_of(sp[at, :], su[at, :], sn[at, :])
            place, speed = travel(state[2], state[3], velocity)
            radius, growth = advance_group(state[0], state[1], state[4], drive, SUBSTEPS // 2)
            for c, x in enumerate((radius, growth, place, speed, state[4], drive)):
                mid_v[c, at, :] = x

    def advance_end(i):
        for g, at in groups(i):
            live = live_v[at, :] > 0.5
            state = [mid_v[c, at, :] for c in range(STATES + 1)]
            new = advance_group(state[0], state[1], state[4], state[5], SUBSTEPS - SUBSTEPS // 2)
            new = new + tuple(state[2:STATES])
            amount_v[at, :] = jnp.where(live, source_amount(new[0], new[1]), 0.0)
            place_v[at, :] = new[2]
            new = (jnp.where(live, new[0], -1.0),) + tuple(new[1:])
            piece = min(cap, GROUP)
            for k in range(0, GROUP, piece):
                n = g * GROUP + k
                for c in range(STATES):
                    send_v[i * per + n // cap, c, n % cap : n % cap + piece, :] = new[c][k : k + piece]

    def spread(i):
        for g in range(chunk // GROUP):
            base = pl.multiple_of(i * chunk + g * GROUP, GROUP)
            amount = amount_v[pl.ds(base, GROUP), :]
            for quad in range(GROUP // QUAD):
                positions = [place_v[pl.ds(base + QUAD * quad + n, 1), :] for n in range(QUAD)]
                rows = spread_quad(quad, positions, amount, columns, tiles)
                for n in range(QUAD):
                    spread_v[pl.ds(base + QUAD * quad + n, 1), :] = rows[n]

    def to_peer(n, place):
        peer = peer_of(n, streams, azims)
        return pltpu.make_async_remote_copy(
            src_ref=send_v.at[n], dst_ref=place, send_sem=send_sems.at[n],
            recv_sem=recv_sems.at[n], device_id=peer, device_id_type=MESH,
        )

    def start_to(n):
        pl.when(n < soon)(to_peer(n, soon_v.at[jnp.minimum(n, soon - 1)]).start)
        pl.when(n >= soon)(to_peer(n, arrived.at[me]).start)

    def dead(n):
        return pltpu.make_async_copy(dead_v, arrived.at[source_of(n, streams, azims)], dead_sems.at[n])

    def wait_soon(n):
        to_peer(n, soon_v.at[n]).wait_recv()

    def wait_late(n):
        to_peer(n, arrived.at[source_of(n, streams, azims)]).wait_recv()

    own = pltpu.make_async_copy(send_v.at[devices - 1], arrived.at[me], own_sem)

    def send(i, end=False):
        for q in range(per):
            if end and q == per - 1:
                own.start()
            else:
                start_to(i * per + q)

    def halo_copies(ref, lands, sends, recvs):
        def copy(n, src, dst, peer):
            return pltpu.make_async_remote_copy(
                src_ref=src, dst_ref=dst, send_sem=sends.at[n], recv_sem=recvs.at[n],
                device_id=peer, device_id_type=MESH,
            )

        up, down = (stream + 1) % streams, (stream + streams - 1) % streams
        right, left = (azim + 1) % azims, (azim + azims - 1) % azims
        return (
            copy(0, ref.at[:, pl.ds(width * length, width)], lands[0], (up, azim)),
            copy(1, ref.at[:, pl.ds(width, width)], lands[1], (down, azim)),
            copy(2, last_v, lands[2], (stream, right)),
            copy(3, first_v, lands[3], (stream, left)),
        )

    def halo_start(copies):
        pl.when(stream < last_stream)(copies[0].start)
        pl.when(stream > 0)(copies[1].start)
        copies[2].start()
        copies[3].start()

    def halo_sent(copies):
        pl.when(stream < last_stream)(copies[0].wait_send)
        pl.when(stream > 0)(copies[1].wait_send)
        copies[2].wait_send()
        copies[3].wait_send()

    def halo_here(copies):
        pl.when(stream > 0)(copies[0].wait_recv)
        pl.when(stream < last_stream)(copies[1].wait_recv)
        copies[2].wait_recv()
        copies[3].wait_recv()

    def set_ends(ref, low, high):
        ref[:, pl.ds(0, width), :] = low
        ref[:, pl.ds((length + 1) * width, width), :] = high

    def edges(ref):
        many = 4

        def edge(n, carry):
            for k in range(many):
                s = n * many + k
                at = pl.multiple_of((s + 1) * width, width)
                for c in range(comps):
                    first_v[c, pl.ds(s, 1), :] = ref[c, pl.ds(at, 1), :]
                    last_v[c, pl.ds(s, 1), :] = ref[c, pl.ds(at + width - 1, 1), :]
            return carry

        lax.fori_loop(0, length // many, edge, 0)

    state_row = lax.broadcasted_iota(jnp.int32, dead_v.shape, 0)
    dead_v[...] = jnp.where(state_row == 0, -1.0, 1.0)
    fin_v[...] = jnp.zeros_like(fin_v)
    sample(0)
    loads[3].wait()
    edges(fluid_v)
    advance_start(0)
    sample(1)
    pl.semaphore_wait(barrier, devices - 1)
    early = halo_copies(fluid_v, (low_v, high_v, left_v, right_v), early_send, early_recv)
    halo_start(early)

    def bury(n, carry):
        dead(n).start()
        return carry

    lax.fori_loop(0, soon, bury, 0)
    advance_end(0)
    advance_start(1)
    sample(2)

    def steady(i):
        spread(i - 3)
        advance_end(i - 2)
        advance_start(i - 1)
        sample(i)
        send(i - 3)

    def plain(i, carry):
        steady(i)
        return carry

    planes = 3
    begin = max(3, chunks - pl.cdiv(length, planes))
    planes = pl.cdiv(length, max(1, chunks - begin))

    def with_flow(i, carry):
        for n in range(planes):
            s = jnp.minimum((i - begin) * planes + n, length - 1)
            flow_plane(s, width, fluid_v, new_v)
        steady(i)
        return carry

    set_ends(fluid_v, zero_v[...], zero_v[...])
    lax.fori_loop(3, begin, plain, 0)
    lax.fori_loop(begin, chunks, with_flow, 0)
    send(chunks - 3)
    spread(chunks - 3)
    advance_end(chunks - 2)
    advance_start(chunks - 1)
    send(chunks - 2)
    spread(chunks - 2)
    advance_end(chunks - 1)
    spread(chunks - 1)
    send(chunks - 1, True)

    halo_here(early)
    halo_sent(early)
    add_halos(new_v, width, length, width, low_v, high_v, left_v, right_v)

    def subtract(at, block, parts):
        rows = pl.ds(at + width, block)
        new_v[0, rows, :] = new_v[0, rows, :] - TIME_STEP * parts[0]

    scatter(tile_v, [spread_v], area, subtract)
    edges(new_v)
    late = halo_copies(new_v, (low_2, high_2, left_2, right_2), late_send, late_recv)
    keeps = [
        pltpu.make_async_copy(new_v.at[0, inner], rows_out.at[0], store_sems.at[0]),
        pltpu.make_async_copy(new_v.at[comps - 1, inner], rows_out.at[1], store_sems.at[1]),
    ]
    for keep in keeps:
        keep.start()
    halo_start(late)

    def sent(n, carry):
        to_peer(n, soon_v.at[0]).wait_send()
        return carry

    zeros = [pltpu.make_async_copy(zero_v, out, zero_sems.at[n]) for n, out in enumerate((low_2, high_2))]
    pl.when(stream == 0)(zeros[0].start)
    pl.when(stream == last_stream)(zeros[1].start)
    set_ends(new_v, zero_v[...], zero_v[...])
    pieces = 4
    part = length // pieces
    outs = []
    for p in range(pieces):
        def flow(n, carry, p=p):
            for k in range(4):
                flow_plane(p * part + 4 * n + k, width, new_v, fluid_v)
            return carry

        lax.fori_loop(0, part // 4, flow, 0)
        outs.append(pltpu.make_async_copy(
            fluid_v.at[:, pl.ds((p * part + 1) * width, part * width)],
            fluid_out.at[:, pl.ds(p * part * width, part * width)], store_sems.at[2 + p],
        ))
        outs[p].start()
    def peers(i):
        for q in range(per):
            yield q, i * per + q

    def arrive(i):
        for _, n in peers(i):
            wait_soon(n)

    def sample_2(i):
        for q in range(chunk // QUAD):
            rows, positions = [], []
            for j in range(QUAD):
                k = q * QUAD + j
                n = i * per + k // cap
                tile = after_ref[source_of(n, streams, azims) * cap + k % cap]
                tile_v[pl.ds(i * chunk + k, 1), :] = jnp.full((1, lanes), tile.astype(f32), f32)
                positions.append(soon_v[n, 2, pl.ds(k % cap, 1), :])
                row = pl.ds(tile + width, 1)
                rows.append((new_v[0, row, :], new_v[comps - 1, row, :]))
            sample_quad(q, i * chunk + q * QUAD, positions, columns, lambda j: rows[j], lhs, sp, su, sn)

    def state_2(i, g):
        piece = min(cap, GROUP)
        parts = []
        for k in range(g * GROUP, (g + 1) * GROUP, piece):
            parts.append([soon_v[i * per + k // cap, c, k % cap : k % cap + piece, :] for c in range(STATES)])
        state = [x[0] if len(parts) == 1 else jnp.concatenate(x, axis=0) for x in zip(*parts)]
        return state, state[0] * state[4] >= 0.0

    def advance_start_2(i):
        for g, at in groups(i):
            state, live = state_2(i, g)
            radius, rest = (jnp.where(live, x, 1.0) for x in (state[0], state[4]))
            drive, velocity = drive_of(sp[at, :], su[at, :], sn[at, :])
            place, speed = travel(state[2], state[3], velocity)
            radius, growth = advance_group(radius, state[1], rest, drive, SUBSTEPS // 2)
            for c, x in enumerate((radius, growth, place, speed, rest, drive)):
                mid_v[c, at, :] = x

    def advance_end_2(i):
        for g, at in groups(i):
            live = state_2(i, g)[1]
            state = [mid_v[c, at, :] for c in range(STATES + 1)]
            new = advance_group(state[0], state[1], state[4], state[5], SUBSTEPS - SUBSTEPS // 2)
            new = new + tuple(state[2:STATES])
            amount_v[at, :] = jnp.where(live, source_amount(new[0], new[1]), 0.0)
            volume_v[at, :] = jnp.where(live, void_amount(new[0]), 0.0)
            place_v[at, :] = new[2]
            piece = min(cap, GROUP)
            for k in range(0, GROUP, piece):
                m = g * GROUP + k
                source = source_of(i * per + m // cap, streams, azims)
                for c in range(STATES):
                    fin_v[c, source, m % cap : m % cap + piece, :] = jnp.where(live, new[c], 0.0)[k : k + piece]

    def spread_2(i):
        for g, at in groups(i):
            base = i * chunk + g * GROUP
            amounts = [amount_v[at, :], volume_v[at, :]]
            for pair in range(GROUP // 2):
                positions = [place_v[pl.ds(base + 2 * pair + n, 1), :] for n in range(2)]
                rows = spread_pair(pair, positions, amounts, columns, tiles)
                for n in range(2):
                    spread_v[pl.ds(base + 2 * pair + n, 1), :] = rows[n]
                    void_v[pl.ds(base + 2 * pair + n, 1), :] = rows[2 + n]

    count = soon // per
    arrive(0)
    sample_2(0)
    arrive(1)
    advance_start_2(0)
    sample_2(1)
    arrive(2)
    advance_end_2(0)
    advance_start_2(1)
    sample_2(2)

    def steady_2(i, carry):
        arrive(i)
        spread_2(i - 3)
        advance_end_2(i - 2)
        advance_start_2(i - 1)
        sample_2(i)
        return carry

    lax.fori_loop(3, count, steady_2, 0)
    spread_2(count - 3)
    advance_end_2(count - 2)
    advance_start_2(count - 1)
    spread_2(count - 2)
    advance_end_2(count - 1)
    spread_2(count - 1)
    done = pl.ds(0, soon * cap)
    for n, (src, dst) in enumerate((
        (fin_v, bubbles_out), (spread_v.at[done], spread_out), (void_v, void_out), (tile_v.at[done], tile_out)
    )):
        outs.append(pltpu.make_async_copy(src, dst, store_sems.at[2 + pieces + n]))
        outs[-1].start()
    lax.fori_loop(0, devices - 1, sent, 0)
    own.wait()

    def came(n, carry):
        wait_late(n)
        return carry

    lax.fori_loop(soon, devices - 1, came, 0)

    def buried(n, carry):
        dead(n).wait()
        return carry

    lax.fori_loop(0, soon, buried, 0)
    halo_here(late)
    halo_sent(late)
    pl.when(stream == 0)(zeros[0].wait)
    pl.when(stream == last_stream)(zeros[1].wait)
    for copy in keeps + outs:
        copy.wait()


def shaped(*shape):
    return jax.ShapeDtypeStruct(shape, f32)


def buffer(*shape):
    return pltpu.VMEM(shape, f32)


def dma(*shape):
    return pltpu.SemaphoreType.DMA(shape)


ANYWHERE = pl.BlockSpec(memory_space=pl.ANY)
SCALARS = pl.BlockSpec(memory_space=pltpu.SMEM)


def first_step(fluid, order, tiles_ids, after_ids, counts, bubbles, length, width):
    streams, azims = lax.axis_size("stream"), lax.axis_size("azim")
    devices = streams * azims
    comps, tiles, cells = fluid.shape
    slots, lanes = order.shape[0], bubbles.shape[1]
    cap = slots // devices
    soon = 5 * devices // 16
    end, side = buffer(comps, width, cells), buffer(comps, length, cells)
    padded = buffer(comps, tiles + 2 * width, cells)
    per_slot = buffer(slots, lanes)
    return pl.pallas_call(
        functools.partial(first_kernel, streams, azims, cap, length, width, soon),
        out_shape=(shaped(*fluid.shape), shaped(2, tiles, cells), shaped(devices, STATES, cap, lanes),
                   *[shaped(*x.shape) for x in (end, end, side, side)],
                   shaped(STATES, devices, cap, lanes), *[shaped(soon * cap, cells)] * 2, shaped(soon * cap, lanes)),
        in_specs=[SCALARS] * 4 + [ANYWHERE] * 2,
        out_specs=(ANYWHERE,) * 11,
        scratch_shapes=[
            padded, padded, buffer(2, tiles, cells), end, end, side, side, side, side,
            end, buffer(*bubbles.shape), buffer(STATES, slots, lanes), buffer(STATES + 1, slots, lanes),
            per_slot, per_slot, per_slot, per_slot, per_slot, per_slot, per_slot,
            buffer(devices, STATES, cap, lanes), buffer(slots, cells),
            buffer(soon, STATES, cap, lanes), buffer(STATES, cap, lanes), buffer(STATES, devices, cap, lanes),
            per_slot, buffer(soon * cap, cells),
            buffer(max(cap, CHUNK) // QUAD, 16, 2 * cells),
            dma(4), dma(10), dma(), dma(soon), dma(devices), dma(devices), dma(4), dma(4), dma(4), dma(4), dma(2),
        ],
        compiler_params=pltpu.CompilerParams(
            vmem_limit_bytes=VMEM_GRANT, collective_id=0, has_side_effects=True
        ),
        cost_estimate=pl.CostEstimate(
            flops=slots * lanes * cells * 2000, bytes_accessed=12 * 2**20,
            transcendentals=2 * slots * lanes * cells,
        ),
        name="first_step",
    )(order, tiles_ids, after_ids, counts, bubbles, fluid)


def live_list(arrived_v, devices, live_v, slots_v, rows_v):
    slots, lanes = live_v.shape
    cap = slots // devices
    for d in range(devices):
        at = d * STATES * cap
        live = arrived_v[at : at + cap, :] * arrived_v[at + 4 * cap : at + 5 * cap, :] >= 0.0
        live_v[d * cap : (d + 1) * cap, :] = jnp.where(live, 1.0, 0.0)
    live = live_v[...]
    row = lax.broadcasted_iota(jnp.int32, (slots, slots), 0)
    column = lax.broadcasted_iota(jnp.int32, (slots, slots), 1)
    before = jnp.where(column < row, 1.0, 0.0).astype(bf16)
    rank = jnp.dot(before, live.astype(bf16), preferred_element_type=f32)
    number = jnp.dot(jnp.ones((16, slots), bf16), live.astype(bf16), preferred_element_type=f32)
    rank = jnp.where(live > 0.5, rank, -1.0)
    place = lax.broadcasted_iota(jnp.int32, (slots, lanes), 1).astype(f32)
    hot = [
        jnp.where(rank - float(at) == place, 1.0, 0.0).astype(bf16)[:, : min(lanes, slots - at)]
        for at in range(0, slots, lanes)
    ]
    which = lax.broadcasted_iota(jnp.int32, (16, slots), 0)
    slot = lax.broadcasted_iota(jnp.int32, (16, slots), 1)
    digits = jnp.where(which == 0, slot // cap, slot % cap).astype(f32).astype(bf16)
    found = jnp.dot(digits, jnp.concatenate(hot, axis=1), preferred_element_type=f32)
    entry = lax.broadcasted_iota(jnp.int32, (1, slots), 1).astype(f32)
    for ref, stride in ((slots_v, cap), (rows_v, STATES * cap)):
        line = float(stride) * found[0:1] + found[1:2]
        line = jnp.where(entry < number[0:1, 0:1], line, line[:, 0:1])
        ref[:, :slots] = line.astype(jnp.int32)
        ref[:, slots:] = number[0:1].astype(jnp.int32)


def second_kernel(devices, length, tiles_ref, arrived_hbm, rows_hbm, flow_hbm, low_hbm, high_hbm, left_hbm, right_hbm,
                  bubbles_hbm, spread_hbm, spread_void_hbm, spread_tile_hbm, fluid_out, bubbles_out, void_out,
                  arrived_v, rows_in, flow_v, low_v, high_v, left_v, right_v, bubbles_v, void_v,
                  now_v, mid_v, fin_v, live_v, tile_v, amount_v, volume_v, sp, su, sn, rows_v, voids_v,
                  lhs, slots_v, places_v, slots_ref, places_ref, load_sems, list_sems, store_sems):
    comps, area, cells_n = flow_hbm.shape
    slots, lanes = sp.shape
    cap = slots // devices
    width = area // length
    ahead = slots - spread_hbm.shape[0]
    behind = pl.ds(ahead, slots - ahead)
    loads = [
        pltpu.make_async_copy(arrived_hbm, arrived_v, load_sems.at[0]),
        pltpu.make_async_copy(rows_hbm, rows_in, load_sems.at[1]),
        pltpu.make_async_copy(flow_hbm, flow_v, load_sems.at[2]),
        pltpu.make_async_copy(low_hbm, low_v, load_sems.at[3]),
        pltpu.make_async_copy(high_hbm, high_v, load_sems.at[4]),
        pltpu.make_async_copy(left_hbm, left_v, load_sems.at[5]),
        pltpu.make_async_copy(right_hbm, right_v, load_sems.at[6]),
        pltpu.make_async_copy(bubbles_hbm, bubbles_v, load_sems.at[7]),
        pltpu.make_async_copy(spread_hbm, rows_v.at[behind], load_sems.at[8]),
        pltpu.make_async_copy(spread_void_hbm, voids_v.at[behind], load_sems.at[9]),
        pltpu.make_async_copy(spread_tile_hbm, tile_v.at[behind], load_sems.at[10]),
    ]
    for load in loads:
        load.start()
    columns = cell_columns(cells_n, lanes)
    tiles = cells_n // 8
    clear_lhs(lhs)
    loads[0].wait()
    live_list(arrived_v, devices, live_v, slots_v, places_v)
    lists = [
        pltpu.make_async_copy(slots_v, slots_ref, list_sems.at[0]),
        pltpu.make_async_copy(places_v, places_ref, list_sems.at[1]),
    ]
    for copy in lists:
        copy.start()
    tile_v[:ahead, :] = jnp.full((ahead, lanes), -1.0, f32)
    rows_v[:ahead, :] = jnp.zeros((ahead, cells_n), f32)
    voids_v[:ahead, :] = jnp.zeros((ahead, cells_n), f32)
    def store(n, src, dst):
        copy = pltpu.make_async_copy(src, dst, store_sems.at[n])
        copy.start()
        return copy

    for load in loads[1:]:
        load.wait()
    add_halos(flow_v, 0, length, width, low_v, high_v, left_v, right_v)
    for copy in lists:
        copy.wait()
    rest = pl.ds(1, comps - 1)
    stores = [store(0, flow_v.at[rest], fluid_out.at[rest])]
    number = slots_ref[0, slots]
    chunks = (number + CHUNK - 1) // CHUNK

    def groups(i):
        for g in range(CHUNK // GROUP):
            base = pl.multiple_of(i * CHUNK + g * GROUP, GROUP)
            yield base, pl.ds(base, GROUP)

    def sample(i):
        for q in range(CHUNK // QUAD):
            at = i * CHUNK + q * QUAD
            rows, positions = [], []
            for j in range(QUAD):
                place = places_ref[0, at + j]
                tile = tiles_ref[slots_ref[0, at + j]]
                for c in range(STATES):
                    now_v[c, pl.ds(at + j, 1), :] = arrived_v[pl.ds(place + c * cap, 1), :]
                tile_v[pl.ds(at + j, 1), :] = jnp.full((1, lanes), tile.astype(f32), f32)
                positions.append(arrived_v[pl.ds(place + 2 * cap, 1), :])
                rows.append((rows_in[0, pl.ds(tile, 1), :], rows_in[1, pl.ds(tile, 1), :]))
            sample_quad(q, at, positions, columns, lambda j: rows[j], lhs, sp, su, sn)

    def ready(i):
        return [
            ([now_v[c, at, :] for c in range(STATES)], (sp[at, :], su[at, :], sn[at, :]))
            for _, at in groups(i)
        ]

    def advance_start(i, loaded=None):
        for (_, at), (state, sums) in zip(groups(i), loaded or ready(i)):
            drive, velocity = drive_of(*sums)
            place, speed = travel(state[2], state[3], velocity)
            radius, growth = advance_group(state[0], state[1], state[4], drive, SUBSTEPS // 2)
            for c, x in enumerate((radius, growth, place, speed, state[4], drive)):
                mid_v[c, at, :] = x

    def advance_end(i):
        for base, at in groups(i):
            state = [mid_v[c, at, :] for c in range(STATES + 1)]
            new = advance_group(state[0], state[1], state[4], state[5], SUBSTEPS - SUBSTEPS // 2)
            new = new + tuple(state[2:STATES])
            live = base + lax.broadcasted_iota(jnp.int32, (GROUP, lanes), 0) < number
            amount_v[at, :] = jnp.where(live, source_amount(new[0], new[1]), 0.0)
            volume_v[at, :] = jnp.where(live, void_amount(new[0]), 0.0)
            for c in range(STATES):
                fin_v[c, at, :] = new[c]

    def spread(i):
        for base, rows_at in groups(i):
            amounts = [amount_v[rows_at, :], volume_v[rows_at, :]]
            for pair in range(GROUP // 2):
                positions = [fin_v[2, pl.ds(base + 2 * pair + n, 1), :] for n in range(2)]
                rows = spread_pair(pair, positions, amounts, columns, tiles)
                for n in range(2):
                    at = base + 2 * pair + n
                    rows_v[pl.ds(at, 1), :] = rows[n]
                    voids_v[pl.ds(at, 1), :] = rows[2 + n]
                    slot = slots_ref[0, at]
                    for c in range(STATES):
                        bubbles_v[pl.ds(c * slots + slot, 1), :] = fin_v[c, pl.ds(at, 1), :]

    @pl.when(number > 0)
    def _():
        def at_most(i):
            return jnp.minimum(i, chunks - 1)

        def before_end(n):
            return jnp.maximum(chunks - n, 0)

        sample(0)
        advance_start(0)
        sample(at_most(1))
        advance_end(0)
        advance_start(at_most(1))
        sample(at_most(2))

        def steady(i, carry):
            loaded = ready(i - 1)
            sample(i)
            spread(i - 3)
            advance_end(i - 2)
            advance_start(i - 1, loaded)
            return carry

        lax.fori_loop(3, chunks, steady, 0)
        spread(before_end(3))
        advance_end(before_end(2))
        advance_start(before_end(1))
        spread(before_end(2))
        advance_end(before_end(1))
        spread(before_end(1))

    stores.append(store(1, bubbles_v, bubbles_out))

    def finish(at, block, parts):
        rows = pl.ds(at, block)
        flow_v[0, rows, :] = flow_v[0, rows, :] - TIME_STEP * parts[0]
        void_v[rows, :] = parts[1]

    scatter(tile_v, [rows_v, voids_v], area, finish)
    stores += [store(2, flow_v.at[0], fluid_out.at[0]), store(3, void_v, void_out)]
    for copy in stores:
        copy.wait()


def second_step(tiles_ids, arrived, rows, flow, halos, bubbles, parts):
    comps, tiles, cells = flow.shape
    slots, lanes = tiles_ids.shape[0], arrived.shape[3]
    devices, length = arrived.shape[0], halos[2].shape[1]
    arrived = arrived.reshape(slots * STATES, lanes)
    per_slot = buffer(slots, lanes)
    return pl.pallas_call(
        functools.partial(second_kernel, devices, length),
        out_shape=(shaped(*flow.shape), shaped(STATES * slots, lanes), shaped(tiles, cells)),
        in_specs=[SCALARS] + [ANYWHERE] * 11,
        out_specs=(ANYWHERE,) * 3,
        scratch_shapes=[
            buffer(*arrived.shape), buffer(*rows.shape), buffer(*flow.shape),
            *[buffer(*x.shape) for x in halos],
            buffer(STATES * slots, lanes), buffer(tiles, cells),
            buffer(STATES, slots, lanes), buffer(STATES + 1, slots, lanes), buffer(STATES, slots, lanes),
            per_slot, per_slot, per_slot, per_slot, per_slot, per_slot, per_slot,
            buffer(slots, cells), buffer(slots, cells),
            buffer(CHUNK // QUAD, 16, 2 * cells),
            *[space((1, slots + lanes), jnp.int32) for space in (pltpu.VMEM, pltpu.VMEM, pltpu.SMEM, pltpu.SMEM)],
            dma(11), dma(2), dma(4),
        ],
        compiler_params=pltpu.CompilerParams(vmem_limit_bytes=VMEM_GRANT),
        cost_estimate=pl.CostEstimate(
            flops=slots * lanes * cells * 2000, bytes_accessed=6 * 2**20,
            transcendentals=2 * slots * lanes * cells,
        ),
        name="second_step",
    )(tiles_ids, arrived, rows, flow, *halos, bubbles.reshape(STATES * slots, lanes), *parts)


def on_device(fluid, bubbles, counts, outgoing_block_order, tiles_first_update, tiles_after):
    comps, length, width, cells = fluid.shape
    slots, states, lanes = bubbles.shape
    flat = (comps, length * width, cells)
    bubbles = bubbles.transpose(1, 0, 2).reshape(states * slots, lanes)
    flow, rows, arrived, *rest = first_step(
        fluid.reshape(flat), outgoing_block_order, tiles_first_update, tiles_after, counts, bubbles, length, width
    )
    fluid, bubbles, void = second_step(tiles_after, arrived, rows, flow, rest[:4], rest[4], rest[5:])
    bubbles = bubbles.reshape(states, slots, lanes).transpose(1, 0, 2)
    return fluid.reshape(comps, length, width, cells), bubbles, void.reshape(length, width, cells)


def solution(mesh):
    return jax.shard_map(
        on_device,
        mesh=mesh,
        in_specs=(
            P(None, "stream", "azim", None),
            P(("stream", "azim"), None, None),
            P(("stream", "azim")),
            P(("stream", "azim")),
            P(("stream", "azim")),
            P(("stream", "azim")),
        ),
        out_specs=(
            P(None, "stream", "azim", None),
            P(("stream", "azim"), None, None),
            P("stream", "azim", None),
        ),
        check_vma=False,
    )
```
